512 devices in a mesh: lon: 32 (over y, x, core), lat: 16 (over z).
Axes of the slice: x: 4, y: 4, z: 16, core: 2. Of those that a mesh axis runs over, the one named last changes fastest.
Arguments:
- ensemble: float32 [3, 512, 256, 256], P(None, 'lon', 'lat'), may hold values from -6 to 6
- bathymetry: int32 [512, 256], P('lon', 'lat'), may hold values from 0 to 15
- obs_cell: int32 [32, 16, 128], P('lon', 'lat'), may hold values from 0 to 767, as said below
- obs_value: float32 [32, 16, 128], P('lon', 'lat'), may hold values from -6 to 6
- obs_weight: float32 [32, 16, 128], P('lon', 'lat'), may hold values from 0.02 to 0.2
Outputs:
- analysis: float32 [3, 512, 256, 256], P(None, 'lon', 'lat')
- transform: float32 [256, 256], replicated
The draws below stay inside these ranges and needn't reach their ends.
Inputs may be any that keep to these rules, and one draw needn't show every extreme that they name: `obs_cell`: entries index a tile's fields field-major, then longitude, then latitude; every tile observes its first cell (entry 0) and its last cell (entry 767).
All inputs are finite; a program needn't handle non-finite values.
Results may differ from the reference program's by a relative error of at most 0.00022.
Values sent between devices are 32-bit elements; how exact they have to be, the bound alone decides.
No kernel may reach another device: no remote copies, remote signals or barrier semaphores. Data moves between devices by JAX's collectives and lax.ppermute only.
A program may use at most 64 MiB of HBM per device.

```python
import math
import jax
import jax.numpy as jnp
from jax import lax

K = 256
CX = 16
CY = 16
NOBS = 128
STEPS = 2
NS_ITERS = 6
LEVELS = 16
NX = 512
NY = 256
N_LON = 32
N_LAT = 16


def draw_obs_cell(key, part):
    cells = 3 * CX * CY
    base = jax.random.randint(key, (N_LON, N_LAT, NOBS), 0, cells)
    high_slot = jax.random.randint(jax.random.fold_in(key, 7), (N_LON, N_LAT, 1), 0, NOBS)
    low_slot = jax.random.randint(jax.random.fold_in(key, 11), (N_LON, N_LAT, 1), 0, NOBS - 1)
    low_slot = jnp.where(low_slot >= high_slot, low_slot + 1, low_slot)
    slots = jnp.arange(NOBS, dtype=jnp.int32)[None, None, :]
    base = jnp.where(slots == high_slot, cells - 1, base)
    base = jnp.where(slots == low_slot, 0, base)
    return base.astype(jnp.int32)


def with_ends(drawn, stream_key, smallest, high):
    longest = drawn.shape.index(max(drawn.shape))
    spots = []
    for shift in (0, 1):
        where = [jax.random.randint(jax.random.fold_in(stream_key, axis), (), 0, length) for axis, length in enumerate(drawn.shape)]
        where[longest] = (where[longest] + shift) % drawn.shape[longest]
        spots.append(tuple(where))
    return drawn.at[spots[0]].set(smallest).at[spots[1]].set(high)


def steps_of(own_key, shape, pieces, smallest, high):
    gain = 1.0
    for dim, blocks in pieces:
        draws = jax.random.uniform(jax.random.fold_in(jax.random.fold_in(own_key, 6), dim), (blocks,), jnp.float32, smallest / len(pieces), high / len(pieces))
        gain = gain * jnp.repeat(jnp.exp(draws), shape[dim] // blocks).reshape((-1,) + (1,) * (len(shape) - 1 - dim))
    return gain


def scatter_about(rng, extent, scale, limit, shards=(), held_as=jnp.bfloat16):
    result = jax.random.normal(rng, extent, jnp.float32) * scale
    if len(shards) > 0:
        result = steps_of(rng, extent, shards, -0.22, 0.18) * result
    return jnp.clip(result, min=-limit, max=limit).astype(held_as)


def setup_inputs(seed: int = 0) -> dict:
    key_list = jax.random.split(jax.random.key(seed), 6)
    return {
        "ensemble": scatter_about(key_list[0], (3, NX, NY, K), 1.0, 6.0, ((1, 32), (2, 16)), jnp.float32),
        "bathymetry": with_ends(jax.random.randint(key_list[1], (NX, NY), 0, LEVELS), jax.random.fold_in(key_list[1], 1), 0, LEVELS - 1).astype(jnp.int32),
        "obs_cell": draw_obs_cell(jax.random.fold_in(key_list[5], 71), 0),
        "obs_value": scatter_about(key_list[3], (N_LON, N_LAT, NOBS), 1.0, 6.0, ((0, 32), (1, 16)), jnp.float32),
        "obs_weight": jnp.clip(jnp.exp(math.log(0.2) - 2.3025851 * jax.random.uniform(key_list[4], (N_LON, N_LAT, NOBS), jnp.float32) ** steps_of(key_list[4], (N_LON, N_LAT, NOBS), ((0, 32), (1, 16)), -0.2, 0.2)), 0.02, 0.2),
    }


time_step = 0.6
gravity = 1.0
rotation = 0.3

def advance(fields, depths, coriolis, inside):
    height = fields[0]
    east_flow = fields[1]
    north_flow = fields[2]
    spread_in = 0.5 * (east_flow[2:, 1:-1] - east_flow[:-2, 1:-1]) + 0.5 * (north_flow[1:-1, 2:] - north_flow[1:-1, :-2])
    new_height = (height[1:-1, 1:-1] - time_step * depths[1:-1, 1:-1, None] * spread_in) * inside[1:-1][None, :, None]
    slope_east = 0.5 * (new_height[2:, 1:-1] - new_height[:-2, 1:-1])
    slope_north = 0.5 * (new_height[1:-1, 2:] - new_height[1:-1, :-2])
    turning = coriolis[2:-2][None, :, None]
    keeper = inside[2:-2][None, :, None]
    new_east = (east_flow[2:-2, 2:-2] + time_step * (turning * north_flow[2:-2, 2:-2] - gravity * slope_east)) * keeper
    new_north = (north_flow[2:-2, 2:-2] + time_step * (-turning * east_flow[2:-2, 2:-2] - gravity * slope_north)) * keeper
    return jnp.stack([new_height[1:-1, 1:-1], new_east, new_north])

def transform_of(gram, projected):
    members = gram.shape[0]
    highest = lax.Precision.HIGHEST
    identity = jnp.eye(members, dtype=jnp.float32)
    system = (members - 1.0) * identity + gram
    scaler = jnp.sqrt(jnp.sum(system * system))
    root = system / scaler
    inverse = identity
    for _ in range(NS_ITERS):
        factor = 1.5 * identity - 0.5 * jnp.dot(inverse, root, precision=highest)
        root = jnp.dot(root, factor, precision=highest)
        inverse = jnp.dot(factor, inverse, precision=highest)
    spread = jnp.sqrt((members - 1.0) / scaler) * inverse
    offset = jnp.dot(inverse, jnp.dot(inverse, projected, precision=highest), precision=highest) / scaler
    return spread + offset[:, None]

def reference(ensemble, bathymetry, obs_cell, obs_value, obs_weight):
    highest = lax.Precision.HIGHEST
    width = 2
    depths = (bathymetry.astype(jnp.float32) + 1.0) / LEVELS
    padded_depth = jnp.pad(jnp.pad(depths, ((width, width), (0, 0)), mode='wrap'), ((0, 0), (width, width)))
    rows = jnp.arange(NY + 2 * width, dtype=jnp.int32) - width
    inside = ((rows >= 0) & (rows < NY)).astype(jnp.float32)
    coriolis = rotation * (2.0 * (rows.astype(jnp.float32) + 0.5) / NY - 1.0)
    state = ensemble
    for _ in range(STEPS):
        extended = jnp.pad(state, ((0, 0), (width, width), (0, 0), (0, 0)), mode='wrap')
        extended = jnp.pad(extended, ((0, 0), (0, 0), (width, width), (0, 0)))
        state = advance(extended, padded_depth, coriolis, inside)
    average = lax.optimization_barrier(jnp.mean(state, axis=-1, keepdims=True))
    anomalies = state - average
    lon_tile = jnp.arange(N_LON, dtype=jnp.int32)[:, None, None]
    lat_tile = jnp.arange(N_LAT, dtype=jnp.int32)[None, :, None]
    per_tile = CX * CY
    field = obs_cell // per_tile
    rest = obs_cell % per_tile
    global_x = lon_tile * CX + rest // CY
    global_y = lat_tile * CY + rest % CY
    flat_index = ((field * NX + global_x) * NY + global_y).reshape(-1).astype(jnp.int32)
    predicted = jnp.take(state.reshape(3 * NX * NY, K), flat_index, axis=0)
    ymean = lax.optimization_barrier(jnp.mean(predicted, axis=-1))
    weight = obs_weight.reshape(-1)
    anomaly_obs = (predicted - ymean[:, None]) * weight[:, None]
    innovation = (obs_value.reshape(-1) - ymean) * weight
    gram = jnp.dot(anomaly_obs.T, anomaly_obs, precision=highest, preferred_element_type=jnp.float32)
    projected = jnp.dot(innovation, anomaly_obs, precision=highest, preferred_element_type=jnp.float32)
    transform = transform_of(gram, projected)
    moved = jnp.dot(anomalies.reshape(-1, K), transform, precision=highest, preferred_element_type=jnp.float32)
    analysis = average + moved.reshape(state.shape)
    return (analysis, transform)
```

```python
import jax
import jax.numpy as jnp
from jax import lax
from jax.sharding import PartitionSpec as P

STEPS = 2
NS_ITERS = 6
LEVELS = 16
REACH = 2 * STEPS

time_step = 0.6
gravity = 1.0
rotation = 0.3


def shift_up(block, axis, wrap):
    count = lax.axis_size(axis)
    pairs = [(i, i + 1) for i in range(count - 1)]
    if wrap:
        pairs.append((count - 1, 0))
    return lax.ppermute(block, axis, pairs)


def shift_down(block, axis, wrap):
    count = lax.axis_size(axis)
    pairs = [(i + 1, i) for i in range(count - 1)]
    if wrap:
        pairs.append((0, count - 1))
    return lax.ppermute(block, axis, pairs)


def with_halo(ensemble, depths):
    fields, tile_lon, tile_lat, members = ensemble.shape

    def lat_message(start):
        cells = lax.slice_in_dim(ensemble, start, start + REACH, axis=2)
        cells = cells.reshape(fields * tile_lon, REACH, members)
        depth = lax.slice_in_dim(depths, start, start + REACH, axis=1).T
        depth = jnp.pad(depth, ((0, 0), (0, members - tile_lon)))
        return jnp.concatenate([cells, depth[None]], axis=0)

    def lat_parts(message):
        cells = message[: fields * tile_lon].reshape(fields, tile_lon, REACH, members)
        return cells, message[fields * tile_lon, :, :tile_lon].T

    low, low_depth = lat_parts(shift_up(lat_message(tile_lat - REACH), "lat", False))
    high, high_depth = lat_parts(shift_down(lat_message(0), "lat", False))
    state = jnp.concatenate([low, ensemble, high], axis=2)
    depth = jnp.concatenate([low_depth, depths, high_depth], axis=1)
    wide = tile_lat + 2 * REACH

    def lon_message(start):
        cells = lax.slice_in_dim(state, start, start + REACH, axis=1)
        cells = cells.reshape(fields * REACH, wide, members)
        strip = lax.slice_in_dim(depth, start, start + REACH, axis=0).T
        strip = jnp.pad(strip, ((0, 0), (0, members - REACH)))
        return jnp.concatenate([cells, strip[None]], axis=0)

    def lon_parts(message):
        cells = message[: fields * REACH].reshape(fields, REACH, wide, members)
        return cells, message[fields * REACH, :, :REACH].T

    low, low_depth = lon_parts(shift_up(lon_message(tile_lon - REACH), "lon", True))
    high, high_depth = lon_parts(shift_down(lon_message(0), "lon", True))
    state = jnp.concatenate([low, state, high], axis=1)
    depth = jnp.concatenate([low_depth, depth, high_depth], axis=0)
    return state, depth


def advance(fields, depths, coriolis, inside):
    height = fields[0]
    east_flow = fields[1]
    north_flow = fields[2]
    spread_in = 0.5 * (east_flow[2:, 1:-1] - east_flow[:-2, 1:-1]) + 0.5 * (
        north_flow[1:-1, 2:] - north_flow[1:-1, :-2]
    )
    new_height = (height[1:-1, 1:-1] - time_step * depths[1:-1, 1:-1, None] * spread_in) * inside[
        1:-1
    ][None, :, None]
    slope_east = 0.5 * (new_height[2:, 1:-1] - new_height[:-2, 1:-1])
    slope_north = 0.5 * (new_height[1:-1, 2:] - new_height[1:-1, :-2])
    turning = coriolis[2:-2][None, :, None]
    keeper = inside[2:-2][None, :, None]
    new_east = (
        east_flow[2:-2, 2:-2]
        + time_step * (turning * north_flow[2:-2, 2:-2] - gravity * slope_east)
    ) * keeper
    new_north = (
        north_flow[2:-2, 2:-2]
        + time_step * (-turning * east_flow[2:-2, 2:-2] - gravity * slope_north)
    ) * keeper
    return jnp.stack([new_height[1:-1, 1:-1], new_east, new_north])


def transform_of(gram, projected):
    members = gram.shape[0]
    highest = lax.Precision.HIGHEST
    identity = jnp.eye(members, dtype=jnp.float32)
    system = (members - 1.0) * identity + gram
    scaler = jnp.sqrt(jnp.sum(system * system))
    root = system / scaler
    inverse = identity
    for _ in range(NS_ITERS):
        factor = 1.5 * identity - 0.5 * jnp.dot(inverse, root, precision=highest)
        root = jnp.dot(root, factor, precision=highest)
        inverse = jnp.dot(factor, inverse, precision=highest)
    spread = jnp.sqrt((members - 1.0) / scaler) * inverse
    offset = (
        jnp.dot(inverse, jnp.dot(inverse, projected, precision=highest), precision=highest) / scaler
    )
    return spread + offset[:, None]


def products(anomaly_obs, innovation):
    highest = lax.Precision.HIGHEST
    gram_part = jnp.dot(
        anomaly_obs.T, anomaly_obs, precision=highest, preferred_element_type=jnp.float32
    )
    proj_part = jnp.dot(
        innovation, anomaly_obs, precision=highest, preferred_element_type=jnp.float32
    )
    return (gram_part, proj_part)


def reduced(gram, projected):
    members = gram.shape[0]
    half = members // 2
    lon = lax.axis_size("lon")
    lat = lax.axis_size("lat")
    packed = jnp.concatenate(
        [
            gram[:half, :half],
            gram[:half, half:],
            gram[half:, half:],
            projected.reshape(2, half),
            jnp.zeros((half - 2, half), jnp.float32),
        ]
    )
    rows = packed.shape[0] // lon
    pieces = lax.all_to_all(packed.reshape(lon, rows, half), "lon", 0, 0)
    piece = jnp.sum(pieces, axis=0)
    pieces = lax.all_to_all(jnp.broadcast_to(piece[None], (lat, rows, half)), "lat", 0, 0)
    piece = jnp.sum(pieces, axis=0)
    pieces = lax.all_to_all(jnp.broadcast_to(piece[None], (lon, rows, half)), "lon", 0, 0)
    packed = pieces.reshape(packed.shape)
    cross = packed[half : 2 * half]
    gram = jnp.concatenate(
        [
            jnp.concatenate([packed[:half], cross], axis=1),
            jnp.concatenate([cross.T, packed[2 * half : 3 * half]], axis=1),
        ]
    )
    return gram, packed[3 * half : 3 * half + 2].reshape(members)


def local(ensemble, bathymetry, obs_cell, obs_value, obs_weight):
    highest = lax.Precision.HIGHEST
    tile_lon = ensemble.shape[1]
    tile_lat = ensemble.shape[2]
    members = ensemble.shape[3]
    total_lat = tile_lat * lax.axis_size("lat")
    depths = (bathymetry.astype(jnp.float32) + 1.0) / LEVELS
    rows = (
        lax.axis_index("lat") * tile_lat - REACH + jnp.arange(tile_lat + 2 * REACH, dtype=jnp.int32)
    )
    inside = ((rows >= 0) & (rows < total_lat)).astype(jnp.float32)
    coriolis = rotation * (2.0 * (rows.astype(jnp.float32) + 0.5) / total_lat - 1.0)
    state, depth_ext = with_halo(ensemble, depths)
    for step in range(STEPS):
        cut = 2 * step
        lon_end = depth_ext.shape[0] - cut
        lat_end = depth_ext.shape[1] - cut
        state = advance(
            state,
            depth_ext[cut:lon_end, cut:lat_end],
            coriolis[cut:lat_end],
            inside[cut:lat_end],
        )
    average = jnp.mean(state, axis=-1, keepdims=True)
    anomalies = state - average
    cells = obs_cell.reshape(-1)
    predicted = jnp.take(state.reshape(3 * tile_lon * tile_lat, members), cells, axis=0)
    ymean = jnp.mean(predicted, axis=-1)
    weight = obs_weight.reshape(-1)
    anomaly_obs = (predicted - ymean[:, None]) * weight[:, None]
    innovation = (obs_value.reshape(-1) - ymean) * weight
    gram, projected = reduced(*products(anomaly_obs, innovation))
    transform = transform_of(gram, projected)
    moved = jnp.dot(
        anomalies.reshape(-1, members),
        transform,
        precision=highest,
        preferred_element_type=jnp.float32,
    )
    analysis = average + moved.reshape(state.shape)
    return (analysis, transform)


def solution(mesh):
    return jax.shard_map(
        local,
        mesh=mesh,
        in_specs=(
            P(None, "lon", "lat", None),
            P("lon", "lat"),
            P("lon", "lat", None),
            P("lon", "lat", None),
            P("lon", "lat", None),
        ),
        out_specs=(P(None, "lon", "lat", None), P()),
        check_vma=False,
    )
```

```python
import functools

import jax
import jax.numpy as jnp
from jax import lax
from jax.experimental import pallas as pl
from jax.experimental.pallas import tpu as pltpu
from jax.sharding import PartitionSpec as P

STEPS = 2
NS_ITERS = 6
LEVELS = 16
REACH = 2 * STEPS
VMEM_BYTES = 24 * 1024 * 1024

time_step = 0.6
gravity = 1.0
rotation = 0.3


def shift_up(block, axis, wrap):
    count = lax.axis_size(axis)
    pairs = [(i, i + 1) for i in range(count - 1)]
    if wrap:
        pairs.append((count - 1, 0))
    return lax.ppermute(block, axis, pairs)


def shift_down(block, axis, wrap):
    count = lax.axis_size(axis)
    pairs = [(i + 1, i) for i in range(count - 1)]
    if wrap:
        pairs.append((0, count - 1))
    return lax.ppermute(block, axis, pairs)


def with_halo(ensemble, depths):
    fields, tile_lon, tile_lat, members = ensemble.shape

    def lat_message(start):
        cells = lax.slice_in_dim(ensemble, start, start + REACH, axis=2)
        cells = cells.reshape(fields * tile_lon, REACH, members)
        depth = lax.slice_in_dim(depths, start, start + REACH, axis=1).T
        depth = jnp.pad(depth, ((0, 0), (0, members - tile_lon)))
        return jnp.concatenate([cells, depth[None]], axis=0)

    def lat_parts(message):
        cells = message[: fields * tile_lon].reshape(fields, tile_lon, REACH, members)
        return cells, message[fields * tile_lon, :, :tile_lon].T

    low, low_depth = lat_parts(shift_up(lat_message(tile_lat - REACH), "lat", False))
    high, high_depth = lat_parts(shift_down(lat_message(0), "lat", False))
    state = jnp.concatenate([low, ensemble, high], axis=2)
    depth = jnp.concatenate([low_depth, depths, high_depth], axis=1)
    wide = tile_lat + 2 * REACH

    def lon_message(start):
        cells = lax.slice_in_dim(state, start, start + REACH, axis=1)
        cells = cells.reshape(fields * REACH, wide, members)
        strip = lax.slice_in_dim(depth, start, start + REACH, axis=0).T
        strip = jnp.pad(strip, ((0, 0), (0, members - REACH)))
        return jnp.concatenate([cells, strip[None]], axis=0)

    def lon_parts(message):
        cells = message[: fields * REACH].reshape(fields, REACH, wide, members)
        return cells, message[fields * REACH, :, :REACH].T

    low, low_depth = lon_parts(shift_up(lon_message(tile_lon - REACH), "lon", True))
    high, high_depth = lon_parts(shift_down(lon_message(0), "lon", True))
    state = jnp.concatenate([low, state, high], axis=1)
    depth = jnp.concatenate([low_depth, depth, high_depth], axis=0)
    return state, depth


def advance(fields, depths, coriolis, inside):
    height = fields[0]
    east_flow = fields[1]
    north_flow = fields[2]
    spread_in = 0.5 * (east_flow[2:, 1:-1] - east_flow[:-2, 1:-1]) + 0.5 * (
        north_flow[1:-1, 2:] - north_flow[1:-1, :-2]
    )
    new_height = (height[1:-1, 1:-1] - time_step * depths[1:-1, 1:-1, None] * spread_in) * inside[
        1:-1
    ][None, :, None]
    slope_east = 0.5 * (new_height[2:, 1:-1] - new_height[:-2, 1:-1])
    slope_north = 0.5 * (new_height[1:-1, 2:] - new_height[1:-1, :-2])
    turning = coriolis[2:-2][None, :, None]
    keeper = inside[2:-2][None, :, None]
    new_east = (
        east_flow[2:-2, 2:-2]
        + time_step * (turning * north_flow[2:-2, 2:-2] - gravity * slope_east)
    ) * keeper
    new_north = (
        north_flow[2:-2, 2:-2]
        + time_step * (-turning * east_flow[2:-2, 2:-2] - gravity * slope_north)
    ) * keeper
    return jnp.stack([new_height[1:-1, 1:-1], new_east, new_north])


def halves(value):
    high = value.astype(jnp.bfloat16)
    return high, (value - high.astype(jnp.float32)).astype(jnp.bfloat16)


def dot3(left, right):
    left_high, left_low = left
    right_high, right_low = right
    dot = functools.partial(jnp.dot, preferred_element_type=jnp.float32)
    return dot(left_high, right_high) + (dot(left_high, right_low) + dot(left_low, right_high))


def finish_kernel(packed_ref, state_ref, analysis_ref, transform_ref):
    half = packed_ref.shape[1]
    members = 2 * half
    square = packed_ref[:half]
    cross = packed_ref[half : 2 * half]
    diagonal = packed_ref[2 * half : 2 * half + 1]
    turned = square.T
    row = lax.broadcasted_iota(jnp.int32, (half, half), 0)
    column = lax.broadcasted_iota(jnp.int32, (half, half), 1)
    first = jnp.where(row <= column, square, turned)
    last = jnp.where(row == column, diagonal, jnp.where(row < column, turned, square))
    gram = jnp.concatenate(
        [jnp.concatenate([first, cross], axis=1), jnp.concatenate([cross.T, last], axis=1)]
    )
    row = lax.broadcasted_iota(jnp.int32, (members, members), 0)
    column = lax.broadcasted_iota(jnp.int32, (members, members), 1)
    on_diagonal = row == column
    system = gram + jnp.where(on_diagonal, members - 1.0, 0.0)
    scaler = jnp.sqrt(
        jnp.sum(jnp.sum(system * system, axis=0, keepdims=True), axis=1, keepdims=True)
    )
    root = system * (1.0 / scaler)
    triple = jnp.where(on_diagonal, 1.5, 0.0)

    inverse = triple - 0.5 * root
    factor = halves(inverse)
    root = halves(dot3(halves(root), factor))
    inverse = factor
    for step in range(1, NS_ITERS):
        factor = halves(triple - 0.5 * dot3(inverse, root))
        if step < NS_ITERS - 1:
            root = halves(dot3(root, factor))
            inverse = halves(dot3(factor, inverse))
        else:
            inverse = dot3(factor, inverse)
    projected = jnp.concatenate(
        [packed_ref[2 * half + 1 : 2 * half + 2], packed_ref[2 * half + 2 : 2 * half + 3]], axis=1
    )
    once = jnp.sum(inverse * projected, axis=1, keepdims=True)
    once = jnp.sum(jnp.where(on_diagonal, once, 0.0), axis=0, keepdims=True)
    offset = jnp.sum(inverse * once, axis=1, keepdims=True) / scaler
    transform = jnp.sqrt((members - 1.0) / scaler) * inverse + offset
    transform_ref[...] = transform
    transform = halves(transform)
    block = 256
    for start in range(0, state_ref.shape[0], block):
        state = state_ref[start : start + block]
        average = jnp.sum(state, axis=1, keepdims=True) * (1.0 / members)
        analysis_ref[start : start + block] = average + dot3(halves(state - average), transform)


def finish(packed, state):
    vmem = pl.BlockSpec(memory_space=pltpu.VMEM)
    members = state.shape[1]
    return pl.pallas_call(
        finish_kernel,
        out_shape=(
            jax.ShapeDtypeStruct(state.shape, jnp.float32),
            jax.ShapeDtypeStruct((members, members), jnp.float32),
        ),
        in_specs=[vmem, vmem],
        out_specs=(vmem, vmem),
        compiler_params=pltpu.CompilerParams(vmem_limit_bytes=VMEM_BYTES),
    )(packed, state)


def products(anomaly_obs, innovation):
    highest = lax.Precision.HIGHEST
    gram_part = jnp.dot(
        anomaly_obs.T, anomaly_obs, precision=highest, preferred_element_type=jnp.float32
    )
    proj_part = jnp.dot(
        innovation, anomaly_obs, precision=highest, preferred_element_type=jnp.float32
    )
    return (gram_part, proj_part)


def reduced(gram, projected):
    members = gram.shape[0]
    half = members // 2
    lon = lax.axis_size("lon")
    lat = lax.axis_size("lat")
    first = gram[:half, :half]
    last = gram[half:, half:]
    line = jnp.arange(half)
    upper = line[:, None] <= line[None, :]
    packed = jnp.concatenate(
        [
            jnp.where(upper, first, last),
            gram[:half, half:],
            jnp.sum(jnp.where(line[:, None] == line[None, :], last, 0.0), axis=0)[None],
            projected.reshape(2, half),
            jnp.zeros((lon - 3, half), jnp.float32),
        ]
    )
    width = packed.size // lon
    pieces = lax.all_to_all(packed.reshape(lon, 1, width), "lon", 0, 0)
    piece = jnp.sum(pieces, axis=0)
    pieces = lax.all_to_all(jnp.broadcast_to(piece[None], (lat, 1, width)), "lat", 0, 0)
    piece = jnp.sum(pieces, axis=0)
    pieces = lax.all_to_all(jnp.broadcast_to(piece[None], (lon, 1, width)), "lon", 0, 0)
    return pieces.reshape(packed.shape)


def local(ensemble, bathymetry, obs_cell, obs_value, obs_weight):
    tile_lon = ensemble.shape[1]
    tile_lat = ensemble.shape[2]
    members = ensemble.shape[3]
    total_lat = tile_lat * lax.axis_size("lat")
    depths = (bathymetry.astype(jnp.float32) + 1.0) / LEVELS
    rows = (
        lax.axis_index("lat") * tile_lat - REACH + jnp.arange(tile_lat + 2 * REACH, dtype=jnp.int32)
    )
    inside = ((rows >= 0) & (rows < total_lat)).astype(jnp.float32)
    coriolis = rotation * (2.0 * (rows.astype(jnp.float32) + 0.5) / total_lat - 1.0)
    state, depth_ext = with_halo(ensemble, depths)
    for step in range(STEPS):
        cut = 2 * step
        lon_end = depth_ext.shape[0] - cut
        lat_end = depth_ext.shape[1] - cut
        state = advance(
            state,
            depth_ext[cut:lon_end, cut:lat_end],
            coriolis[cut:lat_end],
            inside[cut:lat_end],
        )
    shape = state.shape
    state = state.reshape(3 * tile_lon * tile_lat, members)
    cells = obs_cell.reshape(-1)
    predicted = jnp.take(state, cells, axis=0)
    ymean = jnp.mean(predicted, axis=-1)
    weight = obs_weight.reshape(-1)
    anomaly_obs = (predicted - ymean[:, None]) * weight[:, None]
    innovation = (obs_value.reshape(-1) - ymean) * weight
    packed = reduced(*products(anomaly_obs, innovation))
    analysis, transform = finish(packed, state)
    return (analysis.reshape(shape), transform)


def solution(mesh):
    return jax.shard_map(
        local,
        mesh=mesh,
        in_specs=(
            P(None, "lon", "lat", None),
            P("lon", "lat"),
            P("lon", "lat", None),
            P("lon", "lat", None),
            P("lon", "lat", None),
        ),
        out_specs=(P(None, "lon", "lat", None), P()),
        check_vma=False,
    )
```

```python
import functools

import jax
import jax.numpy as jnp
from jax import lax
from jax.experimental import pallas as pl
from jax.experimental.pallas import tpu as pltpu
from jax.sharding import PartitionSpec as P

STEPS = 2
NS_ITERS = 6
LEVELS = 16
REACH = 2 * STEPS
VMEM_BYTES = 24 * 1024 * 1024

time_step = 0.6
gravity = 1.0
rotation = 0.3


def swaps(edge, axis, wrap):
    count = lax.axis_size(axis)
    even = lax.axis_index(axis) % 2 == 0
    across = [(i, i + 1) for i in range(1, count - 1, 2)]
    if wrap:
        across.append((count - 1, 0))
    within = [(i, i + 1) for i in range(0, count, 2)]
    first = lax.ppermute(edge(~even), axis, across + [(j, i) for i, j in across])
    second = lax.ppermute(edge(even), axis, within + [(j, i) for i, j in within])
    low = jnp.where(even, first, second)
    high = jnp.where(even, second, first)
    return low, high


def with_halo(ensemble, depths):
    fields, tile_lon, tile_lat, members = ensemble.shape

    def lat_message(upper):
        start = jnp.where(upper, tile_lat - REACH, 0)
        cells = lax.dynamic_slice_in_dim(ensemble, start, REACH, axis=2)
        cells = cells.reshape(fields * tile_lon, REACH, members)
        depth = lax.dynamic_slice_in_dim(depths, start, REACH, axis=1).T
        depth = jnp.pad(depth, ((0, 0), (0, members - tile_lon)))
        return jnp.concatenate([cells, depth[None]], axis=0)

    def lat_parts(message):
        cells = message[: fields * tile_lon].reshape(fields, tile_lon, REACH, members)
        return cells, message[fields * tile_lon, :, :tile_lon].T

    low, high = swaps(lat_message, "lat", False)
    low, low_depth = lat_parts(low)
    high, high_depth = lat_parts(high)
    state = jnp.concatenate([low, ensemble, high], axis=2)
    depth = jnp.concatenate([low_depth, depths, high_depth], axis=1)
    wide = tile_lat + 2 * REACH

    def lon_message(upper):
        start = jnp.where(upper, tile_lon - REACH, 0)
        cells = lax.dynamic_slice_in_dim(state, start, REACH, axis=1)
        cells = cells.reshape(fields * REACH, wide, members)
        strip = lax.dynamic_slice_in_dim(depth, start, REACH, axis=0).T
        strip = jnp.pad(strip, ((0, 0), (0, members - REACH)))
        return jnp.concatenate([cells, strip[None]], axis=0)

    def lon_parts(message):
        cells = message[: fields * REACH].reshape(fields, REACH, wide, members)
        return cells, message[fields * REACH, :, :REACH].T

    low, high = swaps(lon_message, "lon", True)
    low, low_depth = lon_parts(low)
    high, high_depth = lon_parts(high)
    state = jnp.concatenate([low, state, high], axis=1)
    depth = jnp.concatenate([low_depth, depth, high_depth], axis=0)
    return state, depth


def advance(fields, depths, coriolis, inside):
    height = fields[0]
    east_flow = fields[1]
    north_flow = fields[2]
    spread_in = 0.5 * (east_flow[2:, 1:-1] - east_flow[:-2, 1:-1]) + 0.5 * (
        north_flow[1:-1, 2:] - north_flow[1:-1, :-2]
    )
    new_height = (height[1:-1, 1:-1] - time_step * depths[1:-1, 1:-1, None] * spread_in) * inside[
        1:-1
    ][None, :, None]
    slope_east = 0.5 * (new_height[2:, 1:-1] - new_height[:-2, 1:-1])
    slope_north = 0.5 * (new_height[1:-1, 2:] - new_height[1:-1, :-2])
    turning = coriolis[2:-2][None, :, None]
    keeper = inside[2:-2][None, :, None]
    new_east = (
        east_flow[2:-2, 2:-2]
        + time_step * (turning * north_flow[2:-2, 2:-2] - gravity * slope_east)
    ) * keeper
    new_north = (
        north_flow[2:-2, 2:-2]
        + time_step * (-turning * east_flow[2:-2, 2:-2] - gravity * slope_north)
    ) * keeper
    return jnp.stack([new_height[1:-1, 1:-1], new_east, new_north])


def halves(value):
    high = value.astype(jnp.bfloat16)
    return high, (value - high.astype(jnp.float32)).astype(jnp.bfloat16)


def dot3(left, right):
    left_high, left_low = left
    right_high, right_low = right
    dot = functools.partial(jnp.dot, preferred_element_type=jnp.float32)
    return dot(left_high, right_high) + (dot(left_high, right_low) + dot(left_low, right_high))


def finish_kernel(packed_ref, state_ref, analysis_ref, transform_ref):
    half = packed_ref.shape[1]
    members = 2 * half
    square = packed_ref[:half]
    cross = packed_ref[half : 2 * half]
    diagonal = packed_ref[2 * half : 2 * half + 1]
    turned = square.T
    row = lax.broadcasted_iota(jnp.int32, (half, half), 0)
    column = lax.broadcasted_iota(jnp.int32, (half, half), 1)
    first = jnp.where(row <= column, square, turned)
    last = jnp.where(row == column, diagonal, jnp.where(row < column, turned, square))
    gram = jnp.concatenate(
        [jnp.concatenate([first, cross], axis=1), jnp.concatenate([cross.T, last], axis=1)]
    )
    row = lax.broadcasted_iota(jnp.int32, (members, members), 0)
    column = lax.broadcasted_iota(jnp.int32, (members, members), 1)
    on_diagonal = row == column
    system = gram + jnp.where(on_diagonal, members - 1.0, 0.0)
    scaler = jnp.sqrt(
        jnp.sum(jnp.sum(system * system, axis=0, keepdims=True), axis=1, keepdims=True)
    )
    root = system * (1.0 / scaler)
    triple = jnp.where(on_diagonal, 1.5, 0.0)

    inverse = triple - 0.5 * root
    factor = halves(inverse)
    root = halves(dot3(halves(root), factor))
    inverse = factor
    for step in range(1, NS_ITERS):
        factor = halves(triple - 0.5 * dot3(inverse, root))
        if step < NS_ITERS - 1:
            root = halves(dot3(root, factor))
            inverse = halves(dot3(factor, inverse))
        else:
            inverse = dot3(factor, inverse)
    projected = jnp.concatenate(
        [packed_ref[2 * half + 1 : 2 * half + 2], packed_ref[2 * half + 2 : 2 * half + 3]], axis=1
    )
    once = jnp.sum(inverse * projected, axis=1, keepdims=True)
    once = jnp.sum(jnp.where(on_diagonal, once, 0.0), axis=0, keepdims=True)
    offset = jnp.sum(inverse * once, axis=1, keepdims=True) / scaler
    transform = jnp.sqrt((members - 1.0) / scaler) * inverse + offset
    transform_ref[...] = transform
    transform = halves(transform)
    block = 256
    for start in range(0, state_ref.shape[0], block):
        state = state_ref[start : start + block]
        average = jnp.sum(state, axis=1, keepdims=True) * (1.0 / members)
        analysis_ref[start : start + block] = average + dot3(halves(state - average), transform)


def finish(packed, state):
    vmem = pl.BlockSpec(memory_space=pltpu.VMEM)
    members = state.shape[1]
    return pl.pallas_call(
        finish_kernel,
        out_shape=(
            jax.ShapeDtypeStruct(state.shape, jnp.float32),
            jax.ShapeDtypeStruct((members, members), jnp.float32),
        ),
        in_specs=[vmem, vmem],
        out_specs=(vmem, vmem),
        compiler_params=pltpu.CompilerParams(vmem_limit_bytes=VMEM_BYTES),
    )(packed, state)


def products(anomaly_obs, innovation):
    highest = lax.Precision.HIGHEST
    gram_part = jnp.dot(
        anomaly_obs.T, anomaly_obs, precision=highest, preferred_element_type=jnp.float32
    )
    proj_part = jnp.dot(
        innovation, anomaly_obs, precision=highest, preferred_element_type=jnp.float32
    )
    return (gram_part, proj_part)


def reduced(gram, projected):
    members = gram.shape[0]
    half = members // 2
    lon = lax.axis_size("lon")
    lat = lax.axis_size("lat")
    first = gram[:half, :half]
    last = gram[half:, half:]
    line = jnp.arange(half)
    upper = line[:, None] <= line[None, :]
    packed = jnp.concatenate(
        [
            jnp.where(upper, first, last),
            gram[:half, half:],
            jnp.sum(jnp.where(line[:, None] == line[None, :], last, 0.0), axis=0)[None],
            projected.reshape(2, half),
            jnp.zeros((lon - 3, half), jnp.float32),
        ]
    )
    width = packed.size // lon
    pieces = lax.all_to_all(packed.reshape(lon, 1, width), "lon", 0, 0)
    piece = jnp.sum(pieces, axis=0)
    pieces = lax.all_to_all(jnp.broadcast_to(piece[None], (lat, 1, width)), "lat", 0, 0)
    piece = jnp.sum(pieces, axis=0)
    pieces = lax.all_to_all(jnp.broadcast_to(piece[None], (lon, 1, width)), "lon", 0, 0)
    return pieces.reshape(packed.shape)


def local(ensemble, bathymetry, obs_cell, obs_value, obs_weight):
    tile_lon = ensemble.shape[1]
    tile_lat = ensemble.shape[2]
    members = ensemble.shape[3]
    total_lat = tile_lat * lax.axis_size("lat")
    depths = (bathymetry.astype(jnp.float32) + 1.0) / LEVELS
    rows = (
        lax.axis_index("lat") * tile_lat - REACH + jnp.arange(tile_lat + 2 * REACH, dtype=jnp.int32)
    )
    inside = ((rows >= 0) & (rows < total_lat)).astype(jnp.float32)
    coriolis = rotation * (2.0 * (rows.astype(jnp.float32) + 0.5) / total_lat - 1.0)
    state, depth_ext = with_halo(ensemble, depths)
    for step in range(STEPS):
        cut = 2 * step
        lon_end = depth_ext.shape[0] - cut
        lat_end = depth_ext.shape[1] - cut
        state = advance(
            state,
            depth_ext[cut:lon_end, cut:lat_end],
            coriolis[cut:lat_end],
            inside[cut:lat_end],
        )
    shape = state.shape
    state = state.reshape(3 * tile_lon * tile_lat, members)
    cells = obs_cell.reshape(-1)
    predicted = jnp.take(state, cells, axis=0)
    ymean = jnp.mean(predicted, axis=-1)
    weight = obs_weight.reshape(-1)
    anomaly_obs = (predicted - ymean[:, None]) * weight[:, None]
    innovation = (obs_value.reshape(-1) - ymean) * weight
    packed = reduced(*products(anomaly_obs, innovation))
    analysis, transform = finish(packed, state)
    return (analysis.reshape(shape), transform)


def solution(mesh):
    return jax.shard_map(
        local,
        mesh=mesh,
        in_specs=(
            P(None, "lon", "lat", None),
            P("lon", "lat"),
            P("lon", "lat", None),
            P("lon", "lat", None),
            P("lon", "lat", None),
        ),
        out_specs=(P(None, "lon", "lat", None), P()),
        check_vma=False,
    )
```

```python
import functools

import jax
import jax.numpy as jnp
from jax import lax
from jax.experimental import pallas as pl
from jax.experimental.pallas import tpu as pltpu
from jax.sharding import PartitionSpec as P

STEPS = 2
NS_ITERS = 6
LEVELS = 16
REACH = 2 * STEPS
VMEM_BYTES = 24 * 1024 * 1024
TILE = 16
LAT_ROWS = (3, 3, 4)
ROWS = sum(LAT_ROWS)
LON_ROWS = 192

time_step = 0.6
gravity = 1.0
rotation = 0.3


def shift_up(block, axis, wrap):
    count = lax.axis_size(axis)
    pairs = [(i, i + 1) for i in range(count - 1)]
    if wrap:
        pairs.append((count - 1, 0))
    return lax.ppermute(block, axis, pairs)


def shift_down(block, axis, wrap):
    count = lax.axis_size(axis)
    pairs = [(i + 1, i) for i in range(count - 1)]
    if wrap:
        pairs.append((0, count - 1))
    return lax.ppermute(block, axis, pairs)


def pack_lat_kernel(state_ref, bottom_ref, up_ref, down_ref, depth_ref, square_ref):
    lon, lat = state_ref.shape[1], state_ref.shape[2]
    square_ref[...] = jnp.zeros_like(square_ref)
    square_ref[:lon, :lat] = (bottom_ref[...].astype(jnp.float32) + 1.0) * (1.0 / LEVELS)
    turned = square_ref[...].T[:lat]
    depth_ref[...] = turned
    depth_at = ROWS * lon
    for ref in (up_ref, down_ref):
        ref[depth_at:] = jnp.zeros((ref.shape[0] - depth_at, ref.shape[1]), jnp.float32)
    up_ref[depth_at : depth_at + 3, :128] = turned[lat - 3 : lat]
    down_ref[depth_at : depth_at + 3, :128] = turned[:3]
    for field, count in enumerate(LAT_ROWS):
        for x in range(lon):
            at = lon * sum(LAT_ROWS[:field]) + x * count
            plane = state_ref[field, x]
            up_ref[at : at + count] = plane[lat - count :]
            down_ref[at : at + count] = plane[:count]


def lat_rows(ref, field, x, lon):
    at = lon * sum(LAT_ROWS[:field]) + x * LAT_ROWS[field]
    return ref[at : at + LAT_ROWS[field]]


def lon_layout():
    at = 0
    for field, width, reach in ((0, 3, 3), (1, 4, 4), (2, 3, 4)):
        for distance in range(1, width + 1):
            beyond = reach - distance
            yield field, distance, beyond, at
            at += TILE + 2 * beyond


def pack_lon_kernel(state_ref, low_ref, high_ref, depth_ref, up_ref, down_ref, strip_ref):
    lon = state_ref.shape[1]
    depth_at = ROWS * lon
    strip_ref[...] = jnp.zeros_like(strip_ref)
    strip_ref[1:4] = low_ref[depth_at : depth_at + 3, :128]
    strip_ref[4:20] = depth_ref[...]
    strip_ref[20:23] = high_ref[depth_at : depth_at + 3, :128]
    for ref in (up_ref, down_ref):
        ref[LON_ROWS:, 128:] = jnp.zeros((ref.shape[0] - LON_ROWS, 128), jnp.float32)
        ref[LON_ROWS - 2 : LON_ROWS] = jnp.zeros((2, ref.shape[1]), jnp.float32)
        ref[LON_ROWS:, :128] = strip_ref[...]
    for field, distance, beyond, at in lon_layout():
        for ref, x in ((up_ref, lon - distance), (down_ref, distance - 1)):
            if beyond:
                low = lat_rows(low_ref, field, x, lon)
                ref[at : at + beyond] = low[LAT_ROWS[field] - beyond :]
                high = lat_rows(high_ref, field, x, lon)
                ref[at + beyond + TILE : at + TILE + 2 * beyond] = high[:beyond]
            ref[at + beyond : at + beyond + TILE] = state_ref[field, x]


def dot3_first(left, right):
    dims = (((0,), (0,)), ((), ()))
    dot = functools.partial(lax.dot_general, dimension_numbers=dims, preferred_element_type=jnp.float32)
    left_high, left_low = left
    right_high, right_low = right
    return dot(left_high, right_high) + (dot(left_high, right_low) + dot(left_low, right_high))


def step_kernel(
    state_ref,
    low_ref,
    high_ref,
    west_ref,
    east_ref,
    strip_ref,
    turning_ref,
    inside_ref,
    cell_ref,
    value_ref,
    weight_ref,
    forecast_ref,
    packed_ref,
    field_ref,
    next_ref,
    last_ref,
    picked_ref,
):
    lon = state_ref.shape[1]
    members = state_ref.shape[3]
    wide = TILE + 2 * REACH
    for field, count in enumerate(LAT_ROWS):
        for x in range(lon):
            field_ref[field, REACH + x, REACH : REACH + TILE] = state_ref[field, x]
            field_ref[field, REACH + x, REACH - count : REACH] = lat_rows(low_ref, field, x, lon)
            field_ref[field, REACH + x, REACH + TILE : REACH + TILE + count] = lat_rows(
                high_ref, field, x, lon
            )
    for field, distance, beyond, at in lon_layout():
        rows = slice(REACH - beyond, REACH + TILE + beyond)
        taken = slice(at, at + TILE + 2 * beyond)
        field_ref[field, REACH - distance, rows] = west_ref[taken]
        field_ref[field, REACH + lon - 1 + distance, rows] = east_ref[taken]
    turning = time_step * jnp.broadcast_to(turning_ref[:, :1], (wide, members))
    keeper = jnp.broadcast_to(inside_ref[:, :1], (wide, members))
    pull = 0.5 * time_step * gravity

    def column(x):
        if x < REACH:
            depth = west_ref[LON_ROWS:, lon - REACH + x : lon - REACH + x + 1]
        elif x < REACH + lon:
            depth = strip_ref[:, x - REACH : x - REACH + 1]
        else:
            depth = east_ref[LON_ROWS:, x - REACH - lon : x - REACH - lon + 1]
        return jnp.broadcast_to(0.5 * time_step * depth, (wide, members))

    def along(plane):
        return pltpu.roll(plane, wide - 1, 0) - pltpu.roll(plane, 1, 0)

    def advance_height(source, target, x):
        spread = source[1, x + 1] - source[1, x - 1] + along(source[2, x])
        target[0, x] = source[0, x] - column(x) * spread

    def advance_flow(source, heights, x):
        east = source[1, x]
        north = source[2, x]
        slope_east = heights[0, x + 1] - heights[0, x - 1]
        slope_north = along(heights[0, x])
        return (
            east + (turning * north - pull * slope_east),
            north - (turning * east + pull * slope_north),
        )

    for x in range(1, wide - 1):
        advance_height(field_ref, next_ref, x)
    for x in range(2, wide - 2):
        east, north = advance_flow(field_ref, next_ref, x)
        next_ref[1, x] = east
        next_ref[2, x] = north * keeper
    for x in range(3, wide - 3):
        advance_height(next_ref, last_ref, x)
    for x in range(REACH, REACH + lon):
        east, north = advance_flow(next_ref, last_ref, x)
        for field, plane in enumerate((last_ref[0, x], east, north)):
            at = (field * lon + x - REACH) * TILE
            forecast_ref[at : at + TILE] = plane[REACH : REACH + TILE]

    count = picked_ref.shape[0]
    for k in range(count):
        picked_ref[k : k + 1] = forecast_ref[pl.ds(cell_ref[0, 0, k], 1)]
    picked = picked_ref[...]
    ymean = jnp.sum(picked, axis=1, keepdims=True) * (1.0 / members)
    half = members // 2
    row = lax.broadcasted_iota(jnp.int32, (half, half), 0)
    line = lax.broadcasted_iota(jnp.int32, (half, half), 1)
    on_diagonal = row == line
    weight = jnp.sum(jnp.where(on_diagonal, weight_ref[0], 0.0), axis=1, keepdims=True)
    value = jnp.sum(jnp.where(on_diagonal, value_ref[0], 0.0), axis=1, keepdims=True)
    anomaly = (picked - ymean) * weight
    innovation = (value - ymean) * weight
    projected = jnp.sum(innovation * anomaly, axis=0, keepdims=True)
    left_high, left_low = halves(anomaly[:, :half])
    right_high, right_low = halves(anomaly[:, half:])
    first = dot3_first((left_high, left_low), (left_high, left_low))
    cross = dot3_first((left_high, left_low), (right_high, right_low))
    final = dot3_first((right_high, right_low), (right_high, right_low))
    packed_ref[:half] = jnp.where(row <= line, first, final)
    packed_ref[half : 2 * half] = cross
    packed_ref[2 * half :] = jnp.zeros((packed_ref.shape[0] - 2 * half, half), jnp.float32)
    packed_ref[2 * half : 2 * half + 1] = jnp.sum(
        jnp.where(on_diagonal, final, 0.0), axis=0, keepdims=True
    )
    packed_ref[2 * half + 1 : 2 * half + 2] = projected[:, :half]
    packed_ref[2 * half + 2 : 2 * half + 3] = projected[:, half:]


def on_core(kernel, outs, spaces, scratch):
    return pl.pallas_call(
        kernel,
        out_shape=tuple(jax.ShapeDtypeStruct(shape, jnp.float32) for shape in outs),
        in_specs=[pl.BlockSpec(memory_space=space) for space in spaces],
        out_specs=tuple(pl.BlockSpec(memory_space=pltpu.VMEM) for _ in outs),
        scratch_shapes=scratch,
        compiler_params=pltpu.CompilerParams(vmem_limit_bytes=VMEM_BYTES),
    )


def halves(value):
    high = value.astype(jnp.bfloat16)
    return high, (value - high.astype(jnp.float32)).astype(jnp.bfloat16)


def dot3(left, right):
    left_high, left_low = left
    right_high, right_low = right
    dot = functools.partial(jnp.dot, preferred_element_type=jnp.float32)
    return dot(left_high, right_high) + (dot(left_high, right_low) + dot(left_low, right_high))


def finish_kernel(packed_ref, state_ref, analysis_ref, transform_ref):
    half = packed_ref.shape[1]
    members = 2 * half
    square = packed_ref[:half]
    cross = packed_ref[half : 2 * half]
    diagonal = packed_ref[2 * half : 2 * half + 1]
    turned = square.T
    row = lax.broadcasted_iota(jnp.int32, (half, half), 0)
    column = lax.broadcasted_iota(jnp.int32, (half, half), 1)
    first = jnp.where(row <= column, square, turned)
    last = jnp.where(row == column, diagonal, jnp.where(row < column, turned, square))
    gram = jnp.concatenate(
        [jnp.concatenate([first, cross], axis=1), jnp.concatenate([cross.T, last], axis=1)]
    )
    row = lax.broadcasted_iota(jnp.int32, (members, members), 0)
    column = lax.broadcasted_iota(jnp.int32, (members, members), 1)
    on_diagonal = row == column
    system = gram + jnp.where(on_diagonal, members - 1.0, 0.0)
    scaler = jnp.sqrt(
        jnp.sum(jnp.sum(system * system, axis=0, keepdims=True), axis=1, keepdims=True)
    )
    root = system * (1.0 / scaler)
    triple = jnp.where(on_diagonal, 1.5, 0.0)

    inverse = triple - 0.5 * root
    factor = halves(inverse)
    root = halves(dot3(halves(root), factor))
    inverse = factor
    for step in range(1, NS_ITERS):
        factor = halves(triple - 0.5 * dot3(inverse, root))
        if step < NS_ITERS - 1:
            root = halves(dot3(root, factor))
            inverse = halves(dot3(factor, inverse))
        else:
            inverse = dot3(factor, inverse)
    projected = jnp.concatenate(
        [packed_ref[2 * half + 1 : 2 * half + 2], packed_ref[2 * half + 2 : 2 * half + 3]], axis=1
    )
    once = jnp.sum(inverse * projected, axis=1, keepdims=True)
    once = jnp.sum(jnp.where(on_diagonal, once, 0.0), axis=0, keepdims=True)
    offset = jnp.sum(inverse * once, axis=1, keepdims=True) / scaler
    transform = jnp.sqrt((members - 1.0) / scaler) * inverse + offset
    transform_ref[...] = transform
    transform = halves(transform)
    block = 256
    for start in range(0, state_ref.shape[0], block):
        state = state_ref[start : start + block]
        average = jnp.sum(state, axis=1, keepdims=True) * (1.0 / members)
        analysis_ref[start : start + block] = average + dot3(halves(state - average), transform)


def finish(packed, state):
    vmem = pl.BlockSpec(memory_space=pltpu.VMEM)
    members = state.shape[1]
    return pl.pallas_call(
        finish_kernel,
        out_shape=(
            jax.ShapeDtypeStruct(state.shape, jnp.float32),
            jax.ShapeDtypeStruct((members, members), jnp.float32),
        ),
        in_specs=[vmem, vmem],
        out_specs=(vmem, vmem),
        compiler_params=pltpu.CompilerParams(vmem_limit_bytes=VMEM_BYTES),
    )(packed, state)


def reduced(packed):
    lon = lax.axis_size("lon")
    lat = lax.axis_size("lat")
    width = packed.size // lon
    pieces = lax.all_to_all(packed.reshape(lon, 1, width), "lon", 0, 0)
    piece = jnp.sum(pieces, axis=0)
    pieces = lax.all_to_all(jnp.broadcast_to(piece[None], (lat, 1, width)), "lat", 0, 0)
    piece = jnp.sum(pieces, axis=0)
    pieces = lax.all_to_all(jnp.broadcast_to(piece[None], (lon, 1, width)), "lon", 0, 0)
    return pieces.reshape(packed.shape)


def local(ensemble, bathymetry, obs_cell, obs_value, obs_weight):
    fields, lon, lat, members = ensemble.shape
    vmem = pltpu.VMEM
    total_lat = lat * lax.axis_size("lat")
    wide = lat + 2 * REACH
    rows = lax.axis_index("lat") * lat - REACH + lax.broadcasted_iota(jnp.int32, (wide, 128), 0)
    inside = ((rows >= 0) & (rows < total_lat)).astype(jnp.float32)
    turning = rotation * (2.0 * (rows.astype(jnp.float32) + 0.5) / total_lat - 1.0)
    lat_shape = (ROWS * lon + 8, members)
    lon_shape = (LON_ROWS + wide, members)
    up, down, depth = on_core(
        pack_lat_kernel,
        (lat_shape, lat_shape, (lat, 128)),
        [vmem] * 2,
        [pltpu.VMEM((128, 128), jnp.float32)],
    )(ensemble, bathymetry)
    low = shift_up(up, "lat", False)
    high = shift_down(down, "lat", False)
    up, down, strip = on_core(
        pack_lon_kernel, (lon_shape, lon_shape, (wide, 128)), [vmem] * 4, []
    )(ensemble, low, high, depth)
    west = shift_up(up, "lon", True)
    east = shift_down(down, "lon", True)
    planes = (fields, lon + 2 * REACH, wide, members)
    forecast, packed = on_core(
        step_kernel,
        ((fields * lon * lat, members), (members + 32, members // 2)),
        [vmem] * 8 + [pltpu.SMEM] + [vmem] * 2,
        [pltpu.VMEM(planes, jnp.float32)] * 2
        + [pltpu.VMEM((1,) + planes[1:], jnp.float32)]
        + [pltpu.VMEM((obs_cell.shape[2], members), jnp.float32)],
    )(ensemble, low, high, west, east, strip, turning, inside, obs_cell, obs_value, obs_weight)
    analysis, transform = finish(reduced(packed), forecast)
    return (analysis.reshape(ensemble.shape), transform)


def solution(mesh):
    return jax.shard_map(
        local,
        mesh=mesh,
        in_specs=(
            P(None, "lon", "lat", None),
            P("lon", "lat"),
            P("lon", "lat", None),
            P("lon", "lat", None),
            P("lon", "lat", None),
        ),
        out_specs=(P(None, "lon", "lat", None), P()),
        check_vma=False,
    )
```

```python
import functools

import jax
import jax.numpy as jnp
from jax import lax
from jax.experimental import pallas as pl
from jax.experimental.pallas import tpu as pltpu
from jax.sharding import PartitionSpec as P

STEPS = 2
NS_ITERS = 6
LEVELS = 16
REACH = 2 * STEPS
VMEM_BYTES = 24 * 1024 * 1024
TILE = 16
LAT_ROWS = (3, 3, 4)
ROWS = sum(LAT_ROWS)
LON_ROWS = 192

time_step = 0.6
gravity = 1.0
rotation = 0.3


def shift_up(block, axis, wrap):
    count = lax.axis_size(axis)
    pairs = [(i, i + 1) for i in range(count - 1)]
    if wrap:
        pairs.append((count - 1, 0))
    return lax.ppermute(block, axis, pairs)


def shift_down(block, axis, wrap):
    count = lax.axis_size(axis)
    pairs = [(i + 1, i) for i in range(count - 1)]
    if wrap:
        pairs.append((0, count - 1))
    return lax.ppermute(block, axis, pairs)


def fetch(sources, targets, sems):
    copies = [
        pltpu.make_async_copy(source, target, sems.at[k])
        for k, (source, target) in enumerate(zip(sources, targets))
    ]
    for copy in copies:
        copy.start()
    return copies


def pack_lat_kernel(
    even_ref, ensemble_ref, bathymetry_ref, first_ref, second_ref, depth_ref, state_ref, bottom_ref, square_ref, sems
):
    lon, lat = state_ref.shape[1], state_ref.shape[2]
    copies = fetch((bathymetry_ref, ensemble_ref), (bottom_ref, state_ref), sems)
    square_ref[...] = jnp.zeros_like(square_ref)
    depth_at = ROWS * lon
    for ref in (first_ref, second_ref):
        ref[depth_at:] = jnp.zeros((ref.shape[0] - depth_at, ref.shape[1]), jnp.float32)
    copies[0].wait()
    square_ref[:lon, :lat] = (bottom_ref[...].astype(jnp.float32) + 1.0) * (1.0 / LEVELS)
    turned = square_ref[...].T[:lat]
    depth_ref[...] = turned
    copies[1].wait()

    def pack(up_ref, down_ref):
        up_ref[depth_at : depth_at + 3, :128] = turned[lat - 3 : lat]
        down_ref[depth_at : depth_at + 3, :128] = turned[:3]
        for field, count in enumerate(LAT_ROWS):
            for x in range(lon):
                at = lon * sum(LAT_ROWS[:field]) + x * count
                plane = state_ref[field, x]
                up_ref[at : at + count] = plane[lat - count :]
                down_ref[at : at + count] = plane[:count]

    @pl.when(even_ref[0] == 1)
    def _():
        pack(first_ref, second_ref)

    @pl.when(even_ref[0] != 1)
    def _():
        pack(second_ref, first_ref)


def chosen(even, first_ref, second_ref, rows, lanes=slice(None)):
    return jnp.where(even, first_ref[rows, lanes], second_ref[rows, lanes])


def lat_rows(even, first_ref, second_ref, field, x, lon):
    at = lon * sum(LAT_ROWS[:field]) + x * LAT_ROWS[field]
    return chosen(even, first_ref, second_ref, slice(at, at + LAT_ROWS[field]))


def lon_layout():
    at = 0
    for field, width, reach in ((0, 3, 3), (1, 4, 4), (2, 3, 4)):
        for distance in range(1, width + 1):
            beyond = reach - distance
            yield field, distance, beyond, at
            at += TILE + 2 * beyond


def pack_lon_kernel(
    even_ref, state_ref, first_ref, second_ref, depth_ref, up_ref, down_ref, strip_ref
):
    lon = state_ref.shape[1]
    even = even_ref[0] == 1
    low_rows = functools.partial(lat_rows, even, first_ref, second_ref)
    high_rows = functools.partial(lat_rows, even, second_ref, first_ref)
    depth_at = ROWS * lon
    strip_ref[...] = jnp.zeros_like(strip_ref)
    depths = slice(depth_at, depth_at + 3)
    strip_ref[1:4] = chosen(even, first_ref, second_ref, depths, slice(0, 128))
    strip_ref[4:20] = depth_ref[...]
    strip_ref[20:23] = chosen(even, second_ref, first_ref, depths, slice(0, 128))
    for ref in (up_ref, down_ref):
        ref[LON_ROWS:, 128:] = jnp.zeros((ref.shape[0] - LON_ROWS, 128), jnp.float32)
        ref[LON_ROWS - 2 : LON_ROWS] = jnp.zeros((2, ref.shape[1]), jnp.float32)
        ref[LON_ROWS:, :128] = strip_ref[...]
    for field, distance, beyond, at in lon_layout():
        for ref, x in ((up_ref, lon - distance), (down_ref, distance - 1)):
            if beyond:
                low = low_rows(field, x, lon)
                ref[at : at + beyond] = low[LAT_ROWS[field] - beyond :]
                high = high_rows(field, x, lon)
                ref[at + beyond + TILE : at + TILE + 2 * beyond] = high[:beyond]
            ref[at + beyond : at + beyond + TILE] = state_ref[field, x]


def dot3_first(left, right):
    dims = (((0,), (0,)), ((), ()))
    dot = functools.partial(lax.dot_general, dimension_numbers=dims, preferred_element_type=jnp.float32)
    left_high, left_low = left
    right_high, right_low = right
    return dot(left_high, right_high) + (dot(left_high, right_low) + dot(left_low, right_high))


def step_kernel(
    even_ref,
    state_ref,
    first_ref,
    second_ref,
    west_ref,
    east_ref,
    strip_ref,
    turning_ref,
    inside_ref,
    obs_cell_ref,
    obs_value_ref,
    obs_weight_ref,
    forecast_ref,
    packed_ref,
    field_ref,
    next_ref,
    last_ref,
    picked_ref,
    cell_ref,
    value_ref,
    weight_ref,
    sems,
):
    copies = fetch(
        (obs_cell_ref, obs_value_ref, obs_weight_ref), (cell_ref, value_ref, weight_ref), sems
    )
    lon = state_ref.shape[1]
    even = even_ref[0] == 1
    low_rows = functools.partial(lat_rows, even, first_ref, second_ref)
    high_rows = functools.partial(lat_rows, even, second_ref, first_ref)
    members = state_ref.shape[3]
    wide = TILE + 2 * REACH
    for field, count in enumerate(LAT_ROWS):
        for x in range(lon):
            field_ref[field, REACH + x, REACH : REACH + TILE] = state_ref[field, x]
            field_ref[field, REACH + x, REACH - count : REACH] = low_rows(field, x, lon)
            field_ref[field, REACH + x, REACH + TILE : REACH + TILE + count] = high_rows(
                field, x, lon
            )
    for field, distance, beyond, at in lon_layout():
        rows = slice(REACH - beyond, REACH + TILE + beyond)
        taken = slice(at, at + TILE + 2 * beyond)
        field_ref[field, REACH - distance, rows] = west_ref[taken]
        field_ref[field, REACH + lon - 1 + distance, rows] = east_ref[taken]
    turning = time_step * jnp.broadcast_to(turning_ref[:, :1], (wide, members))
    keeper = jnp.broadcast_to(inside_ref[:, :1], (wide, members))
    pull = 0.5 * time_step * gravity

    def column(x):
        if x < REACH:
            depth = west_ref[LON_ROWS:, lon - REACH + x : lon - REACH + x + 1]
        elif x < REACH + lon:
            depth = strip_ref[:, x - REACH : x - REACH + 1]
        else:
            depth = east_ref[LON_ROWS:, x - REACH - lon : x - REACH - lon + 1]
        return jnp.broadcast_to(0.5 * time_step * depth, (wide, members))

    def along(plane):
        return pltpu.roll(plane, wide - 1, 0) - pltpu.roll(plane, 1, 0)

    def advance_height(source, target, x):
        spread = source[1, x + 1] - source[1, x - 1] + along(source[2, x])
        target[0, x] = source[0, x] - column(x) * spread

    def advance_flow(source, heights, x):
        east = source[1, x]
        north = source[2, x]
        slope_east = heights[0, x + 1] - heights[0, x - 1]
        slope_north = along(heights[0, x])
        return (
            east + (turning * north - pull * slope_east),
            north - (turning * east + pull * slope_north),
        )

    for x in range(1, wide - 1):
        advance_height(field_ref, next_ref, x)
    for x in range(2, wide - 2):
        east, north = advance_flow(field_ref, next_ref, x)
        next_ref[1, x] = east
        next_ref[2, x] = north * keeper
    for x in range(3, wide - 3):
        advance_height(next_ref, last_ref, x)
    for x in range(REACH, REACH + lon):
        east, north = advance_flow(next_ref, last_ref, x)
        for field, plane in enumerate((last_ref[0, x], east, north)):
            at = (field * lon + x - REACH) * TILE
            forecast_ref[at : at + TILE] = plane[REACH : REACH + TILE]

    for copy in copies:
        copy.wait()
    count = picked_ref.shape[0]
    for k in range(count):
        picked_ref[k : k + 1] = forecast_ref[pl.ds(cell_ref[0, 0, k], 1)]
    picked = picked_ref[...]
    ymean = jnp.sum(picked, axis=1, keepdims=True) * (1.0 / members)
    half = members // 2
    row = lax.broadcasted_iota(jnp.int32, (half, half), 0)
    line = lax.broadcasted_iota(jnp.int32, (half, half), 1)
    on_diagonal = row == line
    weight = jnp.sum(jnp.where(on_diagonal, weight_ref[0], 0.0), axis=1, keepdims=True)
    value = jnp.sum(jnp.where(on_diagonal, value_ref[0], 0.0), axis=1, keepdims=True)
    anomaly = (picked - ymean) * weight
    innovation = (value - ymean) * weight
    projected = jnp.sum(innovation * anomaly, axis=0, keepdims=True)
    left_high, left_low = halves(anomaly[:, :half])
    right_high, right_low = halves(anomaly[:, half:])
    first = dot3_first((left_high, left_low), (left_high, left_low))
    cross = dot3_first((left_high, left_low), (right_high, right_low))
    final = dot3_first((right_high, right_low), (right_high, right_low))
    packed_ref[:half] = jnp.where(row <= line, first, final)
    packed_ref[half : 2 * half] = cross
    packed_ref[2 * half :] = jnp.zeros((packed_ref.shape[0] - 2 * half, half), jnp.float32)
    packed_ref[2 * half : 2 * half + 1] = jnp.sum(
        jnp.where(on_diagonal, final, 0.0), axis=0, keepdims=True
    )
    packed_ref[2 * half + 1 : 2 * half + 2] = projected[:, :half]
    packed_ref[2 * half + 2 : 2 * half + 3] = projected[:, half:]


def in_hbm(value):
    return pltpu.with_memory_space_constraint(value, pltpu.HBM)


def on_core(kernel, outs, spaces, scratch, out_space=pltpu.VMEM):
    return pl.pallas_call(
        kernel,
        out_shape=tuple(jax.ShapeDtypeStruct(shape, jnp.float32) for shape in outs),
        in_specs=[pl.BlockSpec(memory_space=space) for space in spaces],
        out_specs=tuple(pl.BlockSpec(memory_space=out_space) for _ in outs),
        scratch_shapes=scratch,
        compiler_params=pltpu.CompilerParams(vmem_limit_bytes=VMEM_BYTES),
    )


def halves(value):
    high = value.astype(jnp.bfloat16)
    return high, (value - high.astype(jnp.float32)).astype(jnp.bfloat16)


def dot3(left, right):
    left_high, left_low = left
    right_high, right_low = right
    dot = functools.partial(jnp.dot, preferred_element_type=jnp.float32)
    return dot(left_high, right_high) + (dot(left_high, right_low) + dot(left_low, right_high))


def finish_kernel(
    packed_ref, state_ref, analysis_ref, transform_ref, moved_ref, matrix_ref, sems
):
    half = packed_ref.shape[1]
    members = 2 * half
    square = packed_ref[:half]
    cross = packed_ref[half : 2 * half]
    diagonal = packed_ref[2 * half : 2 * half + 1]
    turned = square.T
    row = lax.broadcasted_iota(jnp.int32, (half, half), 0)
    column = lax.broadcasted_iota(jnp.int32, (half, half), 1)
    first = jnp.where(row <= column, square, turned)
    last = jnp.where(row == column, diagonal, jnp.where(row < column, turned, square))
    gram = jnp.concatenate(
        [jnp.concatenate([first, cross], axis=1), jnp.concatenate([cross.T, last], axis=1)]
    )
    row = lax.broadcasted_iota(jnp.int32, (members, members), 0)
    column = lax.broadcasted_iota(jnp.int32, (members, members), 1)
    on_diagonal = row == column
    system = gram + jnp.where(on_diagonal, members - 1.0, 0.0)
    scaler = jnp.sqrt(
        jnp.sum(jnp.sum(system * system, axis=0, keepdims=True), axis=1, keepdims=True)
    )
    root = system * (1.0 / scaler)
    level = jnp.where(on_diagonal, 2.25, 0.0)

    product = root
    for step in range(0, NS_ITERS, 2):
        split = halves(product)
        square = dot3(split, split)
        higher = dot3(halves(square), halves(0.0625 * square - 0.5625 * product))
        factor = halves(level - 2.4375 * product + 1.6875 * square + higher)
        if step == 0:
            inverse = factor
        elif step < NS_ITERS - 2:
            inverse = halves(dot3(factor, inverse))
        else:
            inverse = dot3(factor, inverse)
        if step < NS_ITERS - 2:
            product = dot3(factor, halves(dot3(factor, split)))
    projected = jnp.concatenate(
        [packed_ref[2 * half + 1 : 2 * half + 2], packed_ref[2 * half + 2 : 2 * half + 3]], axis=1
    )
    once = jnp.sum(inverse * projected, axis=1, keepdims=True)
    once = jnp.sum(jnp.where(on_diagonal, once, 0.0), axis=0, keepdims=True)
    offset = jnp.sum(inverse * once, axis=1, keepdims=True) / scaler
    transform = jnp.sqrt((members - 1.0) / scaler) * inverse + offset
    matrix_ref[...] = transform
    copies = fetch((matrix_ref,), (transform_ref,), sems)
    transform = halves(transform)
    block = 128
    for start in range(0, state_ref.shape[0], block):
        rows = pl.ds(start, block)
        state = state_ref[rows]
        average = jnp.sum(state, axis=1, keepdims=True) * (1.0 / members)
        moved_ref[rows] = average + dot3(halves(state - average), transform)
        sem = sems.at[pl.ds(1 + start // block, 1)]
        copies += fetch((moved_ref.at[rows],), (analysis_ref.at[rows],), sem)
    for copy in copies:
        copy.wait()


def finish(packed, state):
    members = state.shape[1]
    square = (members, members)
    return on_core(
        finish_kernel,
        (state.shape, square),
        [pltpu.VMEM] * 2,
        [
            pltpu.VMEM(state.shape, jnp.float32),
            pltpu.VMEM(square, jnp.float32),
            pltpu.SemaphoreType.DMA((1 + state.shape[0] // 128,)),
        ],
        pltpu.HBM,
    )(packed, state)


def reduced(packed):
    lon = lax.axis_size("lon")
    lat = lax.axis_size("lat")
    width = packed.size // lon
    pieces = lax.all_to_all(packed.reshape(lon, 1, width), "lon", 0, 0)
    piece = jnp.sum(pieces, axis=0)
    pieces = lax.all_to_all(jnp.broadcast_to(piece[None], (lat, 1, width)), "lat", 0, 0)
    piece = jnp.sum(pieces, axis=0)
    pieces = lax.all_to_all(jnp.broadcast_to(piece[None], (lon, 1, width)), "lon", 0, 0)
    return pieces.reshape(packed.shape)


def local(ensemble, bathymetry, obs_cell, obs_value, obs_weight):
    fields, lon, lat, members = ensemble.shape
    vmem = pltpu.VMEM
    total_lat = lat * lax.axis_size("lat")
    wide = lat + 2 * REACH
    rows = lax.axis_index("lat") * lat - REACH + lax.broadcasted_iota(jnp.int32, (wide, 128), 0)
    inside = ((rows >= 0) & (rows < total_lat)).astype(jnp.float32)
    turning = rotation * (2.0 * (rows.astype(jnp.float32) + 0.5) / total_lat - 1.0)
    lat_shape = (ROWS * lon + 8, members)
    lon_shape = (LON_ROWS + wide, members)
    even = (lax.axis_index("lon") % 2 == 0).astype(jnp.int32).reshape(1)
    first, second, depth = on_core(
        pack_lat_kernel,
        (lat_shape, lat_shape, (lat, 128)),
        [pltpu.SMEM] + [pltpu.HBM] * 2,
        [
            pltpu.VMEM(ensemble.shape, jnp.float32),
            pltpu.VMEM(bathymetry.shape, jnp.int32),
            pltpu.VMEM((128, 128), jnp.float32),
            pltpu.SemaphoreType.DMA((2,)),
        ],
    )(even, in_hbm(ensemble), in_hbm(bathymetry))
    pairs = [[], []]
    last = lax.axis_size("lat") - 1
    for a in range(lax.axis_size("lon")):
        for b in range(last):
            lower = a * (last + 1) + b
            pairs[a % 2].append((lower, lower + 1))
            pairs[1 - a % 2].append((lower + 1, lower))
    first = lax.ppermute(first, ("lon", "lat"), pairs[0])
    second = lax.ppermute(second, ("lon", "lat"), pairs[1])
    up, down, strip = on_core(
        pack_lon_kernel,
        (lon_shape, lon_shape, (wide, 128)),
        [pltpu.SMEM] + [vmem] * 4,
        [],
    )(even, ensemble, first, second, depth)
    west = shift_up(up, "lon", True)
    east = shift_down(down, "lon", True)
    planes = (fields, lon + 2 * REACH, wide, members)
    forecast, packed = on_core(
        step_kernel,
        ((fields * lon * lat, members), (members + 32, members // 2)),
        [pltpu.SMEM] + [vmem] * 8 + [pltpu.HBM] * 3,
        [pltpu.VMEM(planes, jnp.float32)] * 2
        + [pltpu.VMEM((1,) + planes[1:], jnp.float32)]
        + [pltpu.VMEM((obs_cell.shape[2], members), jnp.float32)]
        + [pltpu.SMEM(obs_cell.shape, jnp.int32)]
        + [pltpu.VMEM(obs_value.shape, jnp.float32)] * 2
        + [pltpu.SemaphoreType.DMA((3,))],
    )(
        even,
        ensemble,
        first,
        second,
        west,
        east,
        strip,
        turning,
        inside,
        in_hbm(obs_cell),
        in_hbm(obs_value),
        in_hbm(obs_weight),
    )
    analysis, transform = finish(reduced(packed), forecast)
    return (analysis.reshape(ensemble.shape), transform)


def solution(mesh):
    return jax.shard_map(
        local,
        mesh=mesh,
        in_specs=(
            P(None, "lon", "lat", None),
            P("lon", "lat"),
            P("lon", "lat", None),
            P("lon", "lat", None),
            P("lon", "lat", None),
        ),
        out_specs=(P(None, "lon", "lat", None), P()),
        check_vma=False,
    )
```

```python
import functools

import jax
import jax.numpy as jnp
from jax import lax
from jax.experimental import pallas as pl
from jax.experimental.pallas import tpu as pltpu
from jax.sharding import PartitionSpec as P

STEPS = 2
NS_ITERS = 6
LEVELS = 16
REACH = 2 * STEPS
VMEM_BYTES = 24 * 1024 * 1024
TILE = 16
LAT_ROWS = (3, 3, 4)
ROWS = sum(LAT_ROWS)
LON_ROWS = 192

time_step = 0.6
gravity = 1.0
rotation = 0.3


def fetch(sources, targets, sems):
    copies = [
        pltpu.make_async_copy(source, target, sems.at[k])
        for k, (source, target) in enumerate(zip(sources, targets))
    ]
    for copy in copies:
        copy.start()
    return copies


def pack_lat_kernel(
    parity_ref, ensemble_ref, bathymetry_ref, first_ref, second_ref, depth_ref, state_ref, bottom_ref, square_ref, sems
):
    lon, lat = state_ref.shape[1], state_ref.shape[2]
    copies = fetch((bathymetry_ref, ensemble_ref), (bottom_ref, state_ref), sems)
    square_ref[...] = jnp.zeros_like(square_ref)
    depth_at = ROWS * lon
    for ref in (first_ref, second_ref):
        ref[depth_at:] = jnp.zeros((ref.shape[0] - depth_at, ref.shape[1]), jnp.float32)
    copies[0].wait()
    square_ref[:lon, :lat] = (bottom_ref[...].astype(jnp.float32) + 1.0) * (1.0 / LEVELS)
    turned = square_ref[...].T[:lat]
    depth_ref[...] = turned
    copies[1].wait()

    def pack(up_ref, down_ref):
        up_ref[depth_at : depth_at + 3, :128] = turned[lat - 3 : lat]
        down_ref[depth_at : depth_at + 3, :128] = turned[:3]
        for field, count in enumerate(LAT_ROWS):
            for x in range(lon):
                at = lon * sum(LAT_ROWS[:field]) + x * count
                plane = state_ref[field, x]
                up_ref[at : at + count] = plane[lat - count :]
                down_ref[at : at + count] = plane[:count]

    @pl.when(parity_ref[0] & 1 == 0)
    def _():
        pack(first_ref, second_ref)

    @pl.when(parity_ref[0] & 1 == 1)
    def _():
        pack(second_ref, first_ref)


def chosen(even, first_ref, second_ref, rows, lanes=slice(None)):
    return jnp.where(even, first_ref[rows, lanes], second_ref[rows, lanes])


def lat_rows(even, first_ref, second_ref, field, x, lon):
    at = lon * sum(LAT_ROWS[:field]) + x * LAT_ROWS[field]
    return chosen(even, first_ref, second_ref, slice(at, at + LAT_ROWS[field]))


def lon_layout():
    at = 0
    for field, width, reach in ((0, 3, 3), (1, 4, 4), (2, 3, 4)):
        for distance in range(1, width + 1):
            beyond = reach - distance
            yield field, distance, beyond, at
            at += TILE + 2 * beyond


def pack_lon_kernel(
    parity_ref, state_ref, first_ref, second_ref, depth_ref, across_ref, within_ref, strip_ref
):
    lon = state_ref.shape[1]
    even = parity_ref[0] & 1 == 0
    low_rows = functools.partial(lat_rows, even, second_ref, first_ref)
    high_rows = functools.partial(lat_rows, even, first_ref, second_ref)
    depth_at = ROWS * lon
    strip_ref[...] = jnp.zeros_like(strip_ref)
    depths = slice(depth_at, depth_at + 3)
    strip_ref[1:4] = chosen(even, second_ref, first_ref, depths, slice(0, 128))
    strip_ref[4:20] = depth_ref[...]
    strip_ref[20:23] = chosen(even, first_ref, second_ref, depths, slice(0, 128))
    for ref in (across_ref, within_ref):
        ref[LON_ROWS:, 128:] = jnp.zeros((ref.shape[0] - LON_ROWS, 128), jnp.float32)
        ref[LON_ROWS - 2 : LON_ROWS] = jnp.zeros((2, ref.shape[1]), jnp.float32)
        ref[LON_ROWS:, :128] = strip_ref[...]

    def pack(up_ref, down_ref):
        for field, distance, beyond, at in lon_layout():
            for ref, x in ((up_ref, lon - distance), (down_ref, distance - 1)):
                if beyond:
                    low = low_rows(field, x, lon)
                    ref[at : at + beyond] = low[LAT_ROWS[field] - beyond :]
                    high = high_rows(field, x, lon)
                    ref[at + beyond + TILE : at + TILE + 2 * beyond] = high[:beyond]
                ref[at + beyond : at + beyond + TILE] = state_ref[field, x]

    @pl.when(parity_ref[0] < 2)
    def _():
        pack(within_ref, across_ref)

    @pl.when(parity_ref[0] >= 2)
    def _():
        pack(across_ref, within_ref)


def dot3_first(left, right):
    dims = (((0,), (0,)), ((), ()))
    dot = functools.partial(lax.dot_general, dimension_numbers=dims, preferred_element_type=jnp.float32)
    left_high, left_low = left
    right_high, right_low = right
    return dot(left_high, right_high) + (dot(left_high, right_low) + dot(left_low, right_high))


def step_kernel(
    parity_ref,
    state_ref,
    first_ref,
    second_ref,
    across_ref,
    within_ref,
    strip_ref,
    turning_ref,
    inside_ref,
    obs_cell_ref,
    obs_value_ref,
    obs_weight_ref,
    forecast_ref,
    packed_ref,
    field_ref,
    next_ref,
    last_ref,
    picked_ref,
    cell_ref,
    value_ref,
    weight_ref,
    sems,
):
    copies = fetch(
        (obs_cell_ref, obs_value_ref, obs_weight_ref), (cell_ref, value_ref, weight_ref), sems
    )
    lon = state_ref.shape[1]
    even = parity_ref[0] & 1 == 0
    even_lon = parity_ref[0] < 2
    west = functools.partial(chosen, even_lon, across_ref, within_ref)
    east = functools.partial(chosen, even_lon, within_ref, across_ref)
    low_rows = functools.partial(lat_rows, even, second_ref, first_ref)
    high_rows = functools.partial(lat_rows, even, first_ref, second_ref)
    members = state_ref.shape[3]
    wide = TILE + 2 * REACH
    for field, count in enumerate(LAT_ROWS):
        for x in range(lon):
            field_ref[field, REACH + x, REACH : REACH + TILE] = state_ref[field, x]
            field_ref[field, REACH + x, REACH - count : REACH] = low_rows(field, x, lon)
            field_ref[field, REACH + x, REACH + TILE : REACH + TILE + count] = high_rows(
                field, x, lon
            )
    for field, distance, beyond, at in lon_layout():
        rows = slice(REACH - beyond, REACH + TILE + beyond)
        taken = slice(at, at + TILE + 2 * beyond)
        field_ref[field, REACH - distance, rows] = west(taken)
        field_ref[field, REACH + lon - 1 + distance, rows] = east(taken)
    turning = time_step * jnp.broadcast_to(turning_ref[:, :1], (wide, members))
    keeper = jnp.broadcast_to(inside_ref[:, :1], (wide, members))
    pull = 0.5 * time_step * gravity

    west_depth = west(slice(LON_ROWS, None), slice(0, 128))
    east_depth = east(slice(LON_ROWS, None), slice(0, 128))
    middle_depth = strip_ref[...]

    def column(x):
        if x < REACH:
            depth = west_depth[:, lon - REACH + x : lon - REACH + x + 1]
        elif x < REACH + lon:
            depth = middle_depth[:, x - REACH : x - REACH + 1]
        else:
            depth = east_depth[:, x - REACH - lon : x - REACH - lon + 1]
        return jnp.broadcast_to(0.5 * time_step * depth, (wide, members))

    def along(plane):
        return pltpu.roll(plane, wide - 1, 0) - pltpu.roll(plane, 1, 0)

    def advance_height(source, target, x):
        spread = source[1, x + 1] - source[1, x - 1] + along(source[2, x])
        target[0, x] = source[0, x] - column(x) * spread

    def advance_flow(source, heights, x):
        east = source[1, x]
        north = source[2, x]
        slope_east = heights[0, x + 1] - heights[0, x - 1]
        slope_north = along(heights[0, x])
        return (
            east + (turning * north - pull * slope_east),
            north - (turning * east + pull * slope_north),
        )

    for x in range(1, wide - 1):
        advance_height(field_ref, next_ref, x)
    for x in range(2, wide - 2):
        east, north = advance_flow(field_ref, next_ref, x)
        next_ref[1, x] = east
        next_ref[2, x] = north * keeper
    for x in range(3, wide - 3):
        advance_height(next_ref, last_ref, x)
    for x in range(REACH, REACH + lon):
        east, north = advance_flow(next_ref, last_ref, x)
        for field, plane in enumerate((last_ref[0, x], east, north)):
            at = (field * lon + x - REACH) * TILE
            forecast_ref[at : at + TILE] = plane[REACH : REACH + TILE]

    for copy in copies:
        copy.wait()
    count = picked_ref.shape[0]
    for k in range(count):
        picked_ref[k : k + 1] = forecast_ref[pl.ds(cell_ref[0, 0, k], 1)]
    picked = picked_ref[...]
    ymean = jnp.sum(picked, axis=1, keepdims=True) * (1.0 / members)
    half = members // 2
    row = lax.broadcasted_iota(jnp.int32, (half, half), 0)
    line = lax.broadcasted_iota(jnp.int32, (half, half), 1)
    on_diagonal = row == line
    weight = jnp.sum(jnp.where(on_diagonal, weight_ref[0], 0.0), axis=1, keepdims=True)
    value = jnp.sum(jnp.where(on_diagonal, value_ref[0], 0.0), axis=1, keepdims=True)
    anomaly = (picked - ymean) * weight
    innovation = (value - ymean) * weight
    projected = jnp.sum(innovation * anomaly, axis=0, keepdims=True)
    left_high, left_low = halves(anomaly[:, :half])
    right_high, right_low = halves(anomaly[:, half:])
    first = dot3_first((left_high, left_low), (left_high, left_low))
    cross = dot3_first((left_high, left_low), (right_high, right_low))
    final = dot3_first((right_high, right_low), (right_high, right_low))
    packed_ref[:half] = jnp.where(row <= line, first, final)
    packed_ref[half : 2 * half] = cross
    packed_ref[2 * half :] = jnp.zeros((packed_ref.shape[0] - 2 * half, half), jnp.float32)
    packed_ref[2 * half : 2 * half + 1] = jnp.sum(
        jnp.where(on_diagonal, final, 0.0), axis=0, keepdims=True
    )
    packed_ref[2 * half + 1 : 2 * half + 2] = projected[:, :half]
    packed_ref[2 * half + 2 : 2 * half + 3] = projected[:, half:]


def in_hbm(value):
    return pltpu.with_memory_space_constraint(value, pltpu.HBM)


def on_core(kernel, outs, spaces, scratch, out_space=pltpu.VMEM):
    return pl.pallas_call(
        kernel,
        out_shape=tuple(jax.ShapeDtypeStruct(shape, jnp.float32) for shape in outs),
        in_specs=[pl.BlockSpec(memory_space=space) for space in spaces],
        out_specs=tuple(pl.BlockSpec(memory_space=out_space) for _ in outs),
        scratch_shapes=scratch,
        compiler_params=pltpu.CompilerParams(vmem_limit_bytes=VMEM_BYTES),
    )


def halves(value):
    high = value.astype(jnp.bfloat16)
    return high, (value - high.astype(jnp.float32)).astype(jnp.bfloat16)


def dot3(left, right):
    left_high, left_low = left
    right_high, right_low = right
    dot = functools.partial(jnp.dot, preferred_element_type=jnp.float32)
    return dot(left_high, right_high) + (dot(left_high, right_low) + dot(left_low, right_high))


def finish_kernel(
    packed_ref, state_ref, analysis_ref, transform_ref, moved_ref, matrix_ref, sems
):
    half = packed_ref.shape[1]
    members = 2 * half
    square = packed_ref[:half]
    cross = packed_ref[half : 2 * half]
    diagonal = packed_ref[2 * half : 2 * half + 1]
    turned = square.T
    row = lax.broadcasted_iota(jnp.int32, (half, half), 0)
    column = lax.broadcasted_iota(jnp.int32, (half, half), 1)
    first = jnp.where(row <= column, square, turned)
    last = jnp.where(row == column, diagonal, jnp.where(row < column, turned, square))
    gram = jnp.concatenate(
        [jnp.concatenate([first, cross], axis=1), jnp.concatenate([cross.T, last], axis=1)]
    )
    row = lax.broadcasted_iota(jnp.int32, (members, members), 0)
    column = lax.broadcasted_iota(jnp.int32, (members, members), 1)
    on_diagonal = row == column
    system = gram + jnp.where(on_diagonal, members - 1.0, 0.0)
    scaler = jnp.sqrt(
        jnp.sum(jnp.sum(system * system, axis=0, keepdims=True), axis=1, keepdims=True)
    )
    root = system * (1.0 / scaler)
    level = jnp.where(on_diagonal, 2.25, 0.0)

    product = root
    for step in range(0, NS_ITERS, 2):
        split = halves(product)
        square = dot3(split, split)
        higher = dot3(halves(square), halves(0.0625 * square - 0.5625 * product))
        factor = halves(level - 2.4375 * product + 1.6875 * square + higher)
        if step == 0:
            inverse = factor
        elif step < NS_ITERS - 2:
            inverse = halves(dot3(factor, inverse))
        else:
            inverse = dot3(factor, inverse)
        if step < NS_ITERS - 2:
            product = dot3(factor, halves(dot3(factor, split)))
    projected = jnp.concatenate(
        [packed_ref[2 * half + 1 : 2 * half + 2], packed_ref[2 * half + 2 : 2 * half + 3]], axis=1
    )
    once = jnp.sum(inverse * projected, axis=1, keepdims=True)
    once = jnp.sum(jnp.where(on_diagonal, once, 0.0), axis=0, keepdims=True)
    offset = jnp.sum(inverse * once, axis=1, keepdims=True) / scaler
    transform = jnp.sqrt((members - 1.0) / scaler) * inverse + offset
    matrix_ref[...] = transform
    copies = fetch((matrix_ref,), (transform_ref,), sems)
    transform = halves(transform)
    block = 128
    for start in range(0, state_ref.shape[0], block):
        rows = pl.ds(start, block)
        state = state_ref[rows]
        average = jnp.sum(state, axis=1, keepdims=True) * (1.0 / members)
        moved_ref[rows] = average + dot3(halves(state - average), transform)
        sem = sems.at[pl.ds(1 + start // block, 1)]
        copies += fetch((moved_ref.at[rows],), (analysis_ref.at[rows],), sem)
    for copy in copies:
        copy.wait()


def finish(packed, state):
    members = state.shape[1]
    square = (members, members)
    return on_core(
        finish_kernel,
        (state.shape, square),
        [pltpu.VMEM] * 2,
        [
            pltpu.VMEM(state.shape, jnp.float32),
            pltpu.VMEM(square, jnp.float32),
            pltpu.SemaphoreType.DMA((1 + state.shape[0] // 128,)),
        ],
        pltpu.HBM,
    )(packed, state)


def reduced(packed):
    lon = lax.axis_size("lon")
    lat = lax.axis_size("lat")
    width = packed.size // lon
    pieces = lax.all_to_all(packed.reshape(lon, 1, width), "lon", 0, 0)
    piece = jnp.sum(pieces, axis=0)
    pieces = lax.all_to_all(jnp.broadcast_to(piece[None], (lat, 1, width)), "lat", 0, 0)
    piece = jnp.sum(pieces, axis=0)
    pieces = lax.all_to_all(jnp.broadcast_to(piece[None], (lon, 1, width)), "lon", 0, 0)
    return pieces.reshape(packed.shape)


def local(ensemble, bathymetry, obs_cell, obs_value, obs_weight):
    fields, lon, lat, members = ensemble.shape
    vmem = pltpu.VMEM
    total_lat = lat * lax.axis_size("lat")
    wide = lat + 2 * REACH
    rows = lax.axis_index("lat") * lat - REACH + lax.broadcasted_iota(jnp.int32, (wide, 128), 0)
    inside = ((rows >= 0) & (rows < total_lat)).astype(jnp.float32)
    turning = rotation * (2.0 * (rows.astype(jnp.float32) + 0.5) / total_lat - 1.0)
    lat_shape = (ROWS * lon + 8, members)
    lon_shape = (LON_ROWS + wide, members)
    here = lax.axis_index("lon")
    parity = ((here + lax.axis_index("lat")) & 1) + 2 * (here & 1)
    parity = parity.reshape(1)
    first, second, depth = on_core(
        pack_lat_kernel,
        (lat_shape, lat_shape, (lat, 128)),
        [pltpu.SMEM] + [pltpu.HBM] * 2,
        [
            pltpu.VMEM(ensemble.shape, jnp.float32),
            pltpu.VMEM(bathymetry.shape, jnp.int32),
            pltpu.VMEM((128, 128), jnp.float32),
            pltpu.SemaphoreType.DMA((2,)),
        ],
    )(parity, in_hbm(ensemble), in_hbm(bathymetry))
    across, within = [], []
    columns = lax.axis_size("lon")
    rows_of = lax.axis_size("lat")
    pairs = ([], [])
    for a in range(columns):
        for b in range(rows_of):
            ours = a * rows_of + b
            if b + 1 < rows_of:
                pairs[(a + b) % 2].extend(((ours, ours + 1), (ours + 1, ours)))
        (across if a % 2 else within).extend(((a, (a + 1) % columns), ((a + 1) % columns, a)))
    first = lax.ppermute(first, ("lon", "lat"), pairs[0])
    second = lax.ppermute(second, ("lon", "lat"), pairs[1])
    out_across, out_within, strip = on_core(
        pack_lon_kernel,
        (lon_shape, lon_shape, (wide, 128)),
        [pltpu.SMEM] + [vmem] * 4,
        [],
    )(parity, ensemble, first, second, depth)
    across = lax.ppermute(out_across, "lon", across)
    within = lax.ppermute(out_within, "lon", within)
    planes = (fields, lon + 2 * REACH, wide, members)
    forecast, packed = on_core(
        step_kernel,
        ((fields * lon * lat, members), (members + 32, members // 2)),
        [pltpu.SMEM] + [vmem] * 8 + [pltpu.HBM] * 3,
        [pltpu.VMEM(planes, jnp.float32)] * 2
        + [pltpu.VMEM((1,) + planes[1:], jnp.float32)]
        + [pltpu.VMEM((obs_cell.shape[2], members), jnp.float32)]
        + [pltpu.SMEM(obs_cell.shape, jnp.int32)]
        + [pltpu.VMEM(obs_value.shape, jnp.float32)] * 2
        + [pltpu.SemaphoreType.DMA((3,))],
    )(
        parity,
        ensemble,
        first,
        second,
        across,
        within,
        strip,
        turning,
        inside,
        in_hbm(obs_cell),
        in_hbm(obs_value),
        in_hbm(obs_weight),
    )
    analysis, transform = finish(reduced(packed), forecast)
    return (analysis.reshape(ensemble.shape), transform)


def solution(mesh):
    return jax.shard_map(
        local,
        mesh=mesh,
        in_specs=(
            P(None, "lon", "lat", None),
            P("lon", "lat"),
            P("lon", "lat", None),
            P("lon", "lat", None),
            P("lon", "lat", None),
        ),
        out_specs=(P(None, "lon", "lat", None), P()),
        check_vma=False,
    )
```

```python
import functools

import jax
import jax.numpy as jnp
from jax import lax
from jax.experimental import pallas as pl
from jax.experimental.pallas import tpu as pltpu
from jax.sharding import PartitionSpec as P

STEPS = 2
NS_ITERS = 6
LEVELS = 16
REACH = 2 * STEPS
VMEM_BYTES = 24 * 1024 * 1024
TILE = 16
LAT_ROWS = (3, 3, 4)
ROWS = sum(LAT_ROWS)
LON_ROWS = 192

time_step = 0.6
gravity = 1.0
rotation = 0.3


def fetch(sources, targets, sems):
    copies = [
        pltpu.make_async_copy(source, target, sems.at[k])
        for k, (source, target) in enumerate(zip(sources, targets))
    ]
    for copy in copies:
        copy.start()
    return copies


def pack_lat_kernel(
    parity_ref, ensemble_ref, bathymetry_ref, first_ref, second_ref, depth_ref, state_ref, bottom_ref, square_ref, sems
):
    lon, lat = state_ref.shape[1], state_ref.shape[2]
    copies = fetch((bathymetry_ref, ensemble_ref), (bottom_ref, state_ref), sems)
    square_ref[...] = jnp.zeros_like(square_ref)
    depth_at = ROWS * lon
    for ref in (first_ref, second_ref):
        ref[depth_at:] = jnp.zeros((ref.shape[0] - depth_at, ref.shape[1]), jnp.float32)
    copies[0].wait()
    square_ref[:lon, :lat] = (bottom_ref[...].astype(jnp.float32) + 1.0) * (1.0 / LEVELS)
    turned = square_ref[...].T[:lat]
    depth_ref[...] = turned
    copies[1].wait()

    def pack(up_ref, down_ref):
        up_ref[depth_at : depth_at + 3, :128] = turned[lat - 3 : lat]
        down_ref[depth_at : depth_at + 3, :128] = turned[:3]
        for field, count in enumerate(LAT_ROWS):
            for x in range(lon):
                at = lon * sum(LAT_ROWS[:field]) + x * count
                plane = state_ref[field, x]
                up_ref[at : at + count] = plane[lat - count :]
                down_ref[at : at + count] = plane[:count]

    @pl.when(parity_ref[0] & 1 == 0)
    def _():
        pack(first_ref, second_ref)

    @pl.when(parity_ref[0] & 1 == 1)
    def _():
        pack(second_ref, first_ref)


def chosen(even, first_ref, second_ref, rows, lanes=slice(None)):
    return jnp.where(even, first_ref[rows, lanes], second_ref[rows, lanes])


def lat_rows(even, first_ref, second_ref, field, x, lon):
    at = lon * sum(LAT_ROWS[:field]) + x * LAT_ROWS[field]
    return chosen(even, first_ref, second_ref, slice(at, at + LAT_ROWS[field]))


def lon_layout():
    at = 0
    for field, width, reach in ((0, 3, 3), (1, 4, 4), (2, 3, 4)):
        for distance in range(1, width + 1):
            beyond = reach - distance
            yield field, distance, beyond, at
            at += TILE + 2 * beyond


def pack_lon_kernel(
    parity_ref, state_ref, first_ref, second_ref, depth_ref, across_ref, within_ref, strip_ref
):
    lon = state_ref.shape[1]
    even = parity_ref[0] & 1 == 0
    low_rows = functools.partial(lat_rows, even, second_ref, first_ref)
    high_rows = functools.partial(lat_rows, even, first_ref, second_ref)
    depth_at = ROWS * lon
    strip_ref[...] = jnp.zeros_like(strip_ref)
    depths = slice(depth_at, depth_at + 3)
    strip_ref[1:4] = chosen(even, second_ref, first_ref, depths, slice(0, 128))
    strip_ref[4:20] = depth_ref[...]
    strip_ref[20:23] = chosen(even, first_ref, second_ref, depths, slice(0, 128))
    for ref in (across_ref, within_ref):
        ref[LON_ROWS:, 128:] = jnp.zeros((ref.shape[0] - LON_ROWS, 128), jnp.float32)
        ref[LON_ROWS - 2 : LON_ROWS] = jnp.zeros((2, ref.shape[1]), jnp.float32)
        ref[LON_ROWS:, :128] = strip_ref[...]

    def pack(up_ref, down_ref):
        for field, distance, beyond, at in lon_layout():
            for ref, x in ((up_ref, lon - distance), (down_ref, distance - 1)):
                if beyond:
                    low = low_rows(field, x, lon)
                    ref[at : at + beyond] = low[LAT_ROWS[field] - beyond :]
                    high = high_rows(field, x, lon)
                    ref[at + beyond + TILE : at + TILE + 2 * beyond] = high[:beyond]
                ref[at + beyond : at + beyond + TILE] = state_ref[field, x]

    @pl.when(parity_ref[0] < 2)
    def _():
        pack(within_ref, across_ref)

    @pl.when(parity_ref[0] >= 2)
    def _():
        pack(across_ref, within_ref)


def dot3_first(left, right):
    dims = (((0,), (0,)), ((), ()))
    left_high, left_low = left
    right_high, right_low = right
    return lax.dot_general(
        jnp.concatenate([left_high, left_high, left_low]),
        jnp.concatenate([right_high, right_low, right_high]),
        dims,
        preferred_element_type=jnp.float32,
    )


def along(plane):
    return pltpu.roll(plane, plane.shape[0] - 1, 0) - pltpu.roll(plane, 1, 0)


def advance_height(source, depth, x):
    spread = source(1, x + 1) - source(1, x - 1) + along(source(2, x))
    return source(0, x) - depth(x) * spread


def advance_flow(source, height, turning, x):
    pull = 0.5 * time_step * gravity
    east = source(1, x)
    north = source(2, x)
    slope_east = height(x + 1) - height(x - 1)
    slope_north = along(height(x))
    return (
        east + (turning * north - pull * slope_east),
        north - (turning * east + pull * slope_north),
    )


def spread_out(column, shape):
    return jnp.broadcast_to(column, shape)


HANDED = ((4, 5, 18, 19),) * 3 + ((5, 6, 17, 18),) + ((6, 7, 16, 17),) * 2 + ((7, 8, 15, 16),)


def inner_kernel(
    parity_ref,
    state_ref,
    first_ref,
    second_ref,
    strip_ref,
    turning_ref,
    inside_ref,
    inner_ref,
    handed_ref,
    field_ref,
    next_ref,
    last_ref,
):
    lon = state_ref.shape[1]
    shape = field_ref.shape[2:]
    even = parity_ref[0] & 1 == 0
    low_rows = functools.partial(lat_rows, even, second_ref, first_ref)
    high_rows = functools.partial(lat_rows, even, first_ref, second_ref)
    for field, count in enumerate(LAT_ROWS):
        for x in range(lon):
            field_ref[field, x, REACH : REACH + TILE] = state_ref[field, x]
            field_ref[field, x, REACH - count : REACH] = low_rows(field, x, lon)
            field_ref[field, x, REACH + TILE : REACH + TILE + count] = high_rows(field, x, lon)
    turning = time_step * spread_out(turning_ref[:, :1], shape)
    keeper = spread_out(inside_ref[:, :1], shape)
    strip = 0.5 * time_step * strip_ref[...]
    end = lon + 2 * REACH

    def depth(x):
        return spread_out(strip[:, x - REACH : x - REACH + 1], shape)

    def source(field, x):
        return field_ref[field, x - REACH]

    def after(field, x):
        return next_ref[field, x - REACH]

    def height(x):
        return next_ref[0, x - REACH]

    def last_height(x):
        return last_ref[0, x - REACH]

    for x in range(REACH + 1, end - REACH - 1):
        next_ref[0, x - REACH] = advance_height(source, depth, x)
    for x in range(REACH + 2, end - REACH - 2):
        east, north = advance_flow(source, height, turning, x)
        next_ref[1, x - REACH] = east
        next_ref[2, x - REACH] = north * keeper
    for x in range(REACH + 3, end - REACH - 3):
        last_ref[0, x - REACH] = advance_height(after, depth, x)
    for x in range(2 * REACH, end - 2 * REACH):
        east, north = advance_flow(after, last_height, turning, x)
        for field, plane in enumerate((last_height(x), east, north)):
            inner_ref[field, x - 2 * REACH] = plane[REACH : REACH + TILE]
    kinds = (
        functools.partial(source, 0),
        functools.partial(source, 1),
        functools.partial(source, 2),
        height,
        functools.partial(after, 1),
        functools.partial(after, 2),
        last_height,
    )
    for kind, (columns, plane) in enumerate(zip(HANDED, kinds)):
        for k, x in enumerate(columns):
            handed_ref[kind, k] = plane(x)


def step_kernel(
    parity_ref,
    across_ref,
    within_ref,
    strip_ref,
    turning_ref,
    inside_ref,
    inner_ref,
    handed_ref,
    obs_cell_ref,
    obs_value_ref,
    obs_weight_ref,
    forecast_ref,
    packed_ref,
    field_ref,
    next_ref,
    last_ref,
    picked_ref,
    cell_ref,
    value_ref,
    weight_ref,
    sems,
):
    copies = fetch(
        (obs_cell_ref, obs_value_ref, obs_weight_ref), (cell_ref, value_ref, weight_ref), sems
    )
    shape = field_ref.shape[2:]
    members = shape[1]
    end = next_ref.shape[1]
    lon = end - 2 * REACH
    even_lon = parity_ref[0] < 2
    west = functools.partial(chosen, even_lon, across_ref, within_ref)
    east = functools.partial(chosen, even_lon, within_ref, across_ref)
    for field, distance, beyond, at in lon_layout():
        rows = slice(REACH - beyond, REACH + TILE + beyond)
        taken = slice(at, at + TILE + 2 * beyond)
        field_ref[field, REACH - distance, rows] = west(taken)
        field_ref[field, REACH - 1 + distance, rows] = east(taken)
    turning = time_step * spread_out(turning_ref[:, :1], shape)
    keeper = spread_out(inside_ref[:, :1], shape)
    strips = [
        0.5 * time_step * strip
        for strip in (
            west(slice(LON_ROWS, None), slice(0, 128)),
            strip_ref[...],
            east(slice(LON_ROWS, None), slice(0, 128)),
        )
    ]

    def depth(x):
        if x < REACH:
            column = strips[0][:, lon - REACH + x : lon - REACH + x + 1]
        elif x < REACH + lon:
            column = strips[1][:, x - REACH : x - REACH + 1]
        else:
            column = strips[2][:, x - REACH - lon : x - REACH - lon + 1]
        return spread_out(column, shape)

    def source(field, x):
        if x < REACH:
            return field_ref[field, x]
        if x >= REACH + lon:
            return field_ref[field, x - lon]
        return handed_ref[field, HANDED[field].index(x)]

    def after(field, x):
        if x in HANDED[3 + field]:
            return handed_ref[3 + field, HANDED[3 + field].index(x)]
        return next_ref[field, x]

    def height(x):
        return after(0, x)

    def last_height(x):
        if x in HANDED[6]:
            return handed_ref[6, HANDED[6].index(x)]
        return last_ref[0, x]

    def edges(margin):
        return (*range(margin, margin + REACH), *range(end - margin - REACH, end - margin))

    for x in edges(1):
        next_ref[0, x] = advance_height(source, depth, x)
    for x in edges(2):
        east_flow, north_flow = advance_flow(source, height, turning, x)
        next_ref[1, x] = east_flow
        next_ref[2, x] = north_flow * keeper
    for x in edges(3):
        last_ref[0, x] = advance_height(after, depth, x)
    for x in edges(REACH):
        east_flow, north_flow = advance_flow(after, last_height, turning, x)
        for field, plane in enumerate((last_height(x), east_flow, north_flow)):
            at = (field * lon + x - REACH) * TILE
            forecast_ref[at : at + TILE] = plane[REACH : REACH + TILE]
    for field in range(len(LAT_ROWS)):
        for x in range(REACH, lon - REACH):
            at = (field * lon + x) * TILE
            forecast_ref[at : at + TILE] = inner_ref[field, x - REACH]

    for copy in copies:
        copy.wait()
    count = picked_ref.shape[0]
    for k in range(count):
        picked_ref[k : k + 1] = forecast_ref[pl.ds(cell_ref[0, 0, k], 1)]
    picked = picked_ref[...]
    ymean = jnp.sum(picked, axis=1, keepdims=True) * (1.0 / members)
    half = members // 2
    row = lax.broadcasted_iota(jnp.int32, (half, half), 0)
    line = lax.broadcasted_iota(jnp.int32, (half, half), 1)
    on_diagonal = row == line
    weight = jnp.sum(jnp.where(on_diagonal, weight_ref[0], 0.0), axis=1, keepdims=True)
    value = jnp.sum(jnp.where(on_diagonal, value_ref[0], 0.0), axis=1, keepdims=True)
    anomaly = (picked - ymean) * weight
    innovation = (value - ymean) * weight
    projected = jnp.sum(innovation * anomaly, axis=0, keepdims=True)
    left_high, left_low = halves(anomaly[:, :half])
    right_high, right_low = halves(anomaly[:, half:])
    first = dot3_first((left_high, left_low), (left_high, left_low))
    cross = dot3_first((left_high, left_low), (right_high, right_low))
    final = dot3_first((right_high, right_low), (right_high, right_low))
    packed_ref[:half] = jnp.where(row <= line, first, final)
    packed_ref[half : 2 * half] = cross
    packed_ref[2 * half :] = jnp.zeros((packed_ref.shape[0] - 2 * half, half), jnp.float32)
    packed_ref[2 * half : 2 * half + 1] = jnp.sum(
        jnp.where(on_diagonal, final, 0.0), axis=0, keepdims=True
    )
    packed_ref[2 * half + 1 : 2 * half + 2] = projected[:, :half]
    packed_ref[2 * half + 2 : 2 * half + 3] = projected[:, half:]


def in_hbm(value):
    return pltpu.with_memory_space_constraint(value, pltpu.HBM)


def on_core(kernel, outs, spaces, scratch, out_space=pltpu.VMEM):
    return pl.pallas_call(
        kernel,
        out_shape=tuple(jax.ShapeDtypeStruct(shape, jnp.float32) for shape in outs),
        in_specs=[pl.BlockSpec(memory_space=space) for space in spaces],
        out_specs=tuple(pl.BlockSpec(memory_space=out_space) for _ in outs),
        scratch_shapes=scratch,
        compiler_params=pltpu.CompilerParams(vmem_limit_bytes=VMEM_BYTES),
    )


def halves(value):
    high = value.astype(jnp.bfloat16)
    return high, (value - high.astype(jnp.float32)).astype(jnp.bfloat16)


def dot3(left, right):
    left_high, left_low = left
    right_high, right_low = right
    return jnp.dot(
        jnp.concatenate([left_high, left_high, left_low], axis=1),
        jnp.concatenate([right_high, right_low, right_high], axis=0),
        preferred_element_type=jnp.float32,
    )


def finish_kernel(
    packed_ref, state_ref, analysis_ref, transform_ref, moved_ref, matrix_ref, sems
):
    half = packed_ref.shape[1]
    members = 2 * half
    square = packed_ref[:half]
    cross = packed_ref[half : 2 * half]
    diagonal = packed_ref[2 * half : 2 * half + 1]
    turned = square.T
    row = lax.broadcasted_iota(jnp.int32, (half, half), 0)
    column = lax.broadcasted_iota(jnp.int32, (half, half), 1)
    first = jnp.where(row <= column, square, turned)
    last = jnp.where(row == column, diagonal, jnp.where(row < column, turned, square))
    gram = jnp.concatenate(
        [jnp.concatenate([first, cross], axis=1), jnp.concatenate([cross.T, last], axis=1)]
    )
    row = lax.broadcasted_iota(jnp.int32, (members, members), 0)
    column = lax.broadcasted_iota(jnp.int32, (members, members), 1)
    on_diagonal = row == column
    system = gram + jnp.where(on_diagonal, members - 1.0, 0.0)
    scaler = jnp.sqrt(
        jnp.sum(jnp.sum(system * system, axis=0, keepdims=True), axis=1, keepdims=True)
    )
    root = system * (1.0 / scaler)
    level = jnp.where(on_diagonal, 2.25, 0.0)

    product = root
    for step in range(0, NS_ITERS, 2):
        split = halves(product)
        square = dot3(split, split)
        higher = dot3(halves(square), halves(0.0625 * square - 0.5625 * product))
        factor = halves(level - 2.4375 * product + 1.6875 * square + higher)
        if step == 0:
            inverse = factor
        elif step < NS_ITERS - 2:
            inverse = halves(dot3(factor, inverse))
        else:
            inverse = dot3(factor, inverse)
        if step < NS_ITERS - 2:
            product = dot3(factor, halves(dot3(factor, split)))
    projected = jnp.concatenate(
        [packed_ref[2 * half + 1 : 2 * half + 2], packed_ref[2 * half + 2 : 2 * half + 3]], axis=1
    )
    once = jnp.sum(inverse * projected, axis=1, keepdims=True)
    once = jnp.sum(jnp.where(on_diagonal, once, 0.0), axis=0, keepdims=True)
    offset = jnp.sum(inverse * once, axis=1, keepdims=True) / scaler
    transform = jnp.sqrt((members - 1.0) / scaler) * inverse + offset
    matrix_ref[...] = transform
    copies = fetch((matrix_ref,), (transform_ref,), sems)
    transform = halves(transform)
    block = 128
    for start in range(0, state_ref.shape[0], block):
        rows = pl.ds(start, block)
        state = state_ref[rows]
        average = jnp.sum(state, axis=1, keepdims=True) * (1.0 / members)
        moved_ref[rows] = average + dot3(halves(state - average), transform)
        sem = sems.at[pl.ds(1 + start // block, 1)]
        copies += fetch((moved_ref.at[rows],), (analysis_ref.at[rows],), sem)
    for copy in copies:
        copy.wait()


def finish(packed, state):
    members = state.shape[1]
    square = (members, members)
    return on_core(
        finish_kernel,
        (state.shape, square),
        [pltpu.VMEM] * 2,
        [
            pltpu.VMEM(state.shape, jnp.float32),
            pltpu.VMEM(square, jnp.float32),
            pltpu.SemaphoreType.DMA((1 + state.shape[0] // 128,)),
        ],
        pltpu.HBM,
    )(packed, state)


def reduced(packed):
    lon = lax.axis_size("lon")
    lat = lax.axis_size("lat")
    width = packed.size // lon
    pieces = lax.all_to_all(packed.reshape(lon, 1, width), "lon", 0, 0)
    piece = jnp.sum(pieces, axis=0)
    pieces = lax.all_to_all(jnp.broadcast_to(piece[None], (lat, 1, width)), "lat", 0, 0)
    piece = jnp.sum(pieces, axis=0)
    pieces = lax.all_to_all(jnp.broadcast_to(piece[None], (lon, 1, width)), "lon", 0, 0)
    return pieces.reshape(packed.shape)


def local(ensemble, bathymetry, obs_cell, obs_value, obs_weight):
    fields, lon, lat, members = ensemble.shape
    vmem = pltpu.VMEM
    total_lat = lat * lax.axis_size("lat")
    wide = lat + 2 * REACH
    rows = lax.axis_index("lat") * lat - REACH + lax.broadcasted_iota(jnp.int32, (wide, 128), 0)
    inside = ((rows >= 0) & (rows < total_lat)).astype(jnp.float32)
    turning = rotation * (2.0 * (rows.astype(jnp.float32) + 0.5) / total_lat - 1.0)
    lat_shape = (ROWS * lon + 8, members)
    lon_shape = (LON_ROWS + wide, members)
    here = lax.axis_index("lon")
    parity = ((here + lax.axis_index("lat")) & 1) + 2 * (here & 1)
    parity = parity.reshape(1)
    first, second, depth = on_core(
        pack_lat_kernel,
        (lat_shape, lat_shape, (lat, 128)),
        [pltpu.SMEM] + [pltpu.HBM] * 2,
        [
            pltpu.VMEM(ensemble.shape, jnp.float32),
            pltpu.VMEM(bathymetry.shape, jnp.int32),
            pltpu.VMEM((128, 128), jnp.float32),
            pltpu.SemaphoreType.DMA((2,)),
        ],
    )(parity, in_hbm(ensemble), in_hbm(bathymetry))
    across, within = [], []
    columns = lax.axis_size("lon")
    rows_of = lax.axis_size("lat")
    pairs = ([], [])
    for a in range(columns):
        for b in range(rows_of):
            ours = a * rows_of + b
            if b + 1 < rows_of:
                pairs[(a + b) % 2].extend(((ours, ours + 1), (ours + 1, ours)))
        (across if a % 2 else within).extend(((a, (a + 1) % columns), ((a + 1) % columns, a)))
    first = lax.ppermute(first, ("lon", "lat"), pairs[0])
    second = lax.ppermute(second, ("lon", "lat"), pairs[1])
    out_across, out_within, strip = on_core(
        pack_lon_kernel,
        (lon_shape, lon_shape, (wide, 128)),
        [pltpu.SMEM] + [vmem] * 4,
        [],
    )(parity, ensemble, first, second, depth)
    planes = (fields, lon, wide, members)
    across = lax.ppermute(out_across, "lon", across)
    within = lax.ppermute(out_within, "lon", within)
    inner, handed = on_core(
        inner_kernel,
        ((fields, lon - 2 * REACH, lat, members), (len(HANDED), REACH) + planes[2:]),
        [pltpu.SMEM] + [vmem] * 6,
        [pltpu.VMEM(planes, jnp.float32)] * 2
        + [pltpu.VMEM((1,) + planes[1:], jnp.float32)],
    )(parity, ensemble, first, second, strip, turning, inside)
    planes = (fields, wide, wide, members)
    forecast, packed = on_core(
        step_kernel,
        ((fields * lon * lat, members), (members + 32, members // 2)),
        [pltpu.SMEM] + [vmem] * 7 + [pltpu.HBM] * 3,
        [
            pltpu.VMEM((fields, 2 * REACH) + planes[2:], jnp.float32),
            pltpu.VMEM(planes, jnp.float32),
            pltpu.VMEM((1,) + planes[1:], jnp.float32),
            pltpu.VMEM((obs_cell.shape[2], members), jnp.float32),
            pltpu.SMEM(obs_cell.shape, jnp.int32),
        ]
        + [pltpu.VMEM(obs_value.shape, jnp.float32)] * 2
        + [pltpu.SemaphoreType.DMA((3,))],
    )(
        parity,
        across,
        within,
        strip,
        turning,
        inside,
        inner,
        handed,
        in_hbm(obs_cell),
        in_hbm(obs_value),
        in_hbm(obs_weight),
    )
    analysis, transform = finish(reduced(packed), forecast)
    return (analysis.reshape(ensemble.shape), transform)


def solution(mesh):
    return jax.shard_map(
        local,
        mesh=mesh,
        in_specs=(
            P(None, "lon", "lat", None),
            P("lon", "lat"),
            P("lon", "lat", None),
            P("lon", "lat", None),
            P("lon", "lat", None),
        ),
        out_specs=(P(None, "lon", "lat", None), P()),
        check_vma=False,
    )
```

```python
import functools

import jax
import jax.numpy as jnp
from jax import lax
from jax.experimental import pallas as pl
from jax.experimental.pallas import tpu as pltpu
from jax.sharding import PartitionSpec as P

STEPS = 2
NS_ITERS = 6
LEVELS = 16
REACH = 2 * STEPS
VMEM_BYTES = 24 * 1024 * 1024
TILE = 16
LAT_ROWS = (3, 3, 4)
ROWS = sum(LAT_ROWS)
LON_ROWS = 192

time_step = 0.6
gravity = 1.0
rotation = 0.3


def fetch(sources, targets, sems):
    copies = [
        pltpu.make_async_copy(source, target, sems.at[k])
        for k, (source, target) in enumerate(zip(sources, targets))
    ]
    for copy in copies:
        copy.start()
    return copies


def pack_lat_kernel(
    parity_ref, ensemble_ref, bathymetry_ref, first_ref, second_ref, depth_ref, state_ref, bottom_ref, square_ref, sems
):
    lon, lat = state_ref.shape[1], state_ref.shape[2]
    copies = fetch((bathymetry_ref, ensemble_ref), (bottom_ref, state_ref), sems)
    square_ref[...] = jnp.zeros_like(square_ref)
    depth_at = ROWS * lon
    for ref in (first_ref, second_ref):
        ref[depth_at:] = jnp.zeros((ref.shape[0] - depth_at, ref.shape[1]), jnp.float32)
    copies[0].wait()
    square_ref[:lon, :lat] = (bottom_ref[...].astype(jnp.float32) + 1.0) * (1.0 / LEVELS)
    turned = square_ref[...].T[:lat]
    depth_ref[...] = turned
    copies[1].wait()

    def pack(up_ref, down_ref):
        up_ref[depth_at : depth_at + 3, :128] = turned[lat - 3 : lat]
        down_ref[depth_at : depth_at + 3, :128] = turned[:3]
        for field, count in enumerate(LAT_ROWS):
            for x in range(lon):
                at = lon * sum(LAT_ROWS[:field]) + x * count
                plane = state_ref[field, x]
                up_ref[at : at + count] = plane[lat - count :]
                down_ref[at : at + count] = plane[:count]

    @pl.when(parity_ref[0] == 0)
    def _():
        pack(first_ref, second_ref)

    @pl.when(parity_ref[0] == 1)
    def _():
        pack(second_ref, first_ref)


def chosen(even, first_ref, second_ref, rows, lanes=slice(None)):
    return jnp.where(even, first_ref[rows, lanes], second_ref[rows, lanes])


def lat_rows(even, first_ref, second_ref, field, x, lon):
    at = lon * sum(LAT_ROWS[:field]) + x * LAT_ROWS[field]
    return chosen(even, first_ref, second_ref, slice(at, at + LAT_ROWS[field]))


def lon_layout():
    at = 0
    for field, width, reach in ((0, 3, 3), (1, 4, 4), (2, 3, 4)):
        for distance in range(1, width + 1):
            beyond = reach - distance
            yield field, distance, beyond, at
            at += TILE + 2 * beyond


def pack_lon_kernel(
    parity_ref, state_ref, first_ref, second_ref, depth_ref, across_ref, within_ref, strip_ref
):
    lon = state_ref.shape[1]
    even = parity_ref[0] == 0
    low_rows = functools.partial(lat_rows, even, first_ref, second_ref)
    high_rows = functools.partial(lat_rows, even, second_ref, first_ref)
    depth_at = ROWS * lon
    strip_ref[...] = jnp.zeros_like(strip_ref)
    depths = slice(depth_at, depth_at + 3)
    strip_ref[1:4] = chosen(even, first_ref, second_ref, depths, slice(0, 128))
    strip_ref[4:20] = depth_ref[...]
    strip_ref[20:23] = chosen(even, second_ref, first_ref, depths, slice(0, 128))
    for ref in (across_ref, within_ref):
        ref[LON_ROWS:, 128:] = jnp.zeros((ref.shape[0] - LON_ROWS, 128), jnp.float32)
        ref[LON_ROWS - 2 : LON_ROWS] = jnp.zeros((2, ref.shape[1]), jnp.float32)
        ref[LON_ROWS:, :128] = strip_ref[...]

    def pack(up_ref, down_ref):
        for field, distance, beyond, at in lon_layout():
            for ref, x in ((up_ref, lon - distance), (down_ref, distance - 1)):
                if beyond:
                    low = low_rows(field, x, lon)
                    ref[at : at + beyond] = low[LAT_ROWS[field] - beyond :]
                    high = high_rows(field, x, lon)
                    ref[at + beyond + TILE : at + TILE + 2 * beyond] = high[:beyond]
                ref[at + beyond : at + beyond + TILE] = state_ref[field, x]

    @pl.when(parity_ref[0] == 0)
    def _():
        pack(within_ref, across_ref)

    @pl.when(parity_ref[0] == 1)
    def _():
        pack(across_ref, within_ref)


def dot3_first(left, right):
    dims = (((0,), (0,)), ((), ()))
    left_high, left_low = left
    right_high, right_low = right
    return lax.dot_general(
        jnp.concatenate([left_high, left_high, left_low]),
        jnp.concatenate([right_high, right_low, right_high]),
        dims,
        preferred_element_type=jnp.float32,
    )


def along(plane):
    return pltpu.roll(plane, plane.shape[0] - 1, 0) - pltpu.roll(plane, 1, 0)


def advance_height(source, depth, x):
    spread = source(1, x + 1) - source(1, x - 1) + along(source(2, x))
    return source(0, x) - depth(x) * spread


def advance_flow(source, height, turning, x):
    pull = 0.5 * time_step * gravity
    east = source(1, x)
    north = source(2, x)
    slope_east = height(x + 1) - height(x - 1)
    slope_north = along(height(x))
    return (
        east + (turning * north - pull * slope_east),
        north - (turning * east + pull * slope_north),
    )


def spread_out(column, shape):
    return jnp.broadcast_to(column, shape)


HANDED = ((4, 5, 18, 19),) * 3 + ((5, 6, 17, 18),) + ((6, 7, 16, 17),) * 2 + ((7, 8, 15, 16),)


def inner_kernel(
    parity_ref,
    state_ref,
    first_ref,
    second_ref,
    strip_ref,
    turning_ref,
    inside_ref,
    inner_ref,
    handed_ref,
    field_ref,
    next_ref,
    last_ref,
):
    lon = state_ref.shape[1]
    shape = field_ref.shape[2:]
    even = parity_ref[0] == 0
    low_rows = functools.partial(lat_rows, even, first_ref, second_ref)
    high_rows = functools.partial(lat_rows, even, second_ref, first_ref)
    for field, count in enumerate(LAT_ROWS):
        for x in range(lon):
            field_ref[field, x, REACH : REACH + TILE] = state_ref[field, x]
            field_ref[field, x, REACH - count : REACH] = low_rows(field, x, lon)
            field_ref[field, x, REACH + TILE : REACH + TILE + count] = high_rows(field, x, lon)
    turning = time_step * spread_out(turning_ref[:, :1], shape)
    keeper = spread_out(inside_ref[:, :1], shape)
    strip = 0.5 * time_step * strip_ref[...]
    end = lon + 2 * REACH

    def depth(x):
        return spread_out(strip[:, x - REACH : x - REACH + 1], shape)

    def source(field, x):
        return field_ref[field, x - REACH]

    def after(field, x):
        return next_ref[field, x - REACH]

    def height(x):
        return next_ref[0, x - REACH]

    def last_height(x):
        return last_ref[0, x - REACH]

    for x in range(REACH + 1, end - REACH - 1):
        next_ref[0, x - REACH] = advance_height(source, depth, x)
    for x in range(REACH + 2, end - REACH - 2):
        east, north = advance_flow(source, height, turning, x)
        next_ref[1, x - REACH] = east
        next_ref[2, x - REACH] = north * keeper
    for x in range(REACH + 3, end - REACH - 3):
        last_ref[0, x - REACH] = advance_height(after, depth, x)
    for x in range(2 * REACH, end - 2 * REACH):
        east, north = advance_flow(after, last_height, turning, x)
        for field, plane in enumerate((last_height(x), east, north)):
            inner_ref[field, x - 2 * REACH] = plane[REACH : REACH + TILE]
    kinds = (
        functools.partial(source, 0),
        functools.partial(source, 1),
        functools.partial(source, 2),
        height,
        functools.partial(after, 1),
        functools.partial(after, 2),
        last_height,
    )
    for kind, (columns, plane) in enumerate(zip(HANDED, kinds)):
        for k, x in enumerate(columns):
            handed_ref[kind, k] = plane(x)


def step_kernel(
    parity_ref,
    across_ref,
    within_ref,
    strip_ref,
    turning_ref,
    inside_ref,
    inner_ref,
    handed_ref,
    obs_cell_ref,
    obs_value_ref,
    obs_weight_ref,
    forecast_ref,
    packed_ref,
    field_ref,
    next_ref,
    last_ref,
    picked_ref,
    cell_ref,
    value_ref,
    weight_ref,
    sems,
):
    copies = fetch(
        (obs_cell_ref, obs_value_ref, obs_weight_ref), (cell_ref, value_ref, weight_ref), sems
    )
    shape = field_ref.shape[2:]
    members = shape[1]
    end = next_ref.shape[1]
    lon = end - 2 * REACH
    even_lon = parity_ref[0] == 0
    west = functools.partial(chosen, even_lon, across_ref, within_ref)
    east = functools.partial(chosen, even_lon, within_ref, across_ref)
    for field, distance, beyond, at in lon_layout():
        rows = slice(REACH - beyond, REACH + TILE + beyond)
        taken = slice(at, at + TILE + 2 * beyond)
        field_ref[field, REACH - distance, rows] = west(taken)
        field_ref[field, REACH - 1 + distance, rows] = east(taken)
    turning = time_step * spread_out(turning_ref[:, :1], shape)
    keeper = spread_out(inside_ref[:, :1], shape)
    strips = [
        0.5 * time_step * strip
        for strip in (
            west(slice(LON_ROWS, None), slice(0, 128)),
            strip_ref[...],
            east(slice(LON_ROWS, None), slice(0, 128)),
        )
    ]

    def depth(x):
        if x < REACH:
            column = strips[0][:, lon - REACH + x : lon - REACH + x + 1]
        elif x < REACH + lon:
            column = strips[1][:, x - REACH : x - REACH + 1]
        else:
            column = strips[2][:, x - REACH - lon : x - REACH - lon + 1]
        return spread_out(column, shape)

    def source(field, x):
        if x < REACH:
            return field_ref[field, x]
        if x >= REACH + lon:
            return field_ref[field, x - lon]
        return handed_ref[field, HANDED[field].index(x)]

    def after(field, x):
        if x in HANDED[3 + field]:
            return handed_ref[3 + field, HANDED[3 + field].index(x)]
        return next_ref[field, x]

    def height(x):
        return after(0, x)

    def last_height(x):
        if x in HANDED[6]:
            return handed_ref[6, HANDED[6].index(x)]
        return last_ref[0, x]

    def edges(margin):
        return (*range(margin, margin + REACH), *range(end - margin - REACH, end - margin))

    for x in edges(1):
        next_ref[0, x] = advance_height(source, depth, x)
    for x in edges(2):
        east_flow, north_flow = advance_flow(source, height, turning, x)
        next_ref[1, x] = east_flow
        next_ref[2, x] = north_flow * keeper
    for x in edges(3):
        last_ref[0, x] = advance_height(after, depth, x)
    for x in edges(REACH):
        east_flow, north_flow = advance_flow(after, last_height, turning, x)
        for field, plane in enumerate((last_height(x), east_flow, north_flow)):
            at = (field * lon + x - REACH) * TILE
            forecast_ref[at : at + TILE] = plane[REACH : REACH + TILE]
    for field in range(len(LAT_ROWS)):
        for x in range(REACH, lon - REACH):
            at = (field * lon + x) * TILE
            forecast_ref[at : at + TILE] = inner_ref[field, x - REACH]

    for copy in copies:
        copy.wait()
    count = picked_ref.shape[0]
    for k in range(count):
        picked_ref[k : k + 1] = forecast_ref[pl.ds(cell_ref[0, 0, k], 1)]
    picked = picked_ref[...]
    ymean = jnp.sum(picked, axis=1, keepdims=True) * (1.0 / members)
    half = members // 2
    row = lax.broadcasted_iota(jnp.int32, (half, half), 0)
    line = lax.broadcasted_iota(jnp.int32, (half, half), 1)
    on_diagonal = row == line
    weight = jnp.sum(jnp.where(on_diagonal, weight_ref[0], 0.0), axis=1, keepdims=True)
    value = jnp.sum(jnp.where(on_diagonal, value_ref[0], 0.0), axis=1, keepdims=True)
    anomaly = (picked - ymean) * weight
    innovation = (value - ymean) * weight
    projected = jnp.sum(innovation * anomaly, axis=0, keepdims=True)
    left_high, left_low = halves(anomaly[:, :half])
    right_high, right_low = halves(anomaly[:, half:])
    first = dot3_first((left_high, left_low), (left_high, left_low))
    cross = dot3_first((left_high, left_low), (right_high, right_low))
    final = dot3_first((right_high, right_low), (right_high, right_low))
    packed_ref[:half] = jnp.where(row <= line, first, final)
    packed_ref[half : 2 * half] = cross
    packed_ref[2 * half :] = jnp.zeros((packed_ref.shape[0] - 2 * half, half), jnp.float32)
    packed_ref[2 * half : 2 * half + 1] = jnp.sum(
        jnp.where(on_diagonal, final, 0.0), axis=0, keepdims=True
    )
    packed_ref[2 * half + 1 : 2 * half + 2] = projected[:, :half]
    packed_ref[2 * half + 2 : 2 * half + 3] = projected[:, half:]


def in_hbm(value):
    return pltpu.with_memory_space_constraint(value, pltpu.HBM)


def on_core(kernel, outs, spaces, scratch, out_space=pltpu.VMEM):
    return pl.pallas_call(
        kernel,
        out_shape=tuple(jax.ShapeDtypeStruct(shape, jnp.float32) for shape in outs),
        in_specs=[pl.BlockSpec(memory_space=space) for space in spaces],
        out_specs=tuple(pl.BlockSpec(memory_space=out_space) for _ in outs),
        scratch_shapes=scratch,
        compiler_params=pltpu.CompilerParams(vmem_limit_bytes=VMEM_BYTES),
    )


def halves(value):
    high = value.astype(jnp.bfloat16)
    return high, (value - high.astype(jnp.float32)).astype(jnp.bfloat16)


def dot3(left, right):
    left_high, left_low = left
    right_high, right_low = right
    return jnp.dot(
        jnp.concatenate([left_high, left_high, left_low], axis=1),
        jnp.concatenate([right_high, right_low, right_high], axis=0),
        preferred_element_type=jnp.float32,
    )


def finish_kernel(
    packed_ref, state_ref, analysis_ref, transform_ref, moved_ref, matrix_ref, sems
):
    half = packed_ref.shape[1]
    members = 2 * half
    square = packed_ref[:half]
    cross = packed_ref[half : 2 * half]
    diagonal = packed_ref[2 * half : 2 * half + 1]
    turned = square.T
    row = lax.broadcasted_iota(jnp.int32, (half, half), 0)
    column = lax.broadcasted_iota(jnp.int32, (half, half), 1)
    first = jnp.where(row <= column, square, turned)
    last = jnp.where(row == column, diagonal, jnp.where(row < column, turned, square))
    gram = jnp.concatenate(
        [jnp.concatenate([first, cross], axis=1), jnp.concatenate([cross.T, last], axis=1)]
    )
    row = lax.broadcasted_iota(jnp.int32, (members, members), 0)
    column = lax.broadcasted_iota(jnp.int32, (members, members), 1)
    on_diagonal = row == column
    system = gram + jnp.where(on_diagonal, members - 1.0, 0.0)
    scaler = jnp.sqrt(
        jnp.sum(jnp.sum(system * system, axis=0, keepdims=True), axis=1, keepdims=True)
    )
    root = system * (1.0 / scaler)
    level = jnp.where(on_diagonal, 2.25, 0.0)

    product = root
    for step in range(0, NS_ITERS, 2):
        split = halves(product)
        square = dot3(split, split)
        higher = dot3(halves(square), halves(0.0625 * square - 0.5625 * product))
        factor = halves(level - 2.4375 * product + 1.6875 * square + higher)
        if step == 0:
            inverse = factor
        elif step < NS_ITERS - 2:
            inverse = halves(dot3(factor, inverse))
        else:
            inverse = dot3(factor, inverse)
        if step < NS_ITERS - 2:
            product = dot3(factor, halves(dot3(factor, split)))
    projected = jnp.concatenate(
        [packed_ref[2 * half + 1 : 2 * half + 2], packed_ref[2 * half + 2 : 2 * half + 3]], axis=1
    )
    once = jnp.sum(inverse * projected, axis=1, keepdims=True)
    once = jnp.sum(jnp.where(on_diagonal, once, 0.0), axis=0, keepdims=True)
    offset = jnp.sum(inverse * once, axis=1, keepdims=True) / scaler
    transform = jnp.sqrt((members - 1.0) / scaler) * inverse + offset
    matrix_ref[...] = transform
    copies = fetch((matrix_ref,), (transform_ref,), sems)
    transform = halves(transform)
    block = 128
    for start in range(0, state_ref.shape[0], block):
        rows = pl.ds(start, block)
        state = state_ref[rows]
        average = jnp.sum(state, axis=1, keepdims=True) * (1.0 / members)
        moved_ref[rows] = average + dot3(halves(state - average), transform)
        sem = sems.at[pl.ds(1 + start // block, 1)]
        copies += fetch((moved_ref.at[rows],), (analysis_ref.at[rows],), sem)
    for copy in copies:
        copy.wait()


def finish(packed, state):
    members = state.shape[1]
    square = (members, members)
    return on_core(
        finish_kernel,
        (state.shape, square),
        [pltpu.VMEM] * 2,
        [
            pltpu.VMEM(state.shape, jnp.float32),
            pltpu.VMEM(square, jnp.float32),
            pltpu.SemaphoreType.DMA((1 + state.shape[0] // 128,)),
        ],
        pltpu.HBM,
    )(packed, state)


def reduced(packed):
    lon = lax.axis_size("lon")
    lat = lax.axis_size("lat")
    width = packed.size // lon
    pieces = lax.all_to_all(packed.reshape(lon, 1, width), "lon", 0, 0)
    piece = jnp.sum(pieces, axis=0)
    pieces = lax.all_to_all(jnp.broadcast_to(piece[None], (lat, 1, width)), "lat", 0, 0)
    piece = jnp.sum(pieces, axis=0)
    pieces = lax.all_to_all(jnp.broadcast_to(piece[None], (lon, 1, width)), "lon", 0, 0)
    return pieces.reshape(packed.shape)


def local(ensemble, bathymetry, obs_cell, obs_value, obs_weight):
    fields, lon, lat, members = ensemble.shape
    vmem = pltpu.VMEM
    total_lat = lat * lax.axis_size("lat")
    wide = lat + 2 * REACH
    rows = lax.axis_index("lat") * lat - REACH + lax.broadcasted_iota(jnp.int32, (wide, 128), 0)
    inside = ((rows >= 0) & (rows < total_lat)).astype(jnp.float32)
    turning = rotation * (2.0 * (rows.astype(jnp.float32) + 0.5) / total_lat - 1.0)
    lat_shape = (ROWS * lon + 8, members)
    lon_shape = (LON_ROWS + wide, members)
    here = lax.axis_index("lon")
    parity = (here & 1).reshape(1)
    first, second, depth = on_core(
        pack_lat_kernel,
        (lat_shape, lat_shape, (lat, 128)),
        [pltpu.SMEM] + [pltpu.HBM] * 2,
        [
            pltpu.VMEM(ensemble.shape, jnp.float32),
            pltpu.VMEM(bathymetry.shape, jnp.int32),
            pltpu.VMEM((128, 128), jnp.float32),
            pltpu.SemaphoreType.DMA((2,)),
        ],
    )(parity, in_hbm(ensemble), in_hbm(bathymetry))
    across, within = [], []
    columns = lax.axis_size("lon")
    rows_of = lax.axis_size("lat")
    pairs = ([], [])
    for a in range(columns):
        for b in range(rows_of):
            ours = a * rows_of + b
            if b + 1 < rows_of:
                pairs[a % 2].append((ours, ours + 1))
                pairs[1 - a % 2].append((ours + 1, ours))
        (across if a % 2 else within).extend(((a, (a + 1) % columns), ((a + 1) % columns, a)))
    first = lax.ppermute(first, ("lon", "lat"), pairs[0])
    second = lax.ppermute(second, ("lon", "lat"), pairs[1])
    out_across, out_within, strip = on_core(
        pack_lon_kernel,
        (lon_shape, lon_shape, (wide, 128)),
        [pltpu.SMEM] + [vmem] * 4,
        [],
    )(parity, ensemble, first, second, depth)
    planes = (fields, lon, wide, members)
    across = lax.ppermute(out_across, "lon", across)
    within = lax.ppermute(out_within, "lon", within)
    inner, handed = on_core(
        inner_kernel,
        ((fields, lon - 2 * REACH, lat, members), (len(HANDED), REACH) + planes[2:]),
        [pltpu.SMEM] + [vmem] * 6,
        [pltpu.VMEM(planes, jnp.float32)] * 2
        + [pltpu.VMEM((1,) + planes[1:], jnp.float32)],
    )(parity, ensemble, first, second, strip, turning, inside)
    planes = (fields, wide, wide, members)
    forecast, packed = on_core(
        step_kernel,
        ((fields * lon * lat, members), (members + 32, members // 2)),
        [pltpu.SMEM] + [vmem] * 7 + [pltpu.HBM] * 3,
        [
            pltpu.VMEM((fields, 2 * REACH) + planes[2:], jnp.float32),
            pltpu.VMEM(planes, jnp.float32),
            pltpu.VMEM((1,) + planes[1:], jnp.float32),
            pltpu.VMEM((obs_cell.shape[2], members), jnp.float32),
            pltpu.SMEM(obs_cell.shape, jnp.int32),
        ]
        + [pltpu.VMEM(obs_value.shape, jnp.float32)] * 2
        + [pltpu.SemaphoreType.DMA((3,))],
    )(
        parity,
        across,
        within,
        strip,
        turning,
        inside,
        inner,
        handed,
        in_hbm(obs_cell),
        in_hbm(obs_value),
        in_hbm(obs_weight),
    )
    analysis, transform = finish(reduced(packed), forecast)
    return (analysis.reshape(ensemble.shape), transform)


def solution(mesh):
    return jax.shard_map(
        local,
        mesh=mesh,
        in_specs=(
            P(None, "lon", "lat", None),
            P("lon", "lat"),
            P("lon", "lat", None),
            P("lon", "lat", None),
            P("lon", "lat", None),
        ),
        out_specs=(P(None, "lon", "lat", None), P()),
        check_vma=False,
    )
```

```python
import functools

import jax
import jax.numpy as jnp
from jax import lax
from jax.experimental import pallas as pl
from jax.experimental.pallas import tpu as pltpu
from jax.sharding import PartitionSpec as P

STEPS = 2
NS_ITERS = 6
LEVELS = 16
REACH = 2 * STEPS
VMEM_BYTES = 24 * 1024 * 1024
TILE = 16
LAT_ROWS = (3, 3, 4)
ROWS = sum(LAT_ROWS)
MAIN_ROWS = 160
LON_ROWS = 192

time_step = 0.6
gravity = 1.0
rotation = 0.3


def fetch(sources, targets, sems):
    copies = [
        pltpu.make_async_copy(source, target, sems.at[k])
        for k, (source, target) in enumerate(zip(sources, targets))
    ]
    for copy in copies:
        copy.start()
    return copies


def pack_lat_kernel(
    parity_ref, ensemble_ref, bathymetry_ref, first_ref, second_ref, ahead_ref, depth_ref, state_ref, bottom_ref, square_ref, sems
):
    lon, lat = state_ref.shape[1], state_ref.shape[2]
    copies = fetch((bathymetry_ref, ensemble_ref), (bottom_ref, state_ref), sems)
    square_ref[...] = jnp.zeros_like(square_ref)
    depth_at = ROWS * lon
    for ref in (first_ref, second_ref):
        ref[depth_at:] = jnp.zeros((ref.shape[0] - depth_at, ref.shape[1]), jnp.float32)
    copies[0].wait()
    square_ref[:lon, :lat] = (bottom_ref[...].astype(jnp.float32) + 1.0) * (1.0 / LEVELS)
    turned = square_ref[...].T[:lat]
    depth_ref[...] = turned
    copies[1].wait()

    def pack(up_ref, down_ref):
        up_ref[depth_at : depth_at + 3, :128] = turned[lat - 3 : lat]
        down_ref[depth_at : depth_at + 3, :128] = turned[:3]
        for field, count in enumerate(LAT_ROWS):
            for x in range(lon):
                at = lon * sum(LAT_ROWS[:field]) + x * count
                plane = state_ref[field, x]
                up_ref[at : at + count] = plane[lat - count :]
                down_ref[at : at + count] = plane[:count]

    @pl.when(parity_ref[0] & 1 == 0)
    def _():
        pack(first_ref, second_ref)

    @pl.when(parity_ref[0] & 1 == 1)
    def _():
        pack(second_ref, first_ref)

    even_lon = parity_ref[0] < 2
    for field, distance, _, main, _ in lon_layout():
        down, up = state_ref[field, distance - 1], state_ref[field, lon - distance]
        ahead_ref[main : main + TILE] = jnp.where(even_lon, down, up)


def chosen(even, first_ref, second_ref, rows, lanes=slice(None)):
    return jnp.where(even, first_ref[rows, lanes], second_ref[rows, lanes])


def lat_rows(even, first_ref, second_ref, field, x, lon):
    at = lon * sum(LAT_ROWS[:field]) + x * LAT_ROWS[field]
    return chosen(even, first_ref, second_ref, slice(at, at + LAT_ROWS[field]))


def lon_layout():
    main, corner = 0, MAIN_ROWS
    for field, width, reach in ((0, 3, 3), (1, 4, 4), (2, 3, 4)):
        for distance in range(1, width + 1):
            beyond = reach - distance
            yield field, distance, beyond, main, corner
            main += TILE
            corner += 2 * beyond


def pack_lon_kernel(
    parity_ref, state_ref, first_ref, second_ref, depth_ref, across_ref, within_ref, strip_ref
):
    lon = state_ref.shape[1]
    even = parity_ref[0] & 1 == 0
    low_rows = functools.partial(lat_rows, even, second_ref, first_ref)
    high_rows = functools.partial(lat_rows, even, first_ref, second_ref)
    depth_at = ROWS * lon
    strip_ref[...] = jnp.zeros_like(strip_ref)
    depths = slice(depth_at, depth_at + 3)
    strip_ref[1:4] = chosen(even, second_ref, first_ref, depths, slice(0, 128))
    strip_ref[4:20] = depth_ref[...]
    strip_ref[20:23] = chosen(even, first_ref, second_ref, depths, slice(0, 128))
    for ref, skipped in ((across_ref, MAIN_ROWS), (within_ref, 0)):
        depths = slice(LON_ROWS - skipped, None)
        ref[depths, 128:] = jnp.zeros((strip_ref.shape[0], 128), jnp.float32)
        ref[LON_ROWS - 2 - skipped : LON_ROWS - skipped] = jnp.zeros((2, ref.shape[1]), jnp.float32)
        ref[depths, :128] = strip_ref[...]

    def pack(upward):
        for field, distance, beyond, main, corner in lon_layout():
            up, down = lon - distance, distance - 1
            for ref, x, skipped in (
                (across_ref, up if upward else down, MAIN_ROWS),
                (within_ref, down if upward else up, 0),
            ):
                if beyond:
                    at = corner - skipped
                    low = low_rows(field, x, lon)
                    ref[at : at + beyond] = low[LAT_ROWS[field] - beyond :]
                    high = high_rows(field, x, lon)
                    ref[at + beyond : at + 2 * beyond] = high[:beyond]
                if not skipped:
                    ref[main : main + TILE] = state_ref[field, x]

    @pl.when(parity_ref[0] < 2)
    def _():
        pack(False)

    @pl.when(parity_ref[0] >= 2)
    def _():
        pack(True)


def dot3_first(left, right):
    dims = (((0,), (0,)), ((), ()))
    left_high, left_low = left
    right_high, right_low = right
    return lax.dot_general(
        jnp.concatenate([left_high, left_high, left_low]),
        jnp.concatenate([right_high, right_low, right_high]),
        dims,
        preferred_element_type=jnp.float32,
    )


def along(plane):
    return pltpu.roll(plane, plane.shape[0] - 1, 0) - pltpu.roll(plane, 1, 0)


def advance_height(source, depth, x):
    spread = source(1, x + 1) - source(1, x - 1) + along(source(2, x))
    return source(0, x) - depth(x) * spread


def advance_flow(source, height, turning, x):
    pull = 0.5 * time_step * gravity
    east = source(1, x)
    north = source(2, x)
    slope_east = height(x + 1) - height(x - 1)
    slope_north = along(height(x))
    return (
        east + (turning * north - pull * slope_east),
        north - (turning * east + pull * slope_north),
    )


def spread_out(column, shape):
    return jnp.broadcast_to(column, shape)


HANDED = ((4, 5, 18, 19),) * 3 + ((5, 6, 17, 18),) + ((6, 7, 16, 17),) * 2 + ((7, 8, 15, 16),)


def inner_kernel(
    parity_ref,
    state_ref,
    first_ref,
    second_ref,
    strip_ref,
    turning_ref,
    inside_ref,
    inner_ref,
    handed_ref,
    field_ref,
    next_ref,
    last_ref,
):
    lon = state_ref.shape[1]
    shape = field_ref.shape[2:]
    even = parity_ref[0] & 1 == 0
    low_rows = functools.partial(lat_rows, even, second_ref, first_ref)
    high_rows = functools.partial(lat_rows, even, first_ref, second_ref)
    for field, count in enumerate(LAT_ROWS):
        for x in range(lon):
            field_ref[field, x, REACH : REACH + TILE] = state_ref[field, x]
            field_ref[field, x, REACH - count : REACH] = low_rows(field, x, lon)
            field_ref[field, x, REACH + TILE : REACH + TILE + count] = high_rows(field, x, lon)
    turning = time_step * spread_out(turning_ref[:, :1], shape)
    keeper = spread_out(inside_ref[:, :1], shape)
    strip = 0.5 * time_step * strip_ref[...]
    end = lon + 2 * REACH

    def depth(x):
        return spread_out(strip[:, x - REACH : x - REACH + 1], shape)

    def source(field, x):
        return field_ref[field, x - REACH]

    def after(field, x):
        return next_ref[field, x - REACH]

    def height(x):
        return next_ref[0, x - REACH]

    def last_height(x):
        return last_ref[0, x - REACH]

    for x in range(REACH + 1, end - REACH - 1):
        next_ref[0, x - REACH] = advance_height(source, depth, x)
    for x in range(REACH + 2, end - REACH - 2):
        east, north = advance_flow(source, height, turning, x)
        next_ref[1, x - REACH] = east
        next_ref[2, x - REACH] = north * keeper
    for x in range(REACH + 3, end - REACH - 3):
        last_ref[0, x - REACH] = advance_height(after, depth, x)
    for x in range(2 * REACH, end - 2 * REACH):
        east, north = advance_flow(after, last_height, turning, x)
        for field, plane in enumerate((last_height(x), east, north)):
            inner_ref[field, x - 2 * REACH] = plane[REACH : REACH + TILE]
    kinds = (
        functools.partial(source, 0),
        functools.partial(source, 1),
        functools.partial(source, 2),
        height,
        functools.partial(after, 1),
        functools.partial(after, 2),
        last_height,
    )
    for kind, (columns, plane) in enumerate(zip(HANDED, kinds)):
        for k, x in enumerate(columns):
            handed_ref[kind, k] = plane(x)


def step_kernel(
    parity_ref,
    ahead_ref,
    across_ref,
    within_ref,
    strip_ref,
    turning_ref,
    inside_ref,
    inner_ref,
    handed_ref,
    obs_cell_ref,
    obs_value_ref,
    obs_weight_ref,
    forecast_ref,
    packed_ref,
    field_ref,
    next_ref,
    last_ref,
    picked_ref,
    cell_ref,
    value_ref,
    weight_ref,
    sems,
):
    copies = fetch(
        (obs_cell_ref, obs_value_ref, obs_weight_ref), (cell_ref, value_ref, weight_ref), sems
    )
    shape = field_ref.shape[2:]
    members = shape[1]
    end = next_ref.shape[1]
    lon = end - 2 * REACH
    even_lon = parity_ref[0] < 2

    def taken(rows, lanes=slice(None)):
        start, stop = rows
        if stop <= MAIN_ROWS:
            across = ahead_ref[start:stop, lanes]
        else:
            across = across_ref[start - MAIN_ROWS : stop - MAIN_ROWS, lanes]
        within = within_ref[start:stop, lanes]
        return jnp.where(even_lon, across, within), jnp.where(even_lon, within, across)

    for field, distance, beyond, main, corner in lon_layout():
        parts = [((main, main + TILE), REACH, TILE)]
        if beyond:
            parts.append(((corner, corner + beyond), REACH - beyond, beyond))
            parts.append(((corner + beyond, corner + 2 * beyond), REACH + TILE, beyond))
        for rows, at, count in parts:
            west, east = taken(rows)
            field_ref[field, REACH - distance, at : at + count] = west
            field_ref[field, REACH - 1 + distance, at : at + count] = east
    west_strip, east_strip = taken((LON_ROWS, within_ref.shape[0]), slice(0, 128))
    turning = time_step * spread_out(turning_ref[:, :1], shape)
    keeper = spread_out(inside_ref[:, :1], shape)
    strips = [0.5 * time_step * strip for strip in (west_strip, strip_ref[...], east_strip)]

    def depth(x):
        if x < REACH:
            column = strips[0][:, lon - REACH + x : lon - REACH + x + 1]
        elif x < REACH + lon:
            column = strips[1][:, x - REACH : x - REACH + 1]
        else:
            column = strips[2][:, x - REACH - lon : x - REACH - lon + 1]
        return spread_out(column, shape)

    def source(field, x):
        if x < REACH:
            return field_ref[field, x]
        if x >= REACH + lon:
            return field_ref[field, x - lon]
        return handed_ref[field, HANDED[field].index(x)]

    def after(field, x):
        if x in HANDED[3 + field]:
            return handed_ref[3 + field, HANDED[3 + field].index(x)]
        return next_ref[field, x]

    def height(x):
        return after(0, x)

    def last_height(x):
        if x in HANDED[6]:
            return handed_ref[6, HANDED[6].index(x)]
        return last_ref[0, x]

    def edges(margin):
        return (*range(margin, margin + REACH), *range(end - margin - REACH, end - margin))

    for x in edges(1):
        next_ref[0, x] = advance_height(source, depth, x)
    for x in edges(2):
        east_flow, north_flow = advance_flow(source, height, turning, x)
        next_ref[1, x] = east_flow
        next_ref[2, x] = north_flow * keeper
    for x in edges(3):
        last_ref[0, x] = advance_height(after, depth, x)
    for x in edges(REACH):
        east_flow, north_flow = advance_flow(after, last_height, turning, x)
        for field, plane in enumerate((last_height(x), east_flow, north_flow)):
            at = (field * lon + x - REACH) * TILE
            forecast_ref[at : at + TILE] = plane[REACH : REACH + TILE]
    for field in range(len(LAT_ROWS)):
        for x in range(REACH, lon - REACH):
            at = (field * lon + x) * TILE
            forecast_ref[at : at + TILE] = inner_ref[field, x - REACH]

    for copy in copies:
        copy.wait()
    count = picked_ref.shape[0]
    for k in range(count):
        picked_ref[k : k + 1] = forecast_ref[pl.ds(cell_ref[0, 0, k], 1)]
    picked = picked_ref[...]
    ymean = jnp.sum(picked, axis=1, keepdims=True) * (1.0 / members)
    half = members // 2
    row = lax.broadcasted_iota(jnp.int32, (half, half), 0)
    line = lax.broadcasted_iota(jnp.int32, (half, half), 1)
    on_diagonal = row == line
    weight = jnp.sum(jnp.where(on_diagonal, weight_ref[0], 0.0), axis=1, keepdims=True)
    value = jnp.sum(jnp.where(on_diagonal, value_ref[0], 0.0), axis=1, keepdims=True)
    anomaly = (picked - ymean) * weight
    innovation = (value - ymean) * weight
    projected = jnp.sum(innovation * anomaly, axis=0, keepdims=True)
    left_high, left_low = halves(anomaly[:, :half])
    right_high, right_low = halves(anomaly[:, half:])
    first = dot3_first((left_high, left_low), (left_high, left_low))
    cross = dot3_first((left_high, left_low), (right_high, right_low))
    final = dot3_first((right_high, right_low), (right_high, right_low))
    packed_ref[:half] = jnp.where(row <= line, first, final)
    packed_ref[half : 2 * half] = cross
    packed_ref[2 * half :] = jnp.zeros((packed_ref.shape[0] - 2 * half, half), jnp.float32)
    packed_ref[2 * half : 2 * half + 1] = jnp.sum(
        jnp.where(on_diagonal, final, 0.0), axis=0, keepdims=True
    )
    packed_ref[2 * half + 1 : 2 * half + 2] = projected[:, :half]
    packed_ref[2 * half + 2 : 2 * half + 3] = projected[:, half:]


def in_hbm(value):
    return pltpu.with_memory_space_constraint(value, pltpu.HBM)


def on_core(kernel, outs, spaces, scratch, out_space=pltpu.VMEM):
    return pl.pallas_call(
        kernel,
        out_shape=tuple(jax.ShapeDtypeStruct(shape, jnp.float32) for shape in outs),
        in_specs=[pl.BlockSpec(memory_space=space) for space in spaces],
        out_specs=tuple(pl.BlockSpec(memory_space=out_space) for _ in outs),
        scratch_shapes=scratch,
        compiler_params=pltpu.CompilerParams(vmem_limit_bytes=VMEM_BYTES),
    )


def halves(value):
    high = value.astype(jnp.bfloat16)
    return high, (value - high.astype(jnp.float32)).astype(jnp.bfloat16)


def dot3(left, right):
    left_high, left_low = left
    right_high, right_low = right
    return jnp.dot(
        jnp.concatenate([left_high, left_high, left_low], axis=1),
        jnp.concatenate([right_high, right_low, right_high], axis=0),
        preferred_element_type=jnp.float32,
    )


def finish_kernel(
    packed_ref, state_ref, analysis_ref, transform_ref, moved_ref, matrix_ref, sems
):
    half = packed_ref.shape[1]
    members = 2 * half
    square = packed_ref[:half]
    cross = packed_ref[half : 2 * half]
    diagonal = packed_ref[2 * half : 2 * half + 1]
    turned = square.T
    row = lax.broadcasted_iota(jnp.int32, (half, half), 0)
    column = lax.broadcasted_iota(jnp.int32, (half, half), 1)
    first = jnp.where(row <= column, square, turned)
    last = jnp.where(row == column, diagonal, jnp.where(row < column, turned, square))
    gram = jnp.concatenate(
        [jnp.concatenate([first, cross], axis=1), jnp.concatenate([cross.T, last], axis=1)]
    )
    row = lax.broadcasted_iota(jnp.int32, (members, members), 0)
    column = lax.broadcasted_iota(jnp.int32, (members, members), 1)
    on_diagonal = row == column
    system = gram + jnp.where(on_diagonal, members - 1.0, 0.0)
    scaler = jnp.sqrt(
        jnp.sum(jnp.sum(system * system, axis=0, keepdims=True), axis=1, keepdims=True)
    )
    root = system * (1.0 / scaler)
    level = jnp.where(on_diagonal, 2.25, 0.0)

    product = root
    for step in range(0, NS_ITERS, 2):
        split = halves(product)
        square = dot3(split, split)
        higher = dot3(halves(square), halves(0.0625 * square - 0.5625 * product))
        factor = halves(level - 2.4375 * product + 1.6875 * square + higher)
        if step == 0:
            inverse = factor
        elif step < NS_ITERS - 2:
            inverse = halves(dot3(factor, inverse))
        else:
            inverse = dot3(factor, inverse)
        if step < NS_ITERS - 2:
            product = dot3(factor, halves(dot3(factor, split)))
    projected = jnp.concatenate(
        [packed_ref[2 * half + 1 : 2 * half + 2], packed_ref[2 * half + 2 : 2 * half + 3]], axis=1
    )
    once = jnp.sum(inverse * projected, axis=1, keepdims=True)
    once = jnp.sum(jnp.where(on_diagonal, once, 0.0), axis=0, keepdims=True)
    offset = jnp.sum(inverse * once, axis=1, keepdims=True) / scaler
    transform = jnp.sqrt((members - 1.0) / scaler) * inverse + offset
    matrix_ref[...] = transform
    copies = fetch((matrix_ref,), (transform_ref,), sems)
    transform = halves(transform)
    block = 128
    for start in range(0, state_ref.shape[0], block):
        rows = pl.ds(start, block)
        state = state_ref[rows]
        average = jnp.sum(state, axis=1, keepdims=True) * (1.0 / members)
        moved_ref[rows] = average + dot3(halves(state - average), transform)
        sem = sems.at[pl.ds(1 + start // block, 1)]
        copies += fetch((moved_ref.at[rows],), (analysis_ref.at[rows],), sem)
    for copy in copies:
        copy.wait()


def finish(packed, state):
    members = state.shape[1]
    square = (members, members)
    return on_core(
        finish_kernel,
        (state.shape, square),
        [pltpu.VMEM] * 2,
        [
            pltpu.VMEM(state.shape, jnp.float32),
            pltpu.VMEM(square, jnp.float32),
            pltpu.SemaphoreType.DMA((1 + state.shape[0] // 128,)),
        ],
        pltpu.HBM,
    )(packed, state)


def reduced(packed):
    lon = lax.axis_size("lon")
    lat = lax.axis_size("lat")
    width = packed.size // lon
    pieces = lax.all_to_all(packed.reshape(lon, 1, width), "lon", 0, 0)
    piece = jnp.sum(pieces, axis=0)
    pieces = lax.all_to_all(jnp.broadcast_to(piece[None], (lat, 1, width)), "lat", 0, 0)
    piece = jnp.sum(pieces, axis=0)
    pieces = lax.all_to_all(jnp.broadcast_to(piece[None], (lon, 1, width)), "lon", 0, 0)
    return pieces.reshape(packed.shape)


def local(ensemble, bathymetry, obs_cell, obs_value, obs_weight):
    fields, lon, lat, members = ensemble.shape
    vmem = pltpu.VMEM
    total_lat = lat * lax.axis_size("lat")
    wide = lat + 2 * REACH
    rows = lax.axis_index("lat") * lat - REACH + lax.broadcasted_iota(jnp.int32, (wide, 128), 0)
    inside = ((rows >= 0) & (rows < total_lat)).astype(jnp.float32)
    turning = rotation * (2.0 * (rows.astype(jnp.float32) + 0.5) / total_lat - 1.0)
    lat_shape = (ROWS * lon + 8, members)
    lon_shape = (LON_ROWS + wide, members)
    here = lax.axis_index("lon")
    parity = ((here + lax.axis_index("lat")) & 1) + 2 * (here & 1)
    parity = parity.reshape(1)
    first, second, ahead, depth = on_core(
        pack_lat_kernel,
        (lat_shape, lat_shape, (MAIN_ROWS, members), (lat, 128)),
        [pltpu.SMEM] + [pltpu.HBM] * 2,
        [
            pltpu.VMEM(ensemble.shape, jnp.float32),
            pltpu.VMEM(bathymetry.shape, jnp.int32),
            pltpu.VMEM((128, 128), jnp.float32),
            pltpu.SemaphoreType.DMA((2,)),
        ],
    )(parity, in_hbm(ensemble), in_hbm(bathymetry))
    across, within = [], []
    columns = lax.axis_size("lon")
    rows_of = lax.axis_size("lat")
    pairs = ([], [])
    for a in range(columns):
        for b in range(rows_of):
            ours = a * rows_of + b
            if b + 1 < rows_of:
                pairs[(a + b) % 2].extend(((ours, ours + 1), (ours + 1, ours)))
        (across if a % 2 else within).extend(((a, (a + 1) % columns), ((a + 1) % columns, a)))
    first = lax.ppermute(first, ("lon", "lat"), pairs[0])
    second = lax.ppermute(second, ("lon", "lat"), pairs[1])
    ahead = lax.ppermute(ahead, "lon", across)
    out_across, out_within, strip = on_core(
        pack_lon_kernel,
        ((LON_ROWS + wide - MAIN_ROWS, members), lon_shape, (wide, 128)),
        [pltpu.SMEM] + [vmem] * 4,
        [],
    )(parity, ensemble, first, second, depth)
    planes = (fields, lon, wide, members)
    across = lax.ppermute(out_across, "lon", across)
    within = lax.ppermute(out_within, "lon", within)
    inner, handed = on_core(
        inner_kernel,
        ((fields, lon - 2 * REACH, lat, members), (len(HANDED), REACH) + planes[2:]),
        [pltpu.SMEM] + [vmem] * 6,
        [pltpu.VMEM(planes, jnp.float32)] * 2
        + [pltpu.VMEM((1,) + planes[1:], jnp.float32)],
    )(parity, ensemble, first, second, strip, turning, inside)
    planes = (fields, wide, wide, members)
    forecast, packed = on_core(
        step_kernel,
        ((fields * lon * lat, members), (members + 32, members // 2)),
        [pltpu.SMEM] + [vmem] * 8 + [pltpu.HBM] * 3,
        [
            pltpu.VMEM((fields, 2 * REACH) + planes[2:], jnp.float32),
            pltpu.VMEM(planes, jnp.float32),
            pltpu.VMEM((1,) + planes[1:], jnp.float32),
            pltpu.VMEM((obs_cell.shape[2], members), jnp.float32),
            pltpu.SMEM(obs_cell.shape, jnp.int32),
        ]
        + [pltpu.VMEM(obs_value.shape, jnp.float32)] * 2
        + [pltpu.SemaphoreType.DMA((3,))],
    )(
        parity,
        ahead,
        across,
        within,
        strip,
        turning,
        inside,
        inner,
        handed,
        in_hbm(obs_cell),
        in_hbm(obs_value),
        in_hbm(obs_weight),
    )
    analysis, transform = finish(reduced(packed), forecast)
    return (analysis.reshape(ensemble.shape), transform)


def solution(mesh):
    return jax.shard_map(
        local,
        mesh=mesh,
        in_specs=(
            P(None, "lon", "lat", None),
            P("lon", "lat"),
            P("lon", "lat", None),
            P("lon", "lat", None),
            P("lon", "lat", None),
        ),
        out_specs=(P(None, "lon", "lat", None), P()),
        check_vma=False,
    )
```

```python
import functools

import jax
import jax.numpy as jnp
from jax import lax
from jax.experimental import pallas as pl
from jax.experimental.pallas import tpu as pltpu
from jax.sharding import PartitionSpec as P

STEPS = 2
NS_ITERS = 6
LEVELS = 16
REACH = 2 * STEPS
VMEM_BYTES = 24 * 1024 * 1024
TILE = 16
LAT_ROWS = (3, 3, 4)
ROWS = sum(LAT_ROWS)
MAIN_ROWS = 160
BLOCKS = 2
LON_ROWS = 192

time_step = 0.6
gravity = 1.0
rotation = 0.3


def fetch(sources, targets, sems):
    copies = [
        pltpu.make_async_copy(source, target, sems.at[k])
        for k, (source, target) in enumerate(zip(sources, targets))
    ]
    for copy in copies:
        copy.start()
    return copies


def pack_lat_kernel(
    parity_ref, ensemble_ref, bathymetry_ref, first_ref, second_ref, ahead_ref, depth_ref, state_ref, bottom_ref, square_ref, sems
):
    lon, lat = state_ref.shape[1], state_ref.shape[2]
    copies = fetch((bathymetry_ref, ensemble_ref), (bottom_ref, state_ref), sems)
    square_ref[...] = jnp.zeros_like(square_ref)
    depth_at = ROWS * lon
    for ref in (first_ref, second_ref):
        ref[depth_at:] = jnp.zeros((ref.shape[0] - depth_at, ref.shape[1]), jnp.float32)
    copies[0].wait()
    square_ref[:lon, :lat] = (bottom_ref[...].astype(jnp.float32) + 1.0) * (1.0 / LEVELS)
    turned = square_ref[...].T[:lat]
    depth_ref[...] = turned
    copies[1].wait()

    def pack(up_ref, down_ref):
        up_ref[depth_at : depth_at + 3, :128] = turned[lat - 3 : lat]
        down_ref[depth_at : depth_at + 3, :128] = turned[:3]
        for field, count in enumerate(LAT_ROWS):
            for x in range(lon):
                at = lon * sum(LAT_ROWS[:field]) + x * count
                plane = state_ref[field, x]
                up_ref[at : at + count] = plane[lat - count :]
                down_ref[at : at + count] = plane[:count]

    @pl.when(parity_ref[0] & 1 == 0)
    def _():
        pack(first_ref, second_ref)

    @pl.when(parity_ref[0] & 1 == 1)
    def _():
        pack(second_ref, first_ref)

    even_lon = parity_ref[0] < 2
    for field, distance, _, main, _ in lon_layout():
        down, up = state_ref[field, distance - 1], state_ref[field, lon - distance]
        ahead_ref[main : main + TILE] = jnp.where(even_lon, down, up)


def chosen(even, first_ref, second_ref, rows, lanes=slice(None)):
    return jnp.where(even, first_ref[rows, lanes], second_ref[rows, lanes])


def lat_rows(even, first_ref, second_ref, field, x, lon):
    at = lon * sum(LAT_ROWS[:field]) + x * LAT_ROWS[field]
    return chosen(even, first_ref, second_ref, slice(at, at + LAT_ROWS[field]))


def lon_layout():
    main, corner = 0, MAIN_ROWS
    for field, width, reach in ((0, 3, 3), (1, 4, 4), (2, 3, 4)):
        for distance in range(1, width + 1):
            beyond = reach - distance
            yield field, distance, beyond, main, corner
            main += TILE
            corner += 2 * beyond


def pack_lon_kernel(
    parity_ref, state_ref, first_ref, second_ref, depth_ref, across_ref, within_ref, strip_ref
):
    lon = state_ref.shape[1]
    even = parity_ref[0] & 1 == 0
    low_rows = functools.partial(lat_rows, even, second_ref, first_ref)
    high_rows = functools.partial(lat_rows, even, first_ref, second_ref)
    depth_at = ROWS * lon
    strip_ref[...] = jnp.zeros_like(strip_ref)
    depths = slice(depth_at, depth_at + 3)
    strip_ref[1:4] = chosen(even, second_ref, first_ref, depths, slice(0, 128))
    strip_ref[4:20] = depth_ref[...]
    strip_ref[20:23] = chosen(even, first_ref, second_ref, depths, slice(0, 128))
    for ref, skipped in ((across_ref, MAIN_ROWS), (within_ref, 0)):
        depths = slice(LON_ROWS - skipped, None)
        ref[depths, 128:] = jnp.zeros((strip_ref.shape[0], 128), jnp.float32)
        ref[LON_ROWS - 2 - skipped : LON_ROWS - skipped] = jnp.zeros((2, ref.shape[1]), jnp.float32)
        ref[depths, :128] = strip_ref[...]

    def pack(upward):
        for field, distance, beyond, main, corner in lon_layout():
            up, down = lon - distance, distance - 1
            for ref, x, skipped in (
                (across_ref, up if upward else down, MAIN_ROWS),
                (within_ref, down if upward else up, 0),
            ):
                if beyond:
                    at = corner - skipped
                    low = low_rows(field, x, lon)
                    ref[at : at + beyond] = low[LAT_ROWS[field] - beyond :]
                    high = high_rows(field, x, lon)
                    ref[at + beyond : at + 2 * beyond] = high[:beyond]
                if not skipped:
                    ref[main : main + TILE] = state_ref[field, x]

    @pl.when(parity_ref[0] < 2)
    def _():
        pack(False)

    @pl.when(parity_ref[0] >= 2)
    def _():
        pack(True)


def dot3_first(left, right):
    dims = (((0,), (0,)), ((), ()))
    left_high, left_low = left
    right_high, right_low = right
    return lax.dot_general(
        jnp.concatenate([left_high, left_high, left_low]),
        jnp.concatenate([right_high, right_low, right_high]),
        dims,
        preferred_element_type=jnp.float32,
    )


def along(plane):
    return pltpu.roll(plane, plane.shape[0] - 1, 0) - pltpu.roll(plane, 1, 0)


def advance_height(source, depth, x):
    spread = source(1, x + 1) - source(1, x - 1) + along(source(2, x))
    return source(0, x) - depth(x) * spread


def advance_flow(source, height, turning, x):
    pull = 0.5 * time_step * gravity
    east = source(1, x)
    north = source(2, x)
    slope_east = height(x + 1) - height(x - 1)
    slope_north = along(height(x))
    return (
        east + (turning * north - pull * slope_east),
        north - (turning * east + pull * slope_north),
    )


def spread_out(column, shape):
    return jnp.broadcast_to(column, shape)


HANDED = ((4, 5, 18, 19),) * 3 + ((5, 6, 17, 18),) + ((6, 7, 16, 17),) * 2 + ((7, 8, 15, 16),)


def inner_kernel(
    parity_ref,
    state_ref,
    first_ref,
    second_ref,
    strip_ref,
    turning_ref,
    inside_ref,
    inner_ref,
    handed_ref,
    field_ref,
    next_ref,
    last_ref,
):
    lon = state_ref.shape[1]
    shape = field_ref.shape[2:]
    even = parity_ref[0] & 1 == 0
    low_rows = functools.partial(lat_rows, even, second_ref, first_ref)
    high_rows = functools.partial(lat_rows, even, first_ref, second_ref)
    for field, count in enumerate(LAT_ROWS):
        for x in range(lon):
            field_ref[field, x, REACH : REACH + TILE] = state_ref[field, x]
            field_ref[field, x, REACH - count : REACH] = low_rows(field, x, lon)
            field_ref[field, x, REACH + TILE : REACH + TILE + count] = high_rows(field, x, lon)
    turning = time_step * spread_out(turning_ref[:, :1], shape)
    keeper = spread_out(inside_ref[:, :1], shape)
    strip = 0.5 * time_step * strip_ref[...]
    end = lon + 2 * REACH

    def depth(x):
        return spread_out(strip[:, x - REACH : x - REACH + 1], shape)

    def source(field, x):
        return field_ref[field, x - REACH]

    def after(field, x):
        return next_ref[field, x - REACH]

    def height(x):
        return next_ref[0, x - REACH]

    def last_height(x):
        return last_ref[0, x - REACH]

    for x in range(REACH + 1, end - REACH - 1):
        next_ref[0, x - REACH] = advance_height(source, depth, x)
    for x in range(REACH + 2, end - REACH - 2):
        east, north = advance_flow(source, height, turning, x)
        next_ref[1, x - REACH] = east
        next_ref[2, x - REACH] = north * keeper
    for x in range(REACH + 3, end - REACH - 3):
        last_ref[0, x - REACH] = advance_height(after, depth, x)
    for x in range(2 * REACH, end - 2 * REACH):
        east, north = advance_flow(after, last_height, turning, x)
        for field, plane in enumerate((last_height(x), east, north)):
            inner_ref[field, x - 2 * REACH] = plane[REACH : REACH + TILE]
    kinds = (
        functools.partial(source, 0),
        functools.partial(source, 1),
        functools.partial(source, 2),
        height,
        functools.partial(after, 1),
        functools.partial(after, 2),
        last_height,
    )
    for kind, (columns, plane) in enumerate(zip(HANDED, kinds)):
        for k, x in enumerate(columns):
            handed_ref[kind, k] = plane(x)


def step_kernel(
    parity_ref,
    ahead_ref,
    across_ref,
    within_ref,
    strip_ref,
    turning_ref,
    inside_ref,
    inner_ref,
    handed_ref,
    obs_cell_ref,
    obs_value_ref,
    obs_weight_ref,
    forecast_ref,
    packed_ref,
    field_ref,
    next_ref,
    last_ref,
    picked_ref,
    cell_ref,
    value_ref,
    weight_ref,
    sems,
):
    copies = fetch(
        (obs_cell_ref, obs_value_ref, obs_weight_ref), (cell_ref, value_ref, weight_ref), sems
    )
    shape = field_ref.shape[2:]
    members = shape[1]
    end = next_ref.shape[1]
    lon = end - 2 * REACH
    even_lon = parity_ref[0] < 2

    def taken(rows, lanes=slice(None)):
        start, stop = rows
        if stop <= MAIN_ROWS:
            across = ahead_ref[start:stop, lanes]
        else:
            across = across_ref[start - MAIN_ROWS : stop - MAIN_ROWS, lanes]
        within = within_ref[start:stop, lanes]
        return jnp.where(even_lon, across, within), jnp.where(even_lon, within, across)

    for field, distance, beyond, main, corner in lon_layout():
        parts = [((main, main + TILE), REACH, TILE)]
        if beyond:
            parts.append(((corner, corner + beyond), REACH - beyond, beyond))
            parts.append(((corner + beyond, corner + 2 * beyond), REACH + TILE, beyond))
        for rows, at, count in parts:
            west, east = taken(rows)
            field_ref[field, REACH - distance, at : at + count] = west
            field_ref[field, REACH - 1 + distance, at : at + count] = east
    west_strip, east_strip = taken((LON_ROWS, within_ref.shape[0]), slice(0, 128))
    turning = time_step * spread_out(turning_ref[:, :1], shape)
    keeper = spread_out(inside_ref[:, :1], shape)
    strips = [0.5 * time_step * strip for strip in (west_strip, strip_ref[...], east_strip)]

    def depth(x):
        if x < REACH:
            column = strips[0][:, lon - REACH + x : lon - REACH + x + 1]
        elif x < REACH + lon:
            column = strips[1][:, x - REACH : x - REACH + 1]
        else:
            column = strips[2][:, x - REACH - lon : x - REACH - lon + 1]
        return spread_out(column, shape)

    def source(field, x):
        if x < REACH:
            return field_ref[field, x]
        if x >= REACH + lon:
            return field_ref[field, x - lon]
        return handed_ref[field, HANDED[field].index(x)]

    def after(field, x):
        if x in HANDED[3 + field]:
            return handed_ref[3 + field, HANDED[3 + field].index(x)]
        return next_ref[field, x]

    def height(x):
        return after(0, x)

    def last_height(x):
        if x in HANDED[6]:
            return handed_ref[6, HANDED[6].index(x)]
        return last_ref[0, x]

    def edges(margin):
        return (*range(margin, margin + REACH), *range(end - margin - REACH, end - margin))

    for x in edges(1):
        next_ref[0, x] = advance_height(source, depth, x)
    for x in edges(2):
        east_flow, north_flow = advance_flow(source, height, turning, x)
        next_ref[1, x] = east_flow
        next_ref[2, x] = north_flow * keeper
    for x in edges(3):
        last_ref[0, x] = advance_height(after, depth, x)
    for x in edges(REACH):
        east_flow, north_flow = advance_flow(after, last_height, turning, x)
        for field, plane in enumerate((last_height(x), east_flow, north_flow)):
            at = (field * lon + x - REACH) * TILE
            forecast_ref[at : at + TILE] = plane[REACH : REACH + TILE]
    for field in range(len(LAT_ROWS)):
        for x in range(REACH, lon - REACH):
            at = (field * lon + x) * TILE
            forecast_ref[at : at + TILE] = inner_ref[field, x - REACH]

    for copy in copies:
        copy.wait()
    count = picked_ref.shape[0]
    for k in range(count):
        picked_ref[k : k + 1] = forecast_ref[pl.ds(cell_ref[0, 0, k], 1)]
    picked = picked_ref[...]
    ymean = jnp.sum(picked, axis=1, keepdims=True) * (1.0 / members)
    half = members // 2
    row = lax.broadcasted_iota(jnp.int32, (half, half), 0)
    line = lax.broadcasted_iota(jnp.int32, (half, half), 1)
    on_diagonal = row == line
    weight = jnp.sum(jnp.where(on_diagonal, weight_ref[0], 0.0), axis=1, keepdims=True)
    value = jnp.sum(jnp.where(on_diagonal, value_ref[0], 0.0), axis=1, keepdims=True)
    anomaly = (picked - ymean) * weight
    innovation = (value - ymean) * weight
    projected = jnp.sum(innovation * anomaly, axis=0, keepdims=True)
    left_high, left_low = halves(anomaly[:, :half])
    right_high, right_low = halves(anomaly[:, half:])
    first = dot3_first((left_high, left_low), (left_high, left_low))
    cross = dot3_first((left_high, left_low), (right_high, right_low))
    final = dot3_first((right_high, right_low), (right_high, right_low))
    packed_ref[:half] = jnp.where(row <= line, first, final)
    packed_ref[half : 2 * half] = cross
    packed_ref[2 * half :] = jnp.zeros((packed_ref.shape[0] - 2 * half, half), jnp.float32)
    packed_ref[2 * half : 2 * half + 1] = jnp.sum(
        jnp.where(on_diagonal, final, 0.0), axis=0, keepdims=True
    )
    packed_ref[2 * half + 1 : 2 * half + 2] = projected[:, :half]
    packed_ref[2 * half + 2 : 2 * half + 3] = projected[:, half:]


def in_hbm(value):
    return pltpu.with_memory_space_constraint(value, pltpu.HBM)


def on_core(kernel, outs, spaces, scratch, out_space=pltpu.VMEM):
    return pl.pallas_call(
        kernel,
        out_shape=tuple(jax.ShapeDtypeStruct(shape, jnp.float32) for shape in outs),
        in_specs=[pl.BlockSpec(memory_space=space) for space in spaces],
        out_specs=tuple(pl.BlockSpec(memory_space=out_space) for _ in outs),
        scratch_shapes=scratch,
        compiler_params=pltpu.CompilerParams(vmem_limit_bytes=VMEM_BYTES),
    )


def halves(value):
    high = value.astype(jnp.bfloat16)
    return high, (value - high.astype(jnp.float32)).astype(jnp.bfloat16)


def dot3(left, right):
    left_high, left_low = left
    right_high, right_low = right
    return jnp.dot(
        jnp.concatenate([left_high, left_high, left_low], axis=1),
        jnp.concatenate([right_high, right_low, right_high], axis=0),
        preferred_element_type=jnp.float32,
    )


def finish_kernel(
    packed_ref,
    state_ref,
    analysis_ref,
    transform_ref,
    moved_ref,
    matrix_ref,
    split_ref,
    product_ref,
    square_ref,
    level_ref,
    sems,
):
    half = packed_ref.shape[1]
    members = 2 * half
    square = packed_ref[:half]
    cross = packed_ref[half : 2 * half]
    diagonal = packed_ref[2 * half : 2 * half + 1]
    turned = square.T
    row = lax.broadcasted_iota(jnp.int32, (half, half), 0)
    column = lax.broadcasted_iota(jnp.int32, (half, half), 1)
    first = jnp.where(row <= column, square, turned)
    last = jnp.where(row == column, diagonal, jnp.where(row < column, turned, square))
    gram = jnp.concatenate(
        [jnp.concatenate([first, cross], axis=1), jnp.concatenate([cross.T, last], axis=1)]
    )
    row = lax.broadcasted_iota(jnp.int32, (members, members), 0)
    column = lax.broadcasted_iota(jnp.int32, (members, members), 1)
    on_diagonal = row == column
    system = gram + jnp.where(on_diagonal, members - 1.0, 0.0)
    scaler = jnp.sqrt(
        jnp.sum(jnp.sum(system * system, axis=0, keepdims=True), axis=1, keepdims=True)
    )
    root = system * (1.0 / scaler)
    block = members // BLOCKS
    spans = [slice(k * block, (k + 1) * block) for k in range(BLOCKS)]

    def store(target, rows, value):
        high, low = halves(value)
        split_ref[target, 0, rows] = high
        split_ref[target, 1, rows] = low

    def multiply(left, right, use):
        high, low = split_ref[right, 0], split_ref[right, 1]
        deep = jnp.concatenate([high, low, high], axis=0)
        for rows in spans:
            high, low = split_ref[left, 0, rows], split_ref[left, 1, rows]
            wide = jnp.concatenate([high, high, low], axis=1)
            use(rows, jnp.dot(wide, deep, preferred_element_type=jnp.float32))

    level = jnp.where(on_diagonal, 2.25, 0.0)
    level_ref[...] = level
    product_ref[...] = root
    product, square, mixed, factor, turned_product = range(5)
    inverse, inverse_next = 5, 6
    for rows in spans:
        store(product, rows, root[rows])

    def use_square(rows, value):
        square_ref[rows] = value
        store(square, rows, value)
        store(mixed, rows, 0.0625 * value - 0.5625 * product_ref[rows])

    def use_higher(target, rows, value):
        value = value + (level_ref[rows] - 2.4375 * product_ref[rows] + 1.6875 * square_ref[rows])
        store(target, rows, value)

    def use_product(rows, value):
        product_ref[rows] = value
        store(product, rows, value)

    def use_last(rows, value):
        matrix_ref[rows] = value

    for step in range(0, NS_ITERS, 2):
        multiply(product, product, use_square)
        target = inverse if step == 0 else factor
        multiply(square, mixed, functools.partial(use_higher, target))
        if step < NS_ITERS - 2:
            multiply(target, product, functools.partial(store, turned_product))
            if step > 0:
                multiply(factor, inverse, functools.partial(store, inverse_next))
                inverse, inverse_next = inverse_next, inverse
            multiply(target, turned_product, use_product)
        else:
            multiply(factor, inverse, use_last)
    inverse = matrix_ref[...]
    projected = jnp.concatenate(
        [packed_ref[2 * half + 1 : 2 * half + 2], packed_ref[2 * half + 2 : 2 * half + 3]], axis=1
    )
    once = jnp.sum(inverse * projected, axis=1, keepdims=True)
    once = jnp.sum(jnp.where(on_diagonal, once, 0.0), axis=0, keepdims=True)
    offset = jnp.sum(inverse * once, axis=1, keepdims=True) / scaler
    transform = jnp.sqrt((members - 1.0) / scaler) * inverse + offset
    matrix_ref[...] = transform
    copies = fetch((matrix_ref,), (transform_ref,), sems)
    transform = halves(transform)
    block = 128
    for start in range(0, state_ref.shape[0], block):
        rows = pl.ds(start, block)
        state = state_ref[rows]
        average = jnp.sum(state, axis=1, keepdims=True) * (1.0 / members)
        moved_ref[rows] = average + dot3(halves(state - average), transform)
        sem = sems.at[pl.ds(1 + start // block, 1)]
        copies += fetch((moved_ref.at[rows],), (analysis_ref.at[rows],), sem)
    for copy in copies:
        copy.wait()


def finish(packed, state):
    members = state.shape[1]
    square = (members, members)
    return on_core(
        finish_kernel,
        (state.shape, square),
        [pltpu.VMEM] * 2,
        [
            pltpu.VMEM(state.shape, jnp.float32),
            pltpu.VMEM(square, jnp.float32),
            pltpu.VMEM((7, 2) + square, jnp.bfloat16),
            pltpu.VMEM(square, jnp.float32),
            pltpu.VMEM(square, jnp.float32),
            pltpu.VMEM(square, jnp.float32),
            pltpu.SemaphoreType.DMA((1 + state.shape[0] // 128,)),
        ],
        pltpu.HBM,
    )(packed, state)


def reduced(packed):
    lon = lax.axis_size("lon")
    lat = lax.axis_size("lat")
    width = packed.size // lon
    pieces = lax.all_to_all(packed.reshape(lon, 1, width), "lon", 0, 0)
    piece = jnp.sum(pieces, axis=0)
    pieces = lax.all_to_all(jnp.broadcast_to(piece[None], (lat, 1, width)), "lat", 0, 0)
    piece = jnp.sum(pieces, axis=0)
    pieces = lax.all_to_all(jnp.broadcast_to(piece[None], (lon, 1, width)), "lon", 0, 0)
    return pieces.reshape(packed.shape)


def local(ensemble, bathymetry, obs_cell, obs_value, obs_weight):
    fields, lon, lat, members = ensemble.shape
    vmem = pltpu.VMEM
    total_lat = lat * lax.axis_size("lat")
    wide = lat + 2 * REACH
    rows = lax.axis_index("lat") * lat - REACH + lax.broadcasted_iota(jnp.int32, (wide, 128), 0)
    inside = ((rows >= 0) & (rows < total_lat)).astype(jnp.float32)
    turning = rotation * (2.0 * (rows.astype(jnp.float32) + 0.5) / total_lat - 1.0)
    lat_shape = (ROWS * lon + 8, members)
    lon_shape = (LON_ROWS + wide, members)
    here = lax.axis_index("lon")
    parity = ((here + lax.axis_index("lat")) & 1) + 2 * (here & 1)
    parity = parity.reshape(1)
    first, second, ahead, depth = on_core(
        pack_lat_kernel,
        (lat_shape, lat_shape, (MAIN_ROWS, members), (lat, 128)),
        [pltpu.SMEM] + [pltpu.HBM] * 2,
        [
            pltpu.VMEM(ensemble.shape, jnp.float32),
            pltpu.VMEM(bathymetry.shape, jnp.int32),
            pltpu.VMEM((128, 128), jnp.float32),
            pltpu.SemaphoreType.DMA((2,)),
        ],
    )(parity, in_hbm(ensemble), in_hbm(bathymetry))
    across, within = [], []
    columns = lax.axis_size("lon")
    rows_of = lax.axis_size("lat")
    pairs = ([], [])
    for a in range(columns):
        for b in range(rows_of):
            ours = a * rows_of + b
            if b + 1 < rows_of:
                pairs[(a + b) % 2].extend(((ours, ours + 1), (ours + 1, ours)))
        (across if a % 2 else within).extend(((a, (a + 1) % columns), ((a + 1) % columns, a)))
    first = lax.ppermute(first, ("lon", "lat"), pairs[0])
    second = lax.ppermute(second, ("lon", "lat"), pairs[1])
    ahead = lax.ppermute(ahead, "lon", across)
    out_across, out_within, strip = on_core(
        pack_lon_kernel,
        ((LON_ROWS + wide - MAIN_ROWS, members), lon_shape, (wide, 128)),
        [pltpu.SMEM] + [vmem] * 4,
        [],
    )(parity, ensemble, first, second, depth)
    planes = (fields, lon, wide, members)
    across = lax.ppermute(out_across, "lon", across)
    within = lax.ppermute(out_within, "lon", within)
    inner, handed = on_core(
        inner_kernel,
        ((fields, lon - 2 * REACH, lat, members), (len(HANDED), REACH) + planes[2:]),
        [pltpu.SMEM] + [vmem] * 6,
        [pltpu.VMEM(planes, jnp.float32)] * 2
        + [pltpu.VMEM((1,) + planes[1:], jnp.float32)],
    )(parity, ensemble, first, second, strip, turning, inside)
    planes = (fields, wide, wide, members)
    forecast, packed = on_core(
        step_kernel,
        ((fields * lon * lat, members), (members + 32, members // 2)),
        [pltpu.SMEM] + [vmem] * 8 + [pltpu.HBM] * 3,
        [
            pltpu.VMEM((fields, 2 * REACH) + planes[2:], jnp.float32),
            pltpu.VMEM(planes, jnp.float32),
            pltpu.VMEM((1,) + planes[1:], jnp.float32),
            pltpu.VMEM((obs_cell.shape[2], members), jnp.float32),
            pltpu.SMEM(obs_cell.shape, jnp.int32),
        ]
        + [pltpu.VMEM(obs_value.shape, jnp.float32)] * 2
        + [pltpu.SemaphoreType.DMA((3,))],
    )(
        parity,
        ahead,
        across,
        within,
        strip,
        turning,
        inside,
        inner,
        handed,
        in_hbm(obs_cell),
        in_hbm(obs_value),
        in_hbm(obs_weight),
    )
    analysis, transform = finish(reduced(packed), forecast)
    return (analysis.reshape(ensemble.shape), transform)


def solution(mesh):
    return jax.shard_map(
        local,
        mesh=mesh,
        in_specs=(
            P(None, "lon", "lat", None),
            P("lon", "lat"),
            P("lon", "lat", None),
            P("lon", "lat", None),
            P("lon", "lat", None),
        ),
        out_specs=(P(None, "lon", "lat", None), P()),
        check_vma=False,
    )
```

```python
import functools

import jax
import jax.numpy as jnp
from jax import lax
from jax.experimental import pallas as pl
from jax.experimental.pallas import tpu as pltpu
from jax.sharding import PartitionSpec as P

STEPS = 2
NS_ITERS = 6
LEVELS = 16
REACH = 2 * STEPS
VMEM_BYTES = 24 * 1024 * 1024
TILE = 16
LAT_ROWS = (3, 3, 4)
ROWS = sum(LAT_ROWS)
MAIN_ROWS = 160
BLOCKS = 2
LON_ROWS = 192

time_step = 0.6
gravity = 1.0
rotation = 0.3


def fetch(sources, targets, sems):
    copies = [
        pltpu.make_async_copy(source, target, sems.at[k])
        for k, (source, target) in enumerate(zip(sources, targets))
    ]
    for copy in copies:
        copy.start()
    return copies


def pack_lat_kernel(
    parity_ref, ensemble_ref, bathymetry_ref, first_ref, second_ref, ahead_ref, depth_ref, state_ref, bottom_ref, square_ref, sems
):
    lon, lat = state_ref.shape[1], state_ref.shape[2]
    copies = fetch((bathymetry_ref, ensemble_ref), (bottom_ref, state_ref), sems)
    square_ref[...] = jnp.zeros_like(square_ref)
    depth_at = ROWS * lon
    for ref in (first_ref, second_ref):
        ref[depth_at:] = jnp.zeros((ref.shape[0] - depth_at, ref.shape[1]), jnp.float32)
    copies[0].wait()
    square_ref[:lon, :lat] = (bottom_ref[...].astype(jnp.float32) + 1.0) * (1.0 / LEVELS)
    turned = square_ref[...].T[:lat]
    depth_ref[...] = turned
    copies[1].wait()

    def pack(up_ref, down_ref):
        up_ref[depth_at : depth_at + 3, :128] = turned[lat - 3 : lat]
        down_ref[depth_at : depth_at + 3, :128] = turned[:3]
        for field, count in enumerate(LAT_ROWS):
            for x in range(lon):
                at = lon * sum(LAT_ROWS[:field]) + x * count
                plane = state_ref[field, x]
                up_ref[at : at + count] = plane[lat - count :]
                down_ref[at : at + count] = plane[:count]

    @pl.when(parity_ref[0] == 0)
    def _():
        pack(first_ref, second_ref)

    @pl.when(parity_ref[0] == 1)
    def _():
        pack(second_ref, first_ref)

    even_lon = parity_ref[0] == 0
    for field, distance, _, main, _ in lon_layout():
        down, up = state_ref[field, distance - 1], state_ref[field, lon - distance]
        ahead_ref[main : main + TILE] = jnp.where(even_lon, down, up)


def chosen(even, first_ref, second_ref, rows, lanes=slice(None)):
    return jnp.where(even, first_ref[rows, lanes], second_ref[rows, lanes])


def lat_rows(even, first_ref, second_ref, field, x, lon):
    at = lon * sum(LAT_ROWS[:field]) + x * LAT_ROWS[field]
    return chosen(even, first_ref, second_ref, slice(at, at + LAT_ROWS[field]))


def lon_layout():
    main, corner = 0, MAIN_ROWS
    for field, width, reach in ((0, 3, 3), (1, 4, 4), (2, 3, 4)):
        for distance in range(1, width + 1):
            beyond = reach - distance
            yield field, distance, beyond, main, corner
            main += TILE
            corner += 2 * beyond


def pack_lon_kernel(
    parity_ref, state_ref, first_ref, second_ref, depth_ref, across_ref, within_ref, strip_ref
):
    lon = state_ref.shape[1]
    even = parity_ref[0] == 0
    low_rows = functools.partial(lat_rows, even, first_ref, second_ref)
    high_rows = functools.partial(lat_rows, even, second_ref, first_ref)
    depth_at = ROWS * lon
    strip_ref[...] = jnp.zeros_like(strip_ref)
    depths = slice(depth_at, depth_at + 3)
    strip_ref[1:4] = chosen(even, first_ref, second_ref, depths, slice(0, 128))
    strip_ref[4:20] = depth_ref[...]
    strip_ref[20:23] = chosen(even, second_ref, first_ref, depths, slice(0, 128))
    for ref, skipped in ((across_ref, MAIN_ROWS), (within_ref, 0)):
        depths = slice(LON_ROWS - skipped, None)
        ref[depths, 128:] = jnp.zeros((strip_ref.shape[0], 128), jnp.float32)
        ref[LON_ROWS - 2 - skipped : LON_ROWS - skipped] = jnp.zeros((2, ref.shape[1]), jnp.float32)
        ref[depths, :128] = strip_ref[...]

    def pack(upward):
        for field, distance, beyond, main, corner in lon_layout():
            up, down = lon - distance, distance - 1
            for ref, x, skipped in (
                (across_ref, up if upward else down, MAIN_ROWS),
                (within_ref, down if upward else up, 0),
            ):
                if beyond:
                    at = corner - skipped
                    low = low_rows(field, x, lon)
                    ref[at : at + beyond] = low[LAT_ROWS[field] - beyond :]
                    high = high_rows(field, x, lon)
                    ref[at + beyond : at + 2 * beyond] = high[:beyond]
                if not skipped:
                    ref[main : main + TILE] = state_ref[field, x]

    @pl.when(parity_ref[0] == 0)
    def _():
        pack(False)

    @pl.when(parity_ref[0] == 1)
    def _():
        pack(True)


def dot3_first(left, right):
    dims = (((0,), (0,)), ((), ()))
    left_high, left_low = left
    right_high, right_low = right
    return lax.dot_general(
        jnp.concatenate([left_high, left_high, left_low]),
        jnp.concatenate([right_high, right_low, right_high]),
        dims,
        preferred_element_type=jnp.float32,
    )


def along(plane):
    return pltpu.roll(plane, plane.shape[0] - 1, 0) - pltpu.roll(plane, 1, 0)


def advance_height(source, depth, x):
    spread = source(1, x + 1) - source(1, x - 1) + along(source(2, x))
    return source(0, x) - depth(x) * spread


def advance_flow(source, height, turning, x):
    pull = 0.5 * time_step * gravity
    east = source(1, x)
    north = source(2, x)
    slope_east = height(x + 1) - height(x - 1)
    slope_north = along(height(x))
    return (
        east + (turning * north - pull * slope_east),
        north - (turning * east + pull * slope_north),
    )


def spread_out(column, shape):
    return jnp.broadcast_to(column, shape)


HANDED = ((4, 5, 18, 19),) * 3 + ((5, 6, 17, 18),) + ((6, 7, 16, 17),) * 2 + ((7, 8, 15, 16),)


def inner_kernel(
    parity_ref,
    state_ref,
    first_ref,
    second_ref,
    strip_ref,
    turning_ref,
    inside_ref,
    inner_ref,
    handed_ref,
    field_ref,
    next_ref,
    last_ref,
):
    lon = state_ref.shape[1]
    shape = field_ref.shape[2:]
    even = parity_ref[0] == 0
    low_rows = functools.partial(lat_rows, even, first_ref, second_ref)
    high_rows = functools.partial(lat_rows, even, second_ref, first_ref)
    for field, count in enumerate(LAT_ROWS):
        for x in range(lon):
            field_ref[field, x, REACH : REACH + TILE] = state_ref[field, x]
            field_ref[field, x, REACH - count : REACH] = low_rows(field, x, lon)
            field_ref[field, x, REACH + TILE : REACH + TILE + count] = high_rows(field, x, lon)
    turning = time_step * spread_out(turning_ref[:, :1], shape)
    keeper = spread_out(inside_ref[:, :1], shape)
    strip = 0.5 * time_step * strip_ref[...]
    end = lon + 2 * REACH

    def depth(x):
        return spread_out(strip[:, x - REACH : x - REACH + 1], shape)

    def source(field, x):
        return field_ref[field, x - REACH]

    def after(field, x):
        return next_ref[field, x - REACH]

    def height(x):
        return next_ref[0, x - REACH]

    def last_height(x):
        return last_ref[0, x - REACH]

    for x in range(REACH + 1, end - REACH - 1):
        next_ref[0, x - REACH] = advance_height(source, depth, x)
    for x in range(REACH + 2, end - REACH - 2):
        east, north = advance_flow(source, height, turning, x)
        next_ref[1, x - REACH] = east
        next_ref[2, x - REACH] = north * keeper
    for x in range(REACH + 3, end - REACH - 3):
        last_ref[0, x - REACH] = advance_height(after, depth, x)
    for x in range(2 * REACH, end - 2 * REACH):
        east, north = advance_flow(after, last_height, turning, x)
        for field, plane in enumerate((last_height(x), east, north)):
            inner_ref[field, x - 2 * REACH] = plane[REACH : REACH + TILE]
    kinds = (
        functools.partial(source, 0),
        functools.partial(source, 1),
        functools.partial(source, 2),
        height,
        functools.partial(after, 1),
        functools.partial(after, 2),
        last_height,
    )
    for kind, (columns, plane) in enumerate(zip(HANDED, kinds)):
        for k, x in enumerate(columns):
            handed_ref[kind, k] = plane(x)


def step_kernel(
    parity_ref,
    ahead_ref,
    across_ref,
    within_ref,
    strip_ref,
    turning_ref,
    inside_ref,
    inner_ref,
    handed_ref,
    obs_cell_ref,
    obs_value_ref,
    obs_weight_ref,
    forecast_ref,
    packed_ref,
    field_ref,
    next_ref,
    last_ref,
    picked_ref,
    cell_ref,
    value_ref,
    weight_ref,
    sems,
):
    copies = fetch(
        (obs_cell_ref, obs_value_ref, obs_weight_ref), (cell_ref, value_ref, weight_ref), sems
    )
    shape = field_ref.shape[2:]
    members = shape[1]
    end = next_ref.shape[1]
    lon = end - 2 * REACH
    even_lon = parity_ref[0] == 0

    def taken(rows, lanes=slice(None)):
        start, stop = rows
        if stop <= MAIN_ROWS:
            across = ahead_ref[start:stop, lanes]
        else:
            across = across_ref[start - MAIN_ROWS : stop - MAIN_ROWS, lanes]
        within = within_ref[start:stop, lanes]
        return jnp.where(even_lon, across, within), jnp.where(even_lon, within, across)

    for field, distance, beyond, main, corner in lon_layout():
        parts = [((main, main + TILE), REACH, TILE)]
        if beyond:
            parts.append(((corner, corner + beyond), REACH - beyond, beyond))
            parts.append(((corner + beyond, corner + 2 * beyond), REACH + TILE, beyond))
        for rows, at, count in parts:
            west, east = taken(rows)
            field_ref[field, REACH - distance, at : at + count] = west
            field_ref[field, REACH - 1 + distance, at : at + count] = east
    west_strip, east_strip = taken((LON_ROWS, within_ref.shape[0]), slice(0, 128))
    turning = time_step * spread_out(turning_ref[:, :1], shape)
    keeper = spread_out(inside_ref[:, :1], shape)
    strips = [0.5 * time_step * strip for strip in (west_strip, strip_ref[...], east_strip)]

    def depth(x):
        if x < REACH:
            column = strips[0][:, lon - REACH + x : lon - REACH + x + 1]
        elif x < REACH + lon:
            column = strips[1][:, x - REACH : x - REACH + 1]
        else:
            column = strips[2][:, x - REACH - lon : x - REACH - lon + 1]
        return spread_out(column, shape)

    def source(field, x):
        if x < REACH:
            return field_ref[field, x]
        if x >= REACH + lon:
            return field_ref[field, x - lon]
        return handed_ref[field, HANDED[field].index(x)]

    def after(field, x):
        if x in HANDED[3 + field]:
            return handed_ref[3 + field, HANDED[3 + field].index(x)]
        return next_ref[field, x]

    def height(x):
        return after(0, x)

    def last_height(x):
        if x in HANDED[6]:
            return handed_ref[6, HANDED[6].index(x)]
        return last_ref[0, x]

    def edges(margin):
        return (*range(margin, margin + REACH), *range(end - margin - REACH, end - margin))

    for x in edges(1):
        next_ref[0, x] = advance_height(source, depth, x)
    for x in edges(2):
        east_flow, north_flow = advance_flow(source, height, turning, x)
        next_ref[1, x] = east_flow
        next_ref[2, x] = north_flow * keeper
    for x in edges(3):
        last_ref[0, x] = advance_height(after, depth, x)
    for x in edges(REACH):
        east_flow, north_flow = advance_flow(after, last_height, turning, x)
        for field, plane in enumerate((last_height(x), east_flow, north_flow)):
            at = (field * lon + x - REACH) * TILE
            forecast_ref[at : at + TILE] = plane[REACH : REACH + TILE]
    for field in range(len(LAT_ROWS)):
        for x in range(REACH, lon - REACH):
            at = (field * lon + x) * TILE
            forecast_ref[at : at + TILE] = inner_ref[field, x - REACH]

    for copy in copies:
        copy.wait()
    count = picked_ref.shape[0]
    for k in range(count):
        picked_ref[k : k + 1] = forecast_ref[pl.ds(cell_ref[0, 0, k], 1)]
    picked = picked_ref[...]
    ymean = jnp.sum(picked, axis=1, keepdims=True) * (1.0 / members)
    half = members // 2
    row = lax.broadcasted_iota(jnp.int32, (half, half), 0)
    line = lax.broadcasted_iota(jnp.int32, (half, half), 1)
    on_diagonal = row == line
    weight = jnp.sum(jnp.where(on_diagonal, weight_ref[0], 0.0), axis=1, keepdims=True)
    value = jnp.sum(jnp.where(on_diagonal, value_ref[0], 0.0), axis=1, keepdims=True)
    anomaly = (picked - ymean) * weight
    innovation = (value - ymean) * weight
    projected = jnp.sum(innovation * anomaly, axis=0, keepdims=True)
    left_high, left_low = halves(anomaly[:, :half])
    right_high, right_low = halves(anomaly[:, half:])
    first = dot3_first((left_high, left_low), (left_high, left_low))
    cross = dot3_first((left_high, left_low), (right_high, right_low))
    final = dot3_first((right_high, right_low), (right_high, right_low))
    packed_ref[:half] = jnp.where(row <= line, first, final)
    packed_ref[half : 2 * half] = cross
    packed_ref[2 * half :] = jnp.zeros((packed_ref.shape[0] - 2 * half, half), jnp.float32)
    packed_ref[2 * half : 2 * half + 1] = jnp.sum(
        jnp.where(on_diagonal, final, 0.0), axis=0, keepdims=True
    )
    packed_ref[2 * half + 1 : 2 * half + 2] = projected[:, :half]
    packed_ref[2 * half + 2 : 2 * half + 3] = projected[:, half:]


def in_hbm(value):
    return pltpu.with_memory_space_constraint(value, pltpu.HBM)


def on_core(kernel, outs, spaces, scratch, out_space=pltpu.VMEM):
    return pl.pallas_call(
        kernel,
        out_shape=tuple(jax.ShapeDtypeStruct(shape, jnp.float32) for shape in outs),
        in_specs=[pl.BlockSpec(memory_space=space) for space in spaces],
        out_specs=tuple(pl.BlockSpec(memory_space=out_space) for _ in outs),
        scratch_shapes=scratch,
        compiler_params=pltpu.CompilerParams(vmem_limit_bytes=VMEM_BYTES),
    )


def halves(value):
    high = value.astype(jnp.bfloat16)
    return high, (value - high.astype(jnp.float32)).astype(jnp.bfloat16)


def dot3(left, right):
    left_high, left_low = left
    right_high, right_low = right
    return jnp.dot(
        jnp.concatenate([left_high, left_high, left_low], axis=1),
        jnp.concatenate([right_high, right_low, right_high], axis=0),
        preferred_element_type=jnp.float32,
    )


def finish_kernel(
    packed_ref,
    state_ref,
    analysis_ref,
    transform_ref,
    moved_ref,
    matrix_ref,
    split_ref,
    product_ref,
    square_ref,
    level_ref,
    sems,
):
    half = packed_ref.shape[1]
    members = 2 * half
    square = packed_ref[:half]
    cross = packed_ref[half : 2 * half]
    diagonal = packed_ref[2 * half : 2 * half + 1]
    turned = square.T
    row = lax.broadcasted_iota(jnp.int32, (half, half), 0)
    column = lax.broadcasted_iota(jnp.int32, (half, half), 1)
    first = jnp.where(row <= column, square, turned)
    last = jnp.where(row == column, diagonal, jnp.where(row < column, turned, square))
    gram = jnp.concatenate(
        [jnp.concatenate([first, cross], axis=1), jnp.concatenate([cross.T, last], axis=1)]
    )
    row = lax.broadcasted_iota(jnp.int32, (members, members), 0)
    column = lax.broadcasted_iota(jnp.int32, (members, members), 1)
    on_diagonal = row == column
    system = gram + jnp.where(on_diagonal, members - 1.0, 0.0)
    scaler = jnp.sqrt(
        jnp.sum(jnp.sum(system * system, axis=0, keepdims=True), axis=1, keepdims=True)
    )
    root = system * (1.0 / scaler)
    block = members // BLOCKS
    spans = [slice(k * block, (k + 1) * block) for k in range(BLOCKS)]

    def store(target, rows, value):
        high, low = halves(value)
        split_ref[target, 0, rows] = high
        split_ref[target, 1, rows] = low

    def multiply(left, right, use):
        high, low = split_ref[right, 0], split_ref[right, 1]
        deep = jnp.concatenate([high, low, high], axis=0)
        for rows in spans:
            high, low = split_ref[left, 0, rows], split_ref[left, 1, rows]
            wide = jnp.concatenate([high, high, low], axis=1)
            use(rows, jnp.dot(wide, deep, preferred_element_type=jnp.float32))

    level = jnp.where(on_diagonal, 2.25, 0.0)
    level_ref[...] = level
    product_ref[...] = root
    product, square, mixed, factor, turned_product = range(5)
    inverse, inverse_next = 5, 6
    for rows in spans:
        store(product, rows, root[rows])

    def use_square(rows, value):
        square_ref[rows] = value
        store(square, rows, value)
        store(mixed, rows, 0.0625 * value - 0.5625 * product_ref[rows])

    def use_higher(target, rows, value):
        value = value + (level_ref[rows] - 2.4375 * product_ref[rows] + 1.6875 * square_ref[rows])
        store(target, rows, value)

    def use_product(rows, value):
        product_ref[rows] = value
        store(product, rows, value)

    def use_last(rows, value):
        matrix_ref[rows] = value

    for step in range(0, NS_ITERS, 2):
        multiply(product, product, use_square)
        target = inverse if step == 0 else factor
        multiply(square, mixed, functools.partial(use_higher, target))
        if step < NS_ITERS - 2:
            multiply(target, product, functools.partial(store, turned_product))
            if step > 0:
                multiply(factor, inverse, functools.partial(store, inverse_next))
                inverse, inverse_next = inverse_next, inverse
            multiply(target, turned_product, use_product)
        else:
            multiply(factor, inverse, use_last)
    inverse = matrix_ref[...]
    projected = jnp.concatenate(
        [packed_ref[2 * half + 1 : 2 * half + 2], packed_ref[2 * half + 2 : 2 * half + 3]], axis=1
    )
    once = jnp.sum(inverse * projected, axis=1, keepdims=True)
    once = jnp.sum(jnp.where(on_diagonal, once, 0.0), axis=0, keepdims=True)
    offset = jnp.sum(inverse * once, axis=1, keepdims=True) / scaler
    transform = jnp.sqrt((members - 1.0) / scaler) * inverse + offset
    matrix_ref[...] = transform
    copies = fetch((matrix_ref,), (transform_ref,), sems)
    transform = halves(transform)
    block = 128
    for start in range(0, state_ref.shape[0], block):
        rows = pl.ds(start, block)
        state = state_ref[rows]
        average = jnp.sum(state, axis=1, keepdims=True) * (1.0 / members)
        moved_ref[rows] = average + dot3(halves(state - average), transform)
        sem = sems.at[pl.ds(1 + start // block, 1)]
        copies += fetch((moved_ref.at[rows],), (analysis_ref.at[rows],), sem)
    for copy in copies:
        copy.wait()


def finish(packed, state):
    members = state.shape[1]
    square = (members, members)
    return on_core(
        finish_kernel,
        (state.shape, square),
        [pltpu.VMEM] * 2,
        [
            pltpu.VMEM(state.shape, jnp.float32),
            pltpu.VMEM(square, jnp.float32),
            pltpu.VMEM((7, 2) + square, jnp.bfloat16),
            pltpu.VMEM(square, jnp.float32),
            pltpu.VMEM(square, jnp.float32),
            pltpu.VMEM(square, jnp.float32),
            pltpu.SemaphoreType.DMA((1 + state.shape[0] // 128,)),
        ],
        pltpu.HBM,
    )(packed, state)


def reduced(packed):
    lon = lax.axis_size("lon")
    lat = lax.axis_size("lat")
    width = packed.size // lon
    pieces = lax.all_to_all(packed.reshape(lon, 1, width), "lon", 0, 0)
    piece = jnp.sum(pieces, axis=0)
    pieces = lax.all_to_all(jnp.broadcast_to(piece[None], (lat, 1, width)), "lat", 0, 0)
    piece = jnp.sum(pieces, axis=0)
    pieces = lax.all_to_all(jnp.broadcast_to(piece[None], (lon, 1, width)), "lon", 0, 0)
    return pieces.reshape(packed.shape)


def local(ensemble, bathymetry, obs_cell, obs_value, obs_weight):
    fields, lon, lat, members = ensemble.shape
    vmem = pltpu.VMEM
    total_lat = lat * lax.axis_size("lat")
    wide = lat + 2 * REACH
    rows = lax.axis_index("lat") * lat - REACH + lax.broadcasted_iota(jnp.int32, (wide, 128), 0)
    inside = ((rows >= 0) & (rows < total_lat)).astype(jnp.float32)
    turning = rotation * (2.0 * (rows.astype(jnp.float32) + 0.5) / total_lat - 1.0)
    lat_shape = (ROWS * lon + 8, members)
    lon_shape = (LON_ROWS + wide, members)
    here = lax.axis_index("lon")
    parity = (here & 1).reshape(1)
    first, second, ahead, depth = on_core(
        pack_lat_kernel,
        (lat_shape, lat_shape, (MAIN_ROWS, members), (lat, 128)),
        [pltpu.SMEM] + [pltpu.HBM] * 2,
        [
            pltpu.VMEM(ensemble.shape, jnp.float32),
            pltpu.VMEM(bathymetry.shape, jnp.int32),
            pltpu.VMEM((128, 128), jnp.float32),
            pltpu.SemaphoreType.DMA((2,)),
        ],
    )(parity, in_hbm(ensemble), in_hbm(bathymetry))
    across, within = [], []
    columns = lax.axis_size("lon")
    rows_of = lax.axis_size("lat")
    pairs = ([], [])
    for a in range(columns):
        for b in range(rows_of):
            ours = a * rows_of + b
            if b + 1 < rows_of:
                pairs[a % 2].append((ours, ours + 1))
                pairs[1 - a % 2].append((ours + 1, ours))
        (across if a % 2 else within).extend(((a, (a + 1) % columns), ((a + 1) % columns, a)))
    first = lax.ppermute(first, ("lon", "lat"), pairs[0])
    second = lax.ppermute(second, ("lon", "lat"), pairs[1])
    ahead = lax.ppermute(ahead, "lon", across)
    out_across, out_within, strip = on_core(
        pack_lon_kernel,
        ((LON_ROWS + wide - MAIN_ROWS, members), lon_shape, (wide, 128)),
        [pltpu.SMEM] + [vmem] * 4,
        [],
    )(parity, ensemble, first, second, depth)
    planes = (fields, lon, wide, members)
    across = lax.ppermute(out_across, "lon", across)
    within = lax.ppermute(out_within, "lon", within)
    inner, handed = on_core(
        inner_kernel,
        ((fields, lon - 2 * REACH, lat, members), (len(HANDED), REACH) + planes[2:]),
        [pltpu.SMEM] + [vmem] * 6,
        [pltpu.VMEM(planes, jnp.float32)] * 2
        + [pltpu.VMEM((1,) + planes[1:], jnp.float32)],
    )(parity, ensemble, first, second, strip, turning, inside)
    planes = (fields, wide, wide, members)
    forecast, packed = on_core(
        step_kernel,
        ((fields * lon * lat, members), (members + 32, members // 2)),
        [pltpu.SMEM] + [vmem] * 8 + [pltpu.HBM] * 3,
        [
            pltpu.VMEM((fields, 2 * REACH) + planes[2:], jnp.float32),
            pltpu.VMEM(planes, jnp.float32),
            pltpu.VMEM((1,) + planes[1:], jnp.float32),
            pltpu.VMEM((obs_cell.shape[2], members), jnp.float32),
            pltpu.SMEM(obs_cell.shape, jnp.int32),
        ]
        + [pltpu.VMEM(obs_value.shape, jnp.float32)] * 2
        + [pltpu.SemaphoreType.DMA((3,))],
    )(
        parity,
        ahead,
        across,
        within,
        strip,
        turning,
        inside,
        inner,
        handed,
        in_hbm(obs_cell),
        in_hbm(obs_value),
        in_hbm(obs_weight),
    )
    analysis, transform = finish(reduced(packed), forecast)
    return (analysis.reshape(ensemble.shape), transform)


def solution(mesh):
    return jax.shard_map(
        local,
        mesh=mesh,
        in_specs=(
            P(None, "lon", "lat", None),
            P("lon", "lat"),
            P("lon", "lat", None),
            P("lon", "lat", None),
            P("lon", "lat", None),
        ),
        out_specs=(P(None, "lon", "lat", None), P()),
        check_vma=False,
    )
```

```python
import functools

import jax
import jax.numpy as jnp
from jax import lax
from jax.experimental import pallas as pl
from jax.experimental.pallas import tpu as pltpu
from jax.sharding import PartitionSpec as P

STEPS = 2
NS_ITERS = 6
LEVELS = 16
REACH = 2 * STEPS
VMEM_BYTES = 24 * 1024 * 1024
TILE = 16
LAT_ROWS = (3, 3, 4)
ROWS = sum(LAT_ROWS)
MAIN_ROWS = 160
BLOCKS = 2
LON_ROWS = 192

time_step = 0.6
gravity = 1.0
rotation = 0.3


def fetch(sources, targets, sems):
    copies = [
        pltpu.make_async_copy(source, target, sems.at[k])
        for k, (source, target) in enumerate(zip(sources, targets))
    ]
    for copy in copies:
        copy.start()
    return copies


def pack_lat_kernel(
    parity_ref, ensemble_ref, bathymetry_ref, first_ref, second_ref, ahead_ref, beside_ref, depth_ref, state_ref, bottom_ref, square_ref, sems
):
    lon, lat = state_ref.shape[1], state_ref.shape[2]
    copies = fetch((bathymetry_ref, ensemble_ref), (bottom_ref, state_ref), sems)
    square_ref[...] = jnp.zeros_like(square_ref)
    depth_at = ROWS * lon
    for ref in (first_ref, second_ref):
        ref[depth_at:] = jnp.zeros((ref.shape[0] - depth_at, ref.shape[1]), jnp.float32)
    copies[0].wait()
    square_ref[:lon, :lat] = (bottom_ref[...].astype(jnp.float32) + 1.0) * (1.0 / LEVELS)
    turned = square_ref[...].T[:lat]
    depth_ref[...] = turned
    copies[1].wait()

    def pack(up_ref, down_ref):
        up_ref[depth_at : depth_at + 3, :128] = turned[lat - 3 : lat]
        down_ref[depth_at : depth_at + 3, :128] = turned[:3]
        for field, count in enumerate(LAT_ROWS):
            for x in range(lon):
                at = lon * sum(LAT_ROWS[:field]) + x * count
                plane = state_ref[field, x]
                up_ref[at : at + count] = plane[lat - count :]
                down_ref[at : at + count] = plane[:count]

    @pl.when(parity_ref[0] & 1 == 0)
    def _():
        pack(first_ref, second_ref)

    @pl.when(parity_ref[0] & 1 == 1)
    def _():
        pack(second_ref, first_ref)

    even_lon = parity_ref[0] < 2
    for field, distance, _, main, _ in lon_layout():
        down, up = state_ref[field, distance - 1], state_ref[field, lon - distance]
        ahead_ref[main : main + TILE] = jnp.where(even_lon, down, up)
        beside_ref[main : main + TILE] = jnp.where(even_lon, up, down)


def chosen(even, first_ref, second_ref, rows, lanes=slice(None)):
    return jnp.where(even, first_ref[rows, lanes], second_ref[rows, lanes])


def lat_rows(even, first_ref, second_ref, field, x, lon):
    at = lon * sum(LAT_ROWS[:field]) + x * LAT_ROWS[field]
    return chosen(even, first_ref, second_ref, slice(at, at + LAT_ROWS[field]))


def lon_layout():
    main, corner = 0, MAIN_ROWS
    for field, width, reach in ((0, 3, 3), (1, 4, 4), (2, 3, 4)):
        for distance in range(1, width + 1):
            beyond = reach - distance
            yield field, distance, beyond, main, corner
            main += TILE
            corner += 2 * beyond


def pack_lon_kernel(
    parity_ref, state_ref, first_ref, second_ref, depth_ref, across_ref, within_ref, strip_ref
):
    lon = state_ref.shape[1]
    even = parity_ref[0] & 1 == 0
    low_rows = functools.partial(lat_rows, even, second_ref, first_ref)
    high_rows = functools.partial(lat_rows, even, first_ref, second_ref)
    depth_at = ROWS * lon
    strip_ref[...] = jnp.zeros_like(strip_ref)
    depths = slice(depth_at, depth_at + 3)
    strip_ref[1:4] = chosen(even, second_ref, first_ref, depths, slice(0, 128))
    strip_ref[4:20] = depth_ref[...]
    strip_ref[20:23] = chosen(even, first_ref, second_ref, depths, slice(0, 128))
    for ref in (across_ref, within_ref):
        corners = LON_ROWS - MAIN_ROWS
        ref[corners:, 128:] = jnp.zeros((strip_ref.shape[0], 128), jnp.float32)
        ref[corners - 2 : corners] = jnp.zeros((2, ref.shape[1]), jnp.float32)
        ref[corners:, :128] = strip_ref[...]

    def pack(upward):
        for field, distance, beyond, _, corner in lon_layout():
            up, down = lon - distance, distance - 1
            for ref, x in (
                (across_ref, up if upward else down),
                (within_ref, down if upward else up),
            ):
                if beyond:
                    at = corner - MAIN_ROWS
                    low = low_rows(field, x, lon)
                    ref[at : at + beyond] = low[LAT_ROWS[field] - beyond :]
                    high = high_rows(field, x, lon)
                    ref[at + beyond : at + 2 * beyond] = high[:beyond]

    @pl.when(parity_ref[0] < 2)
    def _():
        pack(False)

    @pl.when(parity_ref[0] >= 2)
    def _():
        pack(True)


def dot3_first(left, right):
    dims = (((0,), (0,)), ((), ()))
    left_high, left_low = left
    right_high, right_low = right
    return lax.dot_general(
        jnp.concatenate([left_high, left_high, left_low]),
        jnp.concatenate([right_high, right_low, right_high]),
        dims,
        preferred_element_type=jnp.float32,
    )


def along(plane):
    return pltpu.roll(plane, plane.shape[0] - 1, 0) - pltpu.roll(plane, 1, 0)


def advance_height(source, depth, x):
    spread = source(1, x + 1) - source(1, x - 1) + along(source(2, x))
    return source(0, x) - depth(x) * spread


def advance_flow(source, height, turning, x):
    pull = 0.5 * time_step * gravity
    east = source(1, x)
    north = source(2, x)
    slope_east = height(x + 1) - height(x - 1)
    slope_north = along(height(x))
    return (
        east + (turning * north - pull * slope_east),
        north - (turning * east + pull * slope_north),
    )


def spread_out(column, shape):
    return jnp.broadcast_to(column, shape)


HANDED = ((4, 5, 18, 19),) * 3 + ((5, 6, 17, 18),) + ((6, 7, 16, 17),) * 2 + ((7, 8, 15, 16),)


def inner_kernel(
    parity_ref,
    state_ref,
    first_ref,
    second_ref,
    strip_ref,
    turning_ref,
    inside_ref,
    inner_ref,
    handed_ref,
    field_ref,
    next_ref,
    last_ref,
):
    lon = state_ref.shape[1]
    shape = field_ref.shape[2:]
    even = parity_ref[0] & 1 == 0
    low_rows = functools.partial(lat_rows, even, second_ref, first_ref)
    high_rows = functools.partial(lat_rows, even, first_ref, second_ref)
    for field, count in enumerate(LAT_ROWS):
        for x in range(lon):
            field_ref[field, x, REACH : REACH + TILE] = state_ref[field, x]
            field_ref[field, x, REACH - count : REACH] = low_rows(field, x, lon)
            field_ref[field, x, REACH + TILE : REACH + TILE + count] = high_rows(field, x, lon)
    turning = time_step * spread_out(turning_ref[:, :1], shape)
    keeper = spread_out(inside_ref[:, :1], shape)
    strip = 0.5 * time_step * strip_ref[...]
    end = lon + 2 * REACH

    def depth(x):
        return spread_out(strip[:, x - REACH : x - REACH + 1], shape)

    def source(field, x):
        return field_ref[field, x - REACH]

    def after(field, x):
        return next_ref[field, x - REACH]

    def height(x):
        return next_ref[0, x - REACH]

    def last_height(x):
        return last_ref[0, x - REACH]

    for x in range(REACH + 1, end - REACH - 1):
        next_ref[0, x - REACH] = advance_height(source, depth, x)
    for x in range(REACH + 2, end - REACH - 2):
        east, north = advance_flow(source, height, turning, x)
        next_ref[1, x - REACH] = east
        next_ref[2, x - REACH] = north * keeper
    for x in range(REACH + 3, end - REACH - 3):
        last_ref[0, x - REACH] = advance_height(after, depth, x)
    for x in range(2 * REACH, end - 2 * REACH):
        east, north = advance_flow(after, last_height, turning, x)
        for field, plane in enumerate((last_height(x), east, north)):
            inner_ref[field, x - 2 * REACH] = plane[REACH : REACH + TILE]
    kinds = (
        functools.partial(source, 0),
        functools.partial(source, 1),
        functools.partial(source, 2),
        height,
        functools.partial(after, 1),
        functools.partial(after, 2),
        last_height,
    )
    for kind, (columns, plane) in enumerate(zip(HANDED, kinds)):
        for k, x in enumerate(columns):
            handed_ref[kind, k] = plane(x)


def step_kernel(
    parity_ref,
    ahead_ref,
    beside_ref,
    across_ref,
    within_ref,
    strip_ref,
    turning_ref,
    inside_ref,
    inner_ref,
    handed_ref,
    obs_cell_ref,
    obs_value_ref,
    obs_weight_ref,
    forecast_ref,
    packed_ref,
    field_ref,
    next_ref,
    last_ref,
    picked_ref,
    cell_ref,
    value_ref,
    weight_ref,
    sems,
):
    copies = fetch(
        (obs_cell_ref, obs_value_ref, obs_weight_ref), (cell_ref, value_ref, weight_ref), sems
    )
    shape = field_ref.shape[2:]
    members = shape[1]
    end = next_ref.shape[1]
    lon = end - 2 * REACH
    even_lon = parity_ref[0] < 2

    def taken(rows, lanes=slice(None)):
        start, stop = rows
        if stop <= MAIN_ROWS:
            across, within = ahead_ref[start:stop, lanes], beside_ref[start:stop, lanes]
        else:
            rows = slice(start - MAIN_ROWS, stop - MAIN_ROWS)
            across, within = across_ref[rows, lanes], within_ref[rows, lanes]
        return jnp.where(even_lon, across, within), jnp.where(even_lon, within, across)

    for field, distance, beyond, main, corner in lon_layout():
        parts = [((main, main + TILE), REACH, TILE)]
        if beyond:
            parts.append(((corner, corner + beyond), REACH - beyond, beyond))
            parts.append(((corner + beyond, corner + 2 * beyond), REACH + TILE, beyond))
        for rows, at, count in parts:
            west, east = taken(rows)
            field_ref[field, REACH - distance, at : at + count] = west
            field_ref[field, REACH - 1 + distance, at : at + count] = east
    west_strip, east_strip = taken((LON_ROWS, MAIN_ROWS + within_ref.shape[0]), slice(0, 128))
    turning = time_step * spread_out(turning_ref[:, :1], shape)
    keeper = spread_out(inside_ref[:, :1], shape)
    strips = [0.5 * time_step * strip for strip in (west_strip, strip_ref[...], east_strip)]

    def depth(x):
        if x < REACH:
            column = strips[0][:, lon - REACH + x : lon - REACH + x + 1]
        elif x < REACH + lon:
            column = strips[1][:, x - REACH : x - REACH + 1]
        else:
            column = strips[2][:, x - REACH - lon : x - REACH - lon + 1]
        return spread_out(column, shape)

    def source(field, x):
        if x < REACH:
            return field_ref[field, x]
        if x >= REACH + lon:
            return field_ref[field, x - lon]
        return handed_ref[field, HANDED[field].index(x)]

    def after(field, x):
        if x in HANDED[3 + field]:
            return handed_ref[3 + field, HANDED[3 + field].index(x)]
        return next_ref[field, x]

    def height(x):
        return after(0, x)

    def last_height(x):
        if x in HANDED[6]:
            return handed_ref[6, HANDED[6].index(x)]
        return last_ref[0, x]

    def edges(margin):
        return (*range(margin, margin + REACH), *range(end - margin - REACH, end - margin))

    for x in edges(1):
        next_ref[0, x] = advance_height(source, depth, x)
    for x in edges(2):
        east_flow, north_flow = advance_flow(source, height, turning, x)
        next_ref[1, x] = east_flow
        next_ref[2, x] = north_flow * keeper
    for x in edges(3):
        last_ref[0, x] = advance_height(after, depth, x)
    for x in edges(REACH):
        east_flow, north_flow = advance_flow(after, last_height, turning, x)
        for field, plane in enumerate((last_height(x), east_flow, north_flow)):
            at = (field * lon + x - REACH) * TILE
            forecast_ref[at : at + TILE] = plane[REACH : REACH + TILE]
    for field in range(len(LAT_ROWS)):
        for x in range(REACH, lon - REACH):
            at = (field * lon + x) * TILE
            forecast_ref[at : at + TILE] = inner_ref[field, x - REACH]

    for copy in copies:
        copy.wait()
    count = picked_ref.shape[0]
    for k in range(count):
        picked_ref[k : k + 1] = forecast_ref[pl.ds(cell_ref[0, 0, k], 1)]
    picked = picked_ref[...]
    ymean = jnp.sum(picked, axis=1, keepdims=True) * (1.0 / members)
    half = members // 2
    row = lax.broadcasted_iota(jnp.int32, (half, half), 0)
    line = lax.broadcasted_iota(jnp.int32, (half, half), 1)
    on_diagonal = row == line
    weight = jnp.sum(jnp.where(on_diagonal, weight_ref[0], 0.0), axis=1, keepdims=True)
    value = jnp.sum(jnp.where(on_diagonal, value_ref[0], 0.0), axis=1, keepdims=True)
    anomaly = (picked - ymean) * weight
    innovation = (value - ymean) * weight
    projected = jnp.sum(innovation * anomaly, axis=0, keepdims=True)
    left_high, left_low = halves(anomaly[:, :half])
    right_high, right_low = halves(anomaly[:, half:])
    first = dot3_first((left_high, left_low), (left_high, left_low))
    cross = dot3_first((left_high, left_low), (right_high, right_low))
    final = dot3_first((right_high, right_low), (right_high, right_low))
    packed_ref[:half] = jnp.where(row <= line, first, final)
    packed_ref[half : 2 * half] = cross
    packed_ref[2 * half :] = jnp.zeros((packed_ref.shape[0] - 2 * half, half), jnp.float32)
    packed_ref[2 * half : 2 * half + 1] = jnp.sum(
        jnp.where(on_diagonal, final, 0.0), axis=0, keepdims=True
    )
    packed_ref[2 * half + 1 : 2 * half + 2] = projected[:, :half]
    packed_ref[2 * half + 2 : 2 * half + 3] = projected[:, half:]


def in_hbm(value):
    return pltpu.with_memory_space_constraint(value, pltpu.HBM)


def on_core(kernel, outs, spaces, scratch, out_space=pltpu.VMEM):
    return pl.pallas_call(
        kernel,
        out_shape=tuple(jax.ShapeDtypeStruct(shape, jnp.float32) for shape in outs),
        in_specs=[pl.BlockSpec(memory_space=space) for space in spaces],
        out_specs=tuple(pl.BlockSpec(memory_space=out_space) for _ in outs),
        scratch_shapes=scratch,
        compiler_params=pltpu.CompilerParams(vmem_limit_bytes=VMEM_BYTES),
    )


def halves(value):
    high = value.astype(jnp.bfloat16)
    return high, (value - high.astype(jnp.float32)).astype(jnp.bfloat16)


def dot3(left, right):
    left_high, left_low = left
    right_high, right_low = right
    return jnp.dot(
        jnp.concatenate([left_high, left_high, left_low], axis=1),
        jnp.concatenate([right_high, right_low, right_high], axis=0),
        preferred_element_type=jnp.float32,
    )


def finish_kernel(
    packed_ref,
    state_ref,
    analysis_ref,
    transform_ref,
    moved_ref,
    matrix_ref,
    split_ref,
    product_ref,
    square_ref,
    level_ref,
    sems,
):
    half = packed_ref.shape[1]
    members = 2 * half
    square = packed_ref[:half]
    cross = packed_ref[half : 2 * half]
    diagonal = packed_ref[2 * half : 2 * half + 1]
    turned = square.T
    row = lax.broadcasted_iota(jnp.int32, (half, half), 0)
    column = lax.broadcasted_iota(jnp.int32, (half, half), 1)
    first = jnp.where(row <= column, square, turned)
    last = jnp.where(row == column, diagonal, jnp.where(row < column, turned, square))
    gram = jnp.concatenate(
        [jnp.concatenate([first, cross], axis=1), jnp.concatenate([cross.T, last], axis=1)]
    )
    row = lax.broadcasted_iota(jnp.int32, (members, members), 0)
    column = lax.broadcasted_iota(jnp.int32, (members, members), 1)
    on_diagonal = row == column
    system = gram + jnp.where(on_diagonal, members - 1.0, 0.0)
    scaler = jnp.sqrt(
        jnp.sum(jnp.sum(system * system, axis=0, keepdims=True), axis=1, keepdims=True)
    )
    root = system * (1.0 / scaler)
    block = members // BLOCKS
    spans = [slice(k * block, (k + 1) * block) for k in range(BLOCKS)]

    def store(target, rows, value):
        high, low = halves(value)
        split_ref[target, 0, rows] = high
        split_ref[target, 1, rows] = low

    def multiply(left, right, use):
        high, low = split_ref[right, 0], split_ref[right, 1]
        deep = jnp.concatenate([high, low, high], axis=0)
        for rows in spans:
            high, low = split_ref[left, 0, rows], split_ref[left, 1, rows]
            wide = jnp.concatenate([high, high, low], axis=1)
            use(rows, jnp.dot(wide, deep, preferred_element_type=jnp.float32))

    level = jnp.where(on_diagonal, 2.25, 0.0)
    level_ref[...] = level
    product_ref[...] = root
    product, square, mixed, factor, turned_product = range(5)
    inverse, inverse_next = 5, 6
    for rows in spans:
        store(product, rows, root[rows])

    def use_square(rows, value):
        square_ref[rows] = value
        store(square, rows, value)
        store(mixed, rows, 0.0625 * value - 0.5625 * product_ref[rows])

    def use_higher(target, rows, value):
        value = value + (level_ref[rows] - 2.4375 * product_ref[rows] + 1.6875 * square_ref[rows])
        store(target, rows, value)

    def use_product(rows, value):
        product_ref[rows] = value
        store(product, rows, value)

    def use_last(rows, value):
        matrix_ref[rows] = value

    for step in range(0, NS_ITERS, 2):
        multiply(product, product, use_square)
        target = inverse if step == 0 else factor
        multiply(square, mixed, functools.partial(use_higher, target))
        if step < NS_ITERS - 2:
            multiply(target, product, functools.partial(store, turned_product))
            if step > 0:
                multiply(factor, inverse, functools.partial(store, inverse_next))
                inverse, inverse_next = inverse_next, inverse
            multiply(target, turned_product, use_product)
        else:
            multiply(factor, inverse, use_last)
    inverse = matrix_ref[...]
    projected = jnp.concatenate(
        [packed_ref[2 * half + 1 : 2 * half + 2], packed_ref[2 * half + 2 : 2 * half + 3]], axis=1
    )
    once = jnp.sum(inverse * projected, axis=1, keepdims=True)
    once = jnp.sum(jnp.where(on_diagonal, once, 0.0), axis=0, keepdims=True)
    offset = jnp.sum(inverse * once, axis=1, keepdims=True) / scaler
    transform = jnp.sqrt((members - 1.0) / scaler) * inverse + offset
    matrix_ref[...] = transform
    copies = fetch((matrix_ref,), (transform_ref,), sems)
    transform = halves(transform)
    block = 128
    for start in range(0, state_ref.shape[0], block):
        rows = pl.ds(start, block)
        state = state_ref[rows]
        average = jnp.sum(state, axis=1, keepdims=True) * (1.0 / members)
        moved_ref[rows] = average + dot3(halves(state - average), transform)
        sem = sems.at[pl.ds(1 + start // block, 1)]
        copies += fetch((moved_ref.at[rows],), (analysis_ref.at[rows],), sem)
    for copy in copies:
        copy.wait()


def finish(packed, state):
    members = state.shape[1]
    square = (members, members)
    return on_core(
        finish_kernel,
        (state.shape, square),
        [pltpu.VMEM] * 2,
        [
            pltpu.VMEM(state.shape, jnp.float32),
            pltpu.VMEM(square, jnp.float32),
            pltpu.VMEM((7, 2) + square, jnp.bfloat16),
            pltpu.VMEM(square, jnp.float32),
            pltpu.VMEM(square, jnp.float32),
            pltpu.VMEM(square, jnp.float32),
            pltpu.SemaphoreType.DMA((1 + state.shape[0] // 128,)),
        ],
        pltpu.HBM,
    )(packed, state)


def reduced(packed):
    lon = lax.axis_size("lon")
    lat = lax.axis_size("lat")
    width = packed.size // lon
    pieces = lax.all_to_all(packed.reshape(lon, 1, width), "lon", 0, 0)
    piece = jnp.sum(pieces, axis=0)
    pieces = lax.all_to_all(jnp.broadcast_to(piece[None], (lat, 1, width)), "lat", 0, 0)
    piece = jnp.sum(pieces, axis=0)
    pieces = lax.all_to_all(jnp.broadcast_to(piece[None], (lon, 1, width)), "lon", 0, 0)
    return pieces.reshape(packed.shape)


def local(ensemble, bathymetry, obs_cell, obs_value, obs_weight):
    fields, lon, lat, members = ensemble.shape
    vmem = pltpu.VMEM
    total_lat = lat * lax.axis_size("lat")
    wide = lat + 2 * REACH
    rows = lax.axis_index("lat") * lat - REACH + lax.broadcasted_iota(jnp.int32, (wide, 128), 0)
    inside = ((rows >= 0) & (rows < total_lat)).astype(jnp.float32)
    turning = rotation * (2.0 * (rows.astype(jnp.float32) + 0.5) / total_lat - 1.0)
    lat_shape = (ROWS * lon + 8, members)
    main_shape = (MAIN_ROWS, members)
    lon_shape = (LON_ROWS - MAIN_ROWS + wide, members)
    here = lax.axis_index("lon")
    parity = ((here + lax.axis_index("lat")) & 1) + 2 * (here & 1)
    parity = parity.reshape(1)
    first, second, ahead, beside, depth = on_core(
        pack_lat_kernel,
        (lat_shape, lat_shape, main_shape, main_shape, (lat, 128)),
        [pltpu.SMEM] + [pltpu.HBM] * 2,
        [
            pltpu.VMEM(ensemble.shape, jnp.float32),
            pltpu.VMEM(bathymetry.shape, jnp.int32),
            pltpu.VMEM((128, 128), jnp.float32),
            pltpu.SemaphoreType.DMA((2,)),
        ],
    )(parity, in_hbm(ensemble), in_hbm(bathymetry))
    across, within = [], []
    columns = lax.axis_size("lon")
    rows_of = lax.axis_size("lat")
    pairs = ([], [])
    for a in range(columns):
        for b in range(rows_of):
            ours = a * rows_of + b
            if b + 1 < rows_of:
                pairs[(a + b) % 2].extend(((ours, ours + 1), (ours + 1, ours)))
        (across if a % 2 else within).extend(((a, (a + 1) % columns), ((a + 1) % columns, a)))
    first = lax.ppermute(first, ("lon", "lat"), pairs[0])
    second = lax.ppermute(second, ("lon", "lat"), pairs[1])
    ahead = lax.ppermute(ahead, "lon", across)
    beside = lax.ppermute(beside, "lon", within)
    out_across, out_within, strip = on_core(
        pack_lon_kernel,
        (lon_shape, lon_shape, (wide, 128)),
        [pltpu.SMEM] + [vmem] * 4,
        [],
    )(parity, ensemble, first, second, depth)
    planes = (fields, lon, wide, members)
    across = lax.ppermute(out_across, "lon", across)
    within = lax.ppermute(out_within, "lon", within)
    inner, handed = on_core(
        inner_kernel,
        ((fields, lon - 2 * REACH, lat, members), (len(HANDED), REACH) + planes[2:]),
        [pltpu.SMEM] + [vmem] * 6,
        [pltpu.VMEM(planes, jnp.float32)] * 2
        + [pltpu.VMEM((1,) + planes[1:], jnp.float32)],
    )(parity, ensemble, first, second, strip, turning, inside)
    planes = (fields, wide, wide, members)
    forecast, packed = on_core(
        step_kernel,
        ((fields * lon * lat, members), (members + 32, members // 2)),
        [pltpu.SMEM] + [vmem] * 9 + [pltpu.HBM] * 3,
        [
            pltpu.VMEM((fields, 2 * REACH) + planes[2:], jnp.float32),
            pltpu.VMEM(planes, jnp.float32),
            pltpu.VMEM((1,) + planes[1:], jnp.float32),
            pltpu.VMEM((obs_cell.shape[2], members), jnp.float32),
            pltpu.SMEM(obs_cell.shape, jnp.int32),
        ]
        + [pltpu.VMEM(obs_value.shape, jnp.float32)] * 2
        + [pltpu.SemaphoreType.DMA((3,))],
    )(
        parity,
        ahead,
        beside,
        across,
        within,
        strip,
        turning,
        inside,
        inner,
        handed,
        in_hbm(obs_cell),
        in_hbm(obs_value),
        in_hbm(obs_weight),
    )
    analysis, transform = finish(reduced(packed), forecast)
    return (analysis.reshape(ensemble.shape), transform)


def solution(mesh):
    return jax.shard_map(
        local,
        mesh=mesh,
        in_specs=(
            P(None, "lon", "lat", None),
            P("lon", "lat"),
            P("lon", "lat", None),
            P("lon", "lat", None),
            P("lon", "lat", None),
        ),
        out_specs=(P(None, "lon", "lat", None), P()),
        check_vma=False,
    )
```

```python
import functools

import jax
import jax.numpy as jnp
from jax import lax
from jax.experimental import pallas as pl
from jax.experimental.pallas import tpu as pltpu
from jax.sharding import PartitionSpec as P

STEPS = 2
NS_ITERS = 6
LEVELS = 16
REACH = 2 * STEPS
VMEM_BYTES = 24 * 1024 * 1024
TILE = 16
LAT_ROWS = (3, 3, 4)
ROWS = sum(LAT_ROWS)
MAIN_ROWS = 160
BLOCKS = 2
LON_ROWS = 192

time_step = 0.6
gravity = 1.0
rotation = 0.3


def fetch(sources, targets, sems):
    copies = [
        pltpu.make_async_copy(source, target, sems.at[k])
        for k, (source, target) in enumerate(zip(sources, targets))
    ]
    for copy in copies:
        copy.start()
    return copies


def pack_lat_kernel(
    parity_ref, ensemble_ref, bathymetry_ref, first_ref, second_ref, ahead_ref, depth_ref, state_ref, bottom_ref, square_ref, sems
):
    lon, lat = state_ref.shape[1], state_ref.shape[2]
    copies = fetch((bathymetry_ref, ensemble_ref), (bottom_ref, state_ref), sems)
    square_ref[...] = jnp.zeros_like(square_ref)
    depth_at = ROWS * lon
    for ref in (first_ref, second_ref):
        ref[depth_at:] = jnp.zeros((ref.shape[0] - depth_at, ref.shape[1]), jnp.float32)
    copies[0].wait()
    square_ref[:lon, :lat] = (bottom_ref[...].astype(jnp.float32) + 1.0) * (1.0 / LEVELS)
    turned = square_ref[...].T[:lat]
    depth_ref[...] = turned
    copies[1].wait()

    def pack(up_ref, down_ref):
        up_ref[depth_at : depth_at + 3, :128] = turned[lat - 3 : lat]
        down_ref[depth_at : depth_at + 3, :128] = turned[:3]
        for field, count in enumerate(LAT_ROWS):
            for x in range(lon):
                at = lon * sum(LAT_ROWS[:field]) + x * count
                plane = state_ref[field, x]
                up_ref[at : at + count] = plane[lat - count :]
                down_ref[at : at + count] = plane[:count]

    @pl.when(parity_ref[0] & 1 == 0)
    def _():
        pack(first_ref, second_ref)

    @pl.when(parity_ref[0] & 1 == 1)
    def _():
        pack(second_ref, first_ref)

    even_lon = parity_ref[0] < 2
    for field, distance, _, main, _ in lon_layout():
        down, up = state_ref[field, distance - 1], state_ref[field, lon - distance]
        ahead_ref[main : main + TILE] = jnp.where(even_lon, down, up)


def chosen(even, first_ref, second_ref, rows, lanes=slice(None)):
    return jnp.where(even, first_ref[rows, lanes], second_ref[rows, lanes])


def lat_rows(even, first_ref, second_ref, field, x, lon):
    at = lon * sum(LAT_ROWS[:field]) + x * LAT_ROWS[field]
    return chosen(even, first_ref, second_ref, slice(at, at + LAT_ROWS[field]))


def lon_layout():
    main, corner = 0, MAIN_ROWS
    for field, width, reach in ((0, 3, 3), (1, 4, 4), (2, 3, 4)):
        for distance in range(1, width + 1):
            beyond = reach - distance
            yield field, distance, beyond, main, corner
            main += TILE
            corner += 2 * beyond


def pack_lon_kernel(
    parity_ref, state_ref, first_ref, second_ref, depth_ref, across_ref, within_ref, strip_ref
):
    lon = state_ref.shape[1]
    even = parity_ref[0] & 1 == 0
    low_rows = functools.partial(lat_rows, even, second_ref, first_ref)
    high_rows = functools.partial(lat_rows, even, first_ref, second_ref)
    depth_at = ROWS * lon
    strip_ref[...] = jnp.zeros_like(strip_ref)
    depths = slice(depth_at, depth_at + 3)
    strip_ref[1:4] = chosen(even, second_ref, first_ref, depths, slice(0, 128))
    strip_ref[4:20] = depth_ref[...]
    strip_ref[20:23] = chosen(even, first_ref, second_ref, depths, slice(0, 128))
    for ref, skipped in ((across_ref, MAIN_ROWS), (within_ref, 0)):
        depths = slice(LON_ROWS - skipped, None)
        ref[depths, 128:] = jnp.zeros((strip_ref.shape[0], 128), jnp.float32)
        ref[LON_ROWS - 2 - skipped : LON_ROWS - skipped] = jnp.zeros((2, ref.shape[1]), jnp.float32)
        ref[depths, :128] = strip_ref[...]

    def pack(upward):
        for field, distance, beyond, main, corner in lon_layout():
            up, down = lon - distance, distance - 1
            for ref, x, skipped in (
                (across_ref, up if upward else down, MAIN_ROWS),
                (within_ref, down if upward else up, 0),
            ):
                if beyond:
                    at = corner - skipped
                    low = low_rows(field, x, lon)
                    ref[at : at + beyond] = low[LAT_ROWS[field] - beyond :]
                    high = high_rows(field, x, lon)
                    ref[at + beyond : at + 2 * beyond] = high[:beyond]
                if not skipped:
                    ref[main : main + TILE] = state_ref[field, x]

    @pl.when(parity_ref[0] < 2)
    def _():
        pack(False)

    @pl.when(parity_ref[0] >= 2)
    def _():
        pack(True)


def dot3_first(left, right):
    dims = (((0,), (0,)), ((), ()))
    left_high, left_low = left
    right_high, right_low = right
    return lax.dot_general(
        jnp.concatenate([left_high, left_high, left_low]),
        jnp.concatenate([right_high, right_low, right_high]),
        dims,
        preferred_element_type=jnp.float32,
    )


def along(plane):
    return pltpu.roll(plane, plane.shape[0] - 1, 0) - pltpu.roll(plane, 1, 0)


def advance_height(source, depth, x):
    spread = source(1, x + 1) - source(1, x - 1) + along(source(2, x))
    return source(0, x) - depth(x) * spread


def advance_flow(source, height, turning, x):
    pull = 0.5 * time_step * gravity
    east = source(1, x)
    north = source(2, x)
    slope_east = height(x + 1) - height(x - 1)
    slope_north = along(height(x))
    return (
        east + (turning * north - pull * slope_east),
        north - (turning * east + pull * slope_north),
    )


def spread_out(column, shape):
    return jnp.broadcast_to(column, shape)


HANDED = ((4, 5, 18, 19),) * 3 + ((5, 6, 17, 18),) + ((6, 7, 16, 17),) * 2 + ((7, 8, 15, 16),)


def inner_kernel(
    parity_ref,
    state_ref,
    first_ref,
    second_ref,
    strip_ref,
    turning_ref,
    inside_ref,
    inner_ref,
    handed_ref,
    field_ref,
    next_ref,
    last_ref,
):
    lon = state_ref.shape[1]
    shape = field_ref.shape[2:]
    even = parity_ref[0] & 1 == 0
    low_rows = functools.partial(lat_rows, even, second_ref, first_ref)
    high_rows = functools.partial(lat_rows, even, first_ref, second_ref)
    for field, count in enumerate(LAT_ROWS):
        for x in range(lon):
            field_ref[field, x, REACH : REACH + TILE] = state_ref[field, x]
            field_ref[field, x, REACH - count : REACH] = low_rows(field, x, lon)
            field_ref[field, x, REACH + TILE : REACH + TILE + count] = high_rows(field, x, lon)
    turning = time_step * spread_out(turning_ref[:, :1], shape)
    keeper = spread_out(inside_ref[:, :1], shape)
    strip = 0.5 * time_step * strip_ref[...]
    end = lon + 2 * REACH

    def depth(x):
        return spread_out(strip[:, x - REACH : x - REACH + 1], shape)

    def source(field, x):
        return field_ref[field, x - REACH]

    def after(field, x):
        return next_ref[field, x - REACH]

    def height(x):
        return next_ref[0, x - REACH]

    def last_height(x):
        return last_ref[0, x - REACH]

    for x in range(REACH + 1, end - REACH - 1):
        next_ref[0, x - REACH] = advance_height(source, depth, x)
    for x in range(REACH + 2, end - REACH - 2):
        east, north = advance_flow(source, height, turning, x)
        next_ref[1, x - REACH] = east
        next_ref[2, x - REACH] = north * keeper
    for x in range(REACH + 3, end - REACH - 3):
        last_ref[0, x - REACH] = advance_height(after, depth, x)
    for x in range(2 * REACH, end - 2 * REACH):
        east, north = advance_flow(after, last_height, turning, x)
        for field, plane in enumerate((last_height(x), east, north)):
            inner_ref[field, x - 2 * REACH] = plane[REACH : REACH + TILE]
    kinds = (
        functools.partial(source, 0),
        functools.partial(source, 1),
        functools.partial(source, 2),
        height,
        functools.partial(after, 1),
        functools.partial(after, 2),
        last_height,
    )
    for kind, (columns, plane) in enumerate(zip(HANDED, kinds)):
        for k, x in enumerate(columns):
            handed_ref[kind, k] = plane(x)


def step_kernel(
    parity_ref,
    ahead_ref,
    across_ref,
    within_ref,
    strip_ref,
    turning_ref,
    inside_ref,
    inner_ref,
    handed_ref,
    obs_cell_ref,
    obs_value_ref,
    obs_weight_ref,
    forecast_ref,
    packed_ref,
    field_ref,
    next_ref,
    last_ref,
    picked_ref,
    left_ref,
    right_ref,
    cell_ref,
    value_ref,
    weight_ref,
    sems,
):
    copies = fetch(
        (obs_cell_ref, obs_value_ref, obs_weight_ref), (cell_ref, value_ref, weight_ref), sems
    )
    shape = field_ref.shape[2:]
    members = shape[1]
    end = next_ref.shape[1]
    lon = end - 2 * REACH
    even_lon = parity_ref[0] < 2

    def taken(rows, lanes=slice(None)):
        start, stop = rows
        if stop <= MAIN_ROWS:
            across = ahead_ref[start:stop, lanes]
        else:
            across = across_ref[start - MAIN_ROWS : stop - MAIN_ROWS, lanes]
        within = within_ref[start:stop, lanes]
        return jnp.where(even_lon, across, within), jnp.where(even_lon, within, across)

    for field, distance, beyond, main, corner in lon_layout():
        parts = [((main, main + TILE), REACH, TILE)]
        if beyond:
            parts.append(((corner, corner + beyond), REACH - beyond, beyond))
            parts.append(((corner + beyond, corner + 2 * beyond), REACH + TILE, beyond))
        for rows, at, count in parts:
            west, east = taken(rows)
            field_ref[field, REACH - distance, at : at + count] = west
            field_ref[field, REACH - 1 + distance, at : at + count] = east
    west_strip, east_strip = taken((LON_ROWS, within_ref.shape[0]), slice(0, 128))
    turning = time_step * spread_out(turning_ref[:, :1], shape)
    keeper = spread_out(inside_ref[:, :1], shape)
    strips = [0.5 * time_step * strip for strip in (west_strip, strip_ref[...], east_strip)]

    def depth(x):
        if x < REACH:
            column = strips[0][:, lon - REACH + x : lon - REACH + x + 1]
        elif x < REACH + lon:
            column = strips[1][:, x - REACH : x - REACH + 1]
        else:
            column = strips[2][:, x - REACH - lon : x - REACH - lon + 1]
        return spread_out(column, shape)

    def source(field, x):
        if x < REACH:
            return field_ref[field, x]
        if x >= REACH + lon:
            return field_ref[field, x - lon]
        return handed_ref[field, HANDED[field].index(x)]

    def after(field, x):
        if x in HANDED[3 + field]:
            return handed_ref[3 + field, HANDED[3 + field].index(x)]
        return next_ref[field, x]

    def height(x):
        return after(0, x)

    def last_height(x):
        if x in HANDED[6]:
            return handed_ref[6, HANDED[6].index(x)]
        return last_ref[0, x]

    def edges(margin):
        return (*range(margin, margin + REACH), *range(end - margin - REACH, end - margin))

    for x in edges(1):
        next_ref[0, x] = advance_height(source, depth, x)
    for x in edges(2):
        east_flow, north_flow = advance_flow(source, height, turning, x)
        next_ref[1, x] = east_flow
        next_ref[2, x] = north_flow * keeper
    for x in edges(3):
        last_ref[0, x] = advance_height(after, depth, x)
    for x in edges(REACH):
        east_flow, north_flow = advance_flow(after, last_height, turning, x)
        for field, plane in enumerate((last_height(x), east_flow, north_flow)):
            at = (field * lon + x - REACH) * TILE
            tile = plane[REACH : REACH + TILE]
            forecast_ref[at : at + TILE] = tile
            left_ref[at : at + TILE], right_ref[at : at + TILE] = tile[:, :128], tile[:, 128:]
    for field in range(len(LAT_ROWS)):
        for x in range(REACH, lon - REACH):
            at = (field * lon + x) * TILE
            tile = inner_ref[field, x - REACH]
            forecast_ref[at : at + TILE] = tile
            left_ref[at : at + TILE], right_ref[at : at + TILE] = tile[:, :128], tile[:, 128:]

    for copy in copies:
        copy.wait()
    count = picked_ref.shape[0]
    for k in range(count):
        cell = cell_ref[0, 0, k]
        picked_ref[k : k + 1, :128] = left_ref[pl.ds(cell, 1)]
        picked_ref[k : k + 1, 128:] = right_ref[pl.ds(cell, 1)]
    picked = picked_ref[...]
    ymean = jnp.sum(picked, axis=1, keepdims=True) * (1.0 / members)
    half = members // 2
    row = lax.broadcasted_iota(jnp.int32, (half, half), 0)
    line = lax.broadcasted_iota(jnp.int32, (half, half), 1)
    on_diagonal = row == line
    weight = jnp.sum(jnp.where(on_diagonal, weight_ref[0], 0.0), axis=1, keepdims=True)
    value = jnp.sum(jnp.where(on_diagonal, value_ref[0], 0.0), axis=1, keepdims=True)
    anomaly = (picked - ymean) * weight
    innovation = (value - ymean) * weight
    projected = jnp.sum(innovation * anomaly, axis=0, keepdims=True)
    left_high, left_low = halves(anomaly[:, :half])
    right_high, right_low = halves(anomaly[:, half:])
    first = dot3_first((left_high, left_low), (left_high, left_low))
    cross = dot3_first((left_high, left_low), (right_high, right_low))
    final = dot3_first((right_high, right_low), (right_high, right_low))
    packed_ref[:half] = jnp.where(row <= line, first, final)
    packed_ref[half : 2 * half] = cross
    packed_ref[2 * half :] = jnp.zeros((packed_ref.shape[0] - 2 * half, half), jnp.float32)
    packed_ref[2 * half : 2 * half + 1] = jnp.sum(
        jnp.where(on_diagonal, final, 0.0), axis=0, keepdims=True
    )
    packed_ref[2 * half + 1 : 2 * half + 2] = projected[:, :half]
    packed_ref[2 * half + 2 : 2 * half + 3] = projected[:, half:]


def in_hbm(value):
    return pltpu.with_memory_space_constraint(value, pltpu.HBM)


def on_core(kernel, outs, spaces, scratch, out_space=pltpu.VMEM):
    return pl.pallas_call(
        kernel,
        out_shape=tuple(jax.ShapeDtypeStruct(shape, jnp.float32) for shape in outs),
        in_specs=[pl.BlockSpec(memory_space=space) for space in spaces],
        out_specs=tuple(pl.BlockSpec(memory_space=out_space) for _ in outs),
        scratch_shapes=scratch,
        compiler_params=pltpu.CompilerParams(vmem_limit_bytes=VMEM_BYTES),
    )


def halves(value):
    high = value.astype(jnp.bfloat16)
    return high, (value - high.astype(jnp.float32)).astype(jnp.bfloat16)


def dot3(left, right):
    left_high, left_low = left
    right_high, right_low = right
    return jnp.dot(
        jnp.concatenate([left_high, left_high, left_low], axis=1),
        jnp.concatenate([right_high, right_low, right_high], axis=0),
        preferred_element_type=jnp.float32,
    )


def finish_kernel(
    packed_ref,
    state_ref,
    analysis_ref,
    transform_ref,
    moved_ref,
    matrix_ref,
    split_ref,
    product_ref,
    square_ref,
    level_ref,
    sems,
):
    half = packed_ref.shape[1]
    members = 2 * half
    square = packed_ref[:half]
    cross = packed_ref[half : 2 * half]
    diagonal = packed_ref[2 * half : 2 * half + 1]
    turned = square.T
    row = lax.broadcasted_iota(jnp.int32, (half, half), 0)
    column = lax.broadcasted_iota(jnp.int32, (half, half), 1)
    first = jnp.where(row <= column, square, turned)
    last = jnp.where(row == column, diagonal, jnp.where(row < column, turned, square))
    gram = jnp.concatenate(
        [jnp.concatenate([first, cross], axis=1), jnp.concatenate([cross.T, last], axis=1)]
    )
    row = lax.broadcasted_iota(jnp.int32, (members, members), 0)
    column = lax.broadcasted_iota(jnp.int32, (members, members), 1)
    on_diagonal = row == column
    system = gram + jnp.where(on_diagonal, members - 1.0, 0.0)
    scaler = jnp.sqrt(
        jnp.sum(jnp.sum(system * system, axis=0, keepdims=True), axis=1, keepdims=True)
    )
    root = system * (1.0 / scaler)
    block = members // BLOCKS
    spans = [slice(k * block, (k + 1) * block) for k in range(BLOCKS)]

    def store(target, rows, value):
        high, low = halves(value)
        split_ref[target, 0, rows] = high
        split_ref[target, 1, rows] = low

    def multiply(left, right, use):
        high, low = split_ref[right, 0], split_ref[right, 1]
        deep = jnp.concatenate([high, low, high], axis=0)
        for rows in spans:
            high, low = split_ref[left, 0, rows], split_ref[left, 1, rows]
            wide = jnp.concatenate([high, high, low], axis=1)
            use(rows, jnp.dot(wide, deep, preferred_element_type=jnp.float32))

    level = jnp.where(on_diagonal, 2.25, 0.0)
    level_ref[...] = level
    product_ref[...] = root
    product, square, mixed, factor, turned_product = range(5)
    inverse, inverse_next = 5, 6
    for rows in spans:
        store(product, rows, root[rows])

    def use_square(rows, value):
        square_ref[rows] = value
        store(square, rows, value)
        store(mixed, rows, 0.0625 * value - 0.5625 * product_ref[rows])

    def use_higher(target, rows, value):
        value = value + (level_ref[rows] - 2.4375 * product_ref[rows] + 1.6875 * square_ref[rows])
        store(target, rows, value)

    def use_product(rows, value):
        product_ref[rows] = value
        store(product, rows, value)

    def use_last(rows, value):
        matrix_ref[rows] = value

    for step in range(0, NS_ITERS, 2):
        multiply(product, product, use_square)
        target = inverse if step == 0 else factor
        multiply(square, mixed, functools.partial(use_higher, target))
        if step < NS_ITERS - 2:
            multiply(target, product, functools.partial(store, turned_product))
            if step > 0:
                multiply(factor, inverse, functools.partial(store, inverse_next))
                inverse, inverse_next = inverse_next, inverse
            multiply(target, turned_product, use_product)
        else:
            multiply(factor, inverse, use_last)
    inverse = matrix_ref[...]
    projected = jnp.concatenate(
        [packed_ref[2 * half + 1 : 2 * half + 2], packed_ref[2 * half + 2 : 2 * half + 3]], axis=1
    )
    once = jnp.sum(inverse * projected, axis=1, keepdims=True)
    once = jnp.sum(jnp.where(on_diagonal, once, 0.0), axis=0, keepdims=True)
    offset = jnp.sum(inverse * once, axis=1, keepdims=True) / scaler
    transform = jnp.sqrt((members - 1.0) / scaler) * inverse + offset
    matrix_ref[...] = transform
    copies = fetch((matrix_ref,), (transform_ref,), sems)
    transform = halves(transform)
    block = 128
    for start in range(0, state_ref.shape[0], block):
        rows = pl.ds(start, block)
        state = state_ref[rows]
        average = jnp.sum(state, axis=1, keepdims=True) * (1.0 / members)
        moved_ref[rows] = average + dot3(halves(state - average), transform)
        sem = sems.at[pl.ds(1 + start // block, 1)]
        copies += fetch((moved_ref.at[rows],), (analysis_ref.at[rows],), sem)
    for copy in copies:
        copy.wait()


def finish(packed, state):
    members = state.shape[1]
    square = (members, members)
    return on_core(
        finish_kernel,
        (state.shape, square),
        [pltpu.VMEM] * 2,
        [
            pltpu.VMEM(state.shape, jnp.float32),
            pltpu.VMEM(square, jnp.float32),
            pltpu.VMEM((7, 2) + square, jnp.bfloat16),
            pltpu.VMEM(square, jnp.float32),
            pltpu.VMEM(square, jnp.float32),
            pltpu.VMEM(square, jnp.float32),
            pltpu.SemaphoreType.DMA((1 + state.shape[0] // 128,)),
        ],
        pltpu.HBM,
    )(packed, state)


def reduced(packed):
    lon = lax.axis_size("lon")
    lat = lax.axis_size("lat")
    width = packed.size // lon
    pieces = lax.all_to_all(packed.reshape(lon, 1, width), "lon", 0, 0)
    piece = jnp.sum(pieces, axis=0)
    pieces = lax.all_to_all(jnp.broadcast_to(piece[None], (lat, 1, width)), "lat", 0, 0)
    piece = jnp.sum(pieces, axis=0)
    pieces = lax.all_to_all(jnp.broadcast_to(piece[None], (lon, 1, width)), "lon", 0, 0)
    return pieces.reshape(packed.shape)


def local(ensemble, bathymetry, obs_cell, obs_value, obs_weight):
    fields, lon, lat, members = ensemble.shape
    vmem = pltpu.VMEM
    total_lat = lat * lax.axis_size("lat")
    wide = lat + 2 * REACH
    rows = lax.axis_index("lat") * lat - REACH + lax.broadcasted_iota(jnp.int32, (wide, 128), 0)
    inside = ((rows >= 0) & (rows < total_lat)).astype(jnp.float32)
    turning = rotation * (2.0 * (rows.astype(jnp.float32) + 0.5) / total_lat - 1.0)
    lat_shape = (ROWS * lon + 8, members)
    lon_shape = (LON_ROWS + wide, members)
    here = lax.axis_index("lon")
    parity = ((here + lax.axis_index("lat")) & 1) + 2 * (here & 1)
    parity = parity.reshape(1)
    first, second, ahead, depth = on_core(
        pack_lat_kernel,
        (lat_shape, lat_shape, (MAIN_ROWS, members), (lat, 128)),
        [pltpu.SMEM] + [pltpu.HBM] * 2,
        [
            pltpu.VMEM(ensemble.shape, jnp.float32),
            pltpu.VMEM(bathymetry.shape, jnp.int32),
            pltpu.VMEM((128, 128), jnp.float32),
            pltpu.SemaphoreType.DMA((2,)),
        ],
    )(parity, in_hbm(ensemble), in_hbm(bathymetry))
    across, within = [], []
    columns = lax.axis_size("lon")
    rows_of = lax.axis_size("lat")
    pairs = ([], [])
    for a in range(columns):
        for b in range(rows_of):
            ours = a * rows_of + b
            if b + 1 < rows_of:
                pairs[(a + b) % 2].extend(((ours, ours + 1), (ours + 1, ours)))
        (across if a % 2 else within).extend(((a, (a + 1) % columns), ((a + 1) % columns, a)))
    first = lax.ppermute(first, ("lon", "lat"), pairs[0])
    second = lax.ppermute(second, ("lon", "lat"), pairs[1])
    ahead = lax.ppermute(ahead, "lon", across)
    out_across, out_within, strip = on_core(
        pack_lon_kernel,
        ((LON_ROWS + wide - MAIN_ROWS, members), lon_shape, (wide, 128)),
        [pltpu.SMEM] + [vmem] * 4,
        [],
    )(parity, ensemble, first, second, depth)
    planes = (fields, lon, wide, members)
    across = lax.ppermute(out_across, "lon", across)
    within = lax.ppermute(out_within, "lon", within)
    inner, handed = on_core(
        inner_kernel,
        ((fields, lon - 2 * REACH, lat, members), (len(HANDED), REACH) + planes[2:]),
        [pltpu.SMEM] + [vmem] * 6,
        [pltpu.VMEM(planes, jnp.float32)] * 2
        + [pltpu.VMEM((1,) + planes[1:], jnp.float32)],
    )(parity, ensemble, first, second, strip, turning, inside)
    planes = (fields, wide, wide, members)
    forecast, packed = on_core(
        step_kernel,
        ((fields * lon * lat, members), (members + 32, members // 2)),
        [pltpu.SMEM] + [vmem] * 8 + [pltpu.HBM] * 3,
        [
            pltpu.VMEM((fields, 2 * REACH) + planes[2:], jnp.float32),
            pltpu.VMEM(planes, jnp.float32),
            pltpu.VMEM((1,) + planes[1:], jnp.float32),
            pltpu.VMEM((obs_cell.shape[2], members), jnp.float32),
            pltpu.VMEM((fields * lon * lat, members // 2), jnp.float32),
            pltpu.VMEM((fields * lon * lat, members // 2), jnp.float32),
            pltpu.SMEM(obs_cell.shape, jnp.int32),
        ]
        + [pltpu.VMEM(obs_value.shape, jnp.float32)] * 2
        + [pltpu.SemaphoreType.DMA((3,))],
    )(
        parity,
        ahead,
        across,
        within,
        strip,
        turning,
        inside,
        inner,
        handed,
        in_hbm(obs_cell),
        in_hbm(obs_value),
        in_hbm(obs_weight),
    )
    analysis, transform = finish(reduced(packed), forecast)
    return (analysis.reshape(ensemble.shape), transform)


def solution(mesh):
    return jax.shard_map(
        local,
        mesh=mesh,
        in_specs=(
            P(None, "lon", "lat", None),
            P("lon", "lat"),
            P("lon", "lat", None),
            P("lon", "lat", None),
            P("lon", "lat", None),
        ),
        out_specs=(P(None, "lon", "lat", None), P()),
        check_vma=False,
    )
```
